32 devices in a mesh: dp: 16 (over z, x, core), tensor: 2 (over y).
Axes of the slice: x: 2, y: 2, z: 4, core: 2. Of those that a mesh axis runs over, the one named last changes fastest.
Arguments:
- entering_activations: float32 [16384, 1024], P(('dp', 'tensor')), may hold values from -6 to 6
- segment_ids: int32 [16, 1024], P('dp'), may hold values from 0 to 7, never falling along the last dimension, each value on 1 to 512 neighbouring positions
- leaving_activation_slope: float32 [16384, 1024], P(('dp', 'tensor')), may hold values from -6 to 6
- qkv_weight: float32 [1024, 3072], P('dp', 'tensor'), may hold values from -0.1875 to 0.1875
- qv_bias: float32 [2048], P('tensor'), may hold values from -1.75 to 1.75
- dense_weight: float32 [1024, 1024], P('tensor', 'dp'), may hold values from -0.5 to 0.5
- dense_bias: float32 [1024], replicated, may hold values from -1.75 to 1.75
- up_weight: float32 [1024, 4096], P('dp', 'tensor'), may hold values from -0.1875 to 0.1875
- up_bias: float32 [4096], P('tensor'), may hold values from -3 to 3
- down_weight: float32 [4096, 1024], P('tensor', 'dp'), may hold values from -0.09375 to 0.09375
- down_bias: float32 [1024], replicated, may hold values from -1.75 to 1.75
- mixer_scale_factor: float32 [1024], replicated, may hold values from 0.1 to 1.9
- mixer_offset_term: float32 [1024], replicated, may hold values from -1.75 to 1.75
- perceptron_scale_factor: float32 [1024], replicated, may hold values from 0.1 to 1.9
- perceptron_offset_term: float32 [1024], replicated, may hold values from -1.75 to 1.75
- first_qkv_weight: float32 [1024, 3072], P('dp', 'tensor'), may hold values from -24 to 24
- first_qv_bias: float32 [2048], P('tensor'), may hold values from -24 to 24
- first_dense_weight: float32 [1024, 1024], P('tensor', 'dp'), may hold values from -24 to 24
- first_dense_bias: float32 [1024], replicated, may hold values from -64 to 64
- first_up_weight: float32 [1024, 4096], P('dp', 'tensor'), may hold values from -24 to 24
- first_up_bias: float32 [4096], P('tensor'), may hold values from -24 to 24
- first_down_weight: float32 [4096, 1024], P('tensor', 'dp'), may hold values from -24 to 24
- first_down_bias: float32 [1024], replicated, may hold values from -64 to 64
- first_norm1_gain: float32 [1024], replicated, may hold values from -64 to 64
- first_norm1_bias: float32 [1024], replicated, may hold values from -64 to 64
- first_norm2_gain: float32 [1024], replicated, may hold values from -64 to 64
- first_norm2_bias: float32 [1024], replicated, may hold values from -64 to 64
- second_qkv_weight: float32 [1024, 3072], P('dp', 'tensor'), may hold values from 64 to 2048
- second_qv_bias: float32 [2048], P('tensor'), may hold values from 64 to 2048
- second_dense_weight: float32 [1024, 1024], P('tensor', 'dp'), may hold values from 64 to 2048
- second_dense_bias: float32 [1024], replicated, may hold values from 1024 to 16384
- second_up_weight: float32 [1024, 4096], P('dp', 'tensor'), may hold values from 64 to 2048
- second_up_bias: float32 [4096], P('tensor'), may hold values from 64 to 2048
- second_down_weight: float32 [4096, 1024], P('tensor', 'dp'), may hold values from 64 to 2048
- second_down_bias: float32 [1024], replicated, may hold values from 1024 to 16384
- second_norm1_gain: float32 [1024], replicated, may hold values from 1024 to 16384
- second_norm1_bias: float32 [1024], replicated, may hold values from 1024 to 16384
- second_norm2_gain: float32 [1024], replicated, may hold values from 1024 to 16384
- second_norm2_bias: float32 [1024], replicated, may hold values from 1024 to 16384
Outputs:
- block_out: float32 [16384, 1024], P(('dp', 'tensor'))
- entering_activation_slope: float32 [16384, 1024], P(('dp', 'tensor'))
- grad_qkv_weight: float32 [1024, 3072], P('dp', 'tensor')
- grad_qv_bias: float32 [2048], P('tensor')
- grad_dense_weight: float32 [1024, 1024], P('tensor', 'dp')
- grad_dense_bias: float32 [1024], replicated
- grad_up_weight: float32 [1024, 4096], P('dp', 'tensor')
- grad_up_bias: float32 [4096], P('tensor')
- grad_down_weight: float32 [4096, 1024], P('tensor', 'dp')
- grad_down_bias: float32 [1024], replicated
- grad_norm1_gain: float32 [1024], replicated
- grad_norm1_bias: float32 [1024], replicated
- grad_norm2_gain: float32 [1024], replicated
- grad_norm2_bias: float32 [1024], replicated
- new_qkv_weight: float32 [1024, 3072], P('dp', 'tensor')
- new_qv_bias: float32 [2048], P('tensor')
- new_dense_weight: float32 [1024, 1024], P('tensor', 'dp')
- new_dense_bias: float32 [1024], replicated
- new_up_weight: float32 [1024, 4096], P('dp', 'tensor')
- new_up_bias: float32 [4096], P('tensor')
- new_down_weight: float32 [4096, 1024], P('tensor', 'dp')
- new_down_bias: float32 [1024], replicated
- new_norm1_gain: float32 [1024], replicated
- new_norm1_bias: float32 [1024], replicated
- new_norm2_gain: float32 [1024], replicated
- new_norm2_bias: float32 [1024], replicated
- new_first_qkv_weight: float32 [1024, 3072], P('dp', 'tensor')
- new_first_qv_bias: float32 [2048], P('tensor')
- new_first_dense_weight: float32 [1024, 1024], P('tensor', 'dp')
- new_first_dense_bias: float32 [1024], replicated
- new_first_up_weight: float32 [1024, 4096], P('dp', 'tensor')
- new_first_up_bias: float32 [4096], P('tensor')
- new_first_down_weight: float32 [4096, 1024], P('tensor', 'dp')
- new_first_down_bias: float32 [1024], replicated
- new_first_norm1_gain: float32 [1024], replicated
- new_first_norm1_bias: float32 [1024], replicated
- new_first_norm2_gain: float32 [1024], replicated
- new_first_norm2_bias: float32 [1024], replicated
- new_second_qkv_weight: float32 [1024, 3072], P('dp', 'tensor')
- new_second_qv_bias: float32 [2048], P('tensor')
- new_second_dense_weight: float32 [1024, 1024], P('tensor', 'dp')
- new_second_dense_bias: float32 [1024], replicated
- new_second_up_weight: float32 [1024, 4096], P('dp', 'tensor')
- new_second_up_bias: float32 [4096], P('tensor')
- new_second_down_weight: float32 [4096, 1024], P('tensor', 'dp')
- new_second_down_bias: float32 [1024], replicated
- new_second_norm1_gain: float32 [1024], replicated
- new_second_norm1_bias: float32 [1024], replicated
- new_second_norm2_gain: float32 [1024], replicated
- new_second_norm2_bias: float32 [1024], replicated
The draws below stay inside these ranges and needn't reach their ends.
Inputs may be any that keep to these rules, and one draw needn't show every extreme that they name: Along each row of segment_ids the numbers never fall.
All inputs are finite; a program needn't handle non-finite values.
Results may differ from the reference program's by a relative error of at most 0.019.
Values may be sent and summed in bfloat16 or wider, within the bound.
A program may use at most 256 MiB of HBM per device.

```python
import math
import jax
import jax.numpy as jnp
import numpy as np
from jax import lax

D = 1024
FOCUS_COUNT = 16
FF = 4096
SEQ_LEN = 1024
DOCS = 8
ADAM_STEP = 4
HEAD_DIM = 64
SEQS = 16
TOKENS = 16384
N_TENSOR = 2


def level_of(rng, extent, shards, smallest, top_value):
    gain, own = 1.0, jax.random.fold_in(rng, 6)
    for dim, blocks in shards:
        steps = jnp.exp(jax.random.uniform(jax.random.fold_in(own, dim), (blocks,), jnp.float32, smallest / len(shards), top_value / len(shards)))
        gain = gain * jnp.repeat(steps, extent[dim] // blocks).reshape([-1 if axis == dim else 1 for axis in range(len(extent))])
    return gain


def length_profile(number_of, total, bound, skew):
    portions = [(1 << 20) // math.isqrt(rank ** skew) + 1 for rank in range(2, number_of + 1)]
    rest, holding = total - bound - (number_of - 1), [1] * (number_of - 1)
    while rest > 0:
        free = [i for i in range(number_of - 1) if holding[i] < bound]
        whole, left = sum([portions[i] for i in free]), rest
        for i in free:
            more = min(bound - holding[i], max(1, left * portions[i] // whole), rest)
            holding[i] = holding[i] + more
            rest = rest - more
    return np.array([bound] + holding)


def ragged(rng, amount, total, bound, lean):
    if amount == 2:
        one = jax.random.randint(rng, (), max(1, total - bound), min(bound, total - 1) + 1)
        return jnp.stack([one, total - one])
    sizes = jnp.asarray(length_profile(amount, total, bound, lean), jnp.int32)
    couples = (amount - 1) // 2
    source_of, receiver = sizes[1:1 + 2 * couples:2], sizes[2:2 + 2 * couples:2]
    slack = jnp.minimum(source_of - 1, bound - receiver)
    shifted = jax.random.randint(jax.random.fold_in(rng, 1), (couples,), 0, 1 << 20) % (slack + 1)
    sizes = sizes.at[1:1 + 2 * couples:2].set(source_of - shifted).at[2:2 + 2 * couples:2].set(receiver + shifted)
    return sizes[jax.random.permutation(jax.random.fold_in(rng, 2), amount)]


def noise(key, shape, scale, reach, cuts=(), kind=jnp.bfloat16):
    drawn = scale * jax.random.normal(key, shape, jnp.float32)
    if cuts:
        drawn = drawn * level_of(key, shape, cuts, -0.22, 0.18)
    return jnp.clip(drawn, -reach, reach).astype(kind)


def setup_inputs(seed: int = 0) -> dict:
    key_list = jax.random.split(jax.random.key(seed), 40)
    return {
        "entering_activations": noise(key_list[0], (TOKENS, D), 1.0, 6.0, ((0, 32),), jnp.float32),
        "segment_ids": jax.vmap(lambda own: jnp.searchsorted(jnp.cumsum(ragged(own, DOCS, SEQ_LEN, SEQ_LEN // 2, 2)), jnp.arange(SEQ_LEN), side="right"))(jax.random.split(key_list[1], SEQS)).reshape((SEQS, SEQ_LEN)).astype(jnp.int32),
        "leaving_activation_slope": noise(key_list[2], (TOKENS, D), 1.0, 6.0, ((0, 32),), jnp.float32),
        "qkv_weight": noise(key_list[3], (D, 3 * D), D ** -0.5, 0.1875, ((0, 16), (1, 2)), jnp.float32),
        "qv_bias": noise(key_list[4], (2 * D,), 0.3, 1.75, ((0, 2),), jnp.float32),
        "dense_weight": noise(key_list[5], (D, D), (D // 8) ** -0.5, 0.5, ((0, 2), (1, 16)), jnp.float32),
        "dense_bias": noise(key_list[6], (D,), 0.3, 1.75, (), jnp.float32),
        "up_weight": noise(key_list[7], (D, FF), D ** -0.5, 0.1875, ((0, 16), (1, 2)), jnp.float32),
        "up_bias": noise(key_list[8], (FF,), 0.5, 3.0, ((0, 2),), jnp.float32),
        "down_weight": noise(key_list[9], (FF, D), FF ** -0.5, 0.09375, ((0, 2), (1, 16)), jnp.float32),
        "down_bias": noise(key_list[10], (D,), 0.3, 1.75, (), jnp.float32),
        "mixer_scale_factor": jnp.clip(1.0 + 0.18 * jax.random.normal(key_list[11], (D,), jnp.float32), 0.1, 1.9),
        "mixer_offset_term": noise(key_list[12], (D,), 0.3, 1.75, (), jnp.float32),
        "perceptron_scale_factor": jnp.clip(1.0 + 0.18 * jax.random.normal(key_list[13], (D,), jnp.float32), 0.1, 1.9),
        "perceptron_offset_term": noise(key_list[14], (D,), 0.3, 1.75, (), jnp.float32),
        "first_qkv_weight": noise(key_list[15], (D, 3 * D), 4.0, 24.0, ((0, 16), (1, 2)), jnp.float32),
        "first_qv_bias": noise(key_list[16], (2 * D,), 4.0, 24.0, ((0, 2),), jnp.float32),
        "first_dense_weight": noise(key_list[17], (D, D), 4.0, 24.0, ((0, 2), (1, 16)), jnp.float32),
        "first_dense_bias": noise(key_list[18], (D,), 10.0, 64.0, (), jnp.float32),
        "first_up_weight": noise(key_list[19], (D, FF), 4.0, 24.0, ((0, 16), (1, 2)), jnp.float32),
        "first_up_bias": noise(key_list[20], (FF,), 4.0, 24.0, ((0, 2),), jnp.float32),
        "first_down_weight": noise(key_list[21], (FF, D), 4.0, 24.0, ((0, 2), (1, 16)), jnp.float32),
        "first_down_bias": noise(key_list[22], (D,), 10.0, 64.0, (), jnp.float32),
        "first_norm1_gain": noise(key_list[23], (D,), 10.0, 64.0, (), jnp.float32),
        "first_norm1_bias": noise(key_list[24], (D,), 10.0, 64.0, (), jnp.float32),
        "first_norm2_gain": noise(key_list[25], (D,), 10.0, 64.0, (), jnp.float32),
        "first_norm2_bias": noise(key_list[26], (D,), 10.0, 64.0, (), jnp.float32),
        "second_qkv_weight": jnp.clip(jnp.exp(math.log(2048.0) - 3.465736 * jax.random.uniform(key_list[27], (D, 3 * D), jnp.float32) ** level_of(key_list[27], (D, 3 * D), ((0, 16), (1, 2)), -0.2, 0.2)), 64.0, 2048.0),
        "second_qv_bias": jnp.clip(jnp.exp(math.log(2048.0) - 3.465736 * jax.random.uniform(key_list[28], (2 * D,), jnp.float32) ** level_of(key_list[28], (2 * D,), ((0, 2),), -0.2, 0.2)), 64.0, 2048.0),
        "second_dense_weight": jnp.clip(jnp.exp(math.log(2048.0) - 3.465736 * jax.random.uniform(key_list[29], (D, D), jnp.float32) ** level_of(key_list[29], (D, D), ((0, 2), (1, 16)), -0.2, 0.2)), 64.0, 2048.0),
        "second_dense_bias": jnp.clip(jnp.exp(jax.random.uniform(key_list[30], (D,), jnp.float32, math.log(1024.0), math.log(16384.0))), 1024.0, 16384.0),
        "second_up_weight": jnp.clip(jnp.exp(math.log(2048.0) - 3.465736 * jax.random.uniform(key_list[31], (D, FF), jnp.float32) ** level_of(key_list[31], (D, FF), ((0, 16), (1, 2)), -0.2, 0.2)), 64.0, 2048.0),
        "second_up_bias": jnp.clip(jnp.exp(math.log(2048.0) - 3.465736 * jax.random.uniform(key_list[32], (FF,), jnp.float32) ** level_of(key_list[32], (FF,), ((0, 2),), -0.2, 0.2)), 64.0, 2048.0),
        "second_down_weight": jnp.clip(jnp.exp(math.log(2048.0) - 3.465736 * jax.random.uniform(key_list[33], (FF, D), jnp.float32) ** level_of(key_list[33], (FF, D), ((0, 2), (1, 16)), -0.2, 0.2)), 64.0, 2048.0),
        "second_down_bias": jnp.clip(jnp.exp(jax.random.uniform(key_list[34], (D,), jnp.float32, math.log(1024.0), math.log(16384.0))), 1024.0, 16384.0),
        "second_norm1_gain": jnp.clip(jnp.exp(jax.random.uniform(key_list[35], (D,), jnp.float32, math.log(1024.0), math.log(16384.0))), 1024.0, 16384.0),
        "second_norm1_bias": jnp.clip(jnp.exp(jax.random.uniform(key_list[36], (D,), jnp.float32, math.log(1024.0), math.log(16384.0))), 1024.0, 16384.0),
        "second_norm2_gain": jnp.clip(jnp.exp(jax.random.uniform(key_list[37], (D,), jnp.float32, math.log(1024.0), math.log(16384.0))), 1024.0, 16384.0),
        "second_norm2_bias": jnp.clip(jnp.exp(jax.random.uniform(key_list[38], (D,), jnp.float32, math.log(1024.0), math.log(16384.0))), 1024.0, 16384.0),
    }


beta_first = 0.9
beta_second = 0.95

def rounded(values):
    return lax.optimization_barrier(values.astype(jnp.bfloat16)).astype(jnp.float32)

def standardise_features(values, elementwise_multiplier, additive_offset):
    feature_midpoint = lax.optimization_barrier(jnp.mean(values, axis=-1, keepdims=True))
    demeaned_entries = values - feature_midpoint
    reciprocal_spread = lax.rsqrt(lax.optimization_barrier(jnp.mean(demeaned_entries * demeaned_entries, axis=-1, keepdims=True)) + 1e-05)
    unit_spread_entries = demeaned_entries * reciprocal_spread
    return ((unit_spread_entries * elementwise_multiplier + additive_offset).astype(jnp.bfloat16), unit_spread_entries, reciprocal_spread)

def standardise_features_reverse(loss_slope, unit_spread_entries, reciprocal_spread, elementwise_multiplier):
    multiplied_entries = loss_slope * elementwise_multiplier
    return reciprocal_spread * (multiplied_entries - lax.optimization_barrier(jnp.mean(multiplied_entries, axis=-1, keepdims=True)) - unit_spread_entries * lax.optimization_barrier(jnp.mean(multiplied_entries * unit_spread_entries, axis=-1, keepdims=True)))

def gelu_parts(pre):
    inner = 0.7978845608 * (pre + 0.044715 * pre * pre * pre)
    tanh_val = jnp.tanh(inner)
    value = 0.5 * pre * (1.0 + tanh_val)
    slope = 0.5 * (1.0 + tanh_val) + 0.5 * pre * (1.0 - tanh_val * tanh_val) * 0.7978845608 * (1.0 + 3.0 * 0.044715 * pre * pre)
    return (value, slope)

def grouped(left, right):
    rows, inner = left.shape
    width = inner // N_TENSOR
    parts = jnp.einsum('lgc,gcn->gln', left.reshape(rows, N_TENSOR, width).astype(jnp.float32), right.reshape(N_TENSOR, width, right.shape[1]).astype(jnp.float32))
    return lax.optimization_barrier(jnp.sum(rounded(parts), axis=0))

def head_slopes(first, count):
    index = (first + jnp.arange(count)).astype(jnp.float32)
    return jnp.exp2(-8.0 * (index + 1.0) / FOCUS_COUNT)

def full_bias(qv_bias, heads):
    pair = qv_bias.reshape(heads, 2, HEAD_DIM)
    return jnp.stack([pair[:, 0], jnp.zeros_like(pair[:, 0]), pair[:, 1]], axis=1).reshape(heads * 3 * HEAD_DIM)

def masked_scores(query, keys, start, segments, slopes):
    block = query.shape[0]
    length = keys.shape[0]
    raw = jnp.einsum('qhd,khd->hqk', query, keys) * HEAD_DIM ** (-0.5)
    rows = start + jnp.arange(block)
    cols = jnp.arange(length)
    offset = (cols[None, :] - rows[:, None]).astype(jnp.float32)
    seg_rows = segments[start:start + block]
    allowed = (cols[None, :] <= rows[:, None]) & (seg_rows[:, None] == segments[None, :])
    return jnp.where(allowed[None], raw + slopes[:, None, None] * offset[None], -1e+30)

def split_heads(qkv_low):
    length = qkv_low.shape[0]
    heads = qkv_low.shape[1] // (3 * HEAD_DIM)
    split = qkv_low.reshape(length, heads, 3, HEAD_DIM).astype(jnp.float32)
    return (split[:, :, 0], split[:, :, 1], split[:, :, 2], heads)

def attention_forward(qkv_low, segments, slopes):
    query, keys, values, heads = split_heads(qkv_low)
    length = query.shape[0]
    block = min(512, length)
    contexts = []
    totals = []
    for start in range(0, length, block):
        scores = masked_scores(query[start:start + block], keys, start, segments, slopes)
        peak = lax.optimization_barrier(jnp.max(scores, axis=-1, keepdims=True))
        total = peak + jnp.log(lax.optimization_barrier(jnp.sum(jnp.exp(scores - peak), axis=-1, keepdims=True)))
        probs = rounded(jnp.exp(scores - total))
        context = jnp.einsum('hqk,khd->qhd', probs, values)
        contexts.append(context.reshape(block, heads * HEAD_DIM).astype(jnp.bfloat16))
        totals.append(total)
    return (jnp.concatenate(contexts, axis=0), totals)

def attention_backward(qkv_low, segments, slopes, totals, dcontext):
    query, keys, values, heads = split_heads(qkv_low)
    length = query.shape[0]
    block = min(512, length)
    scale = HEAD_DIM ** (-0.5)
    dkeys = jnp.zeros(keys.shape, jnp.float32)
    dvalues = jnp.zeros(values.shape, jnp.float32)
    dquery_parts = []
    for number, start in enumerate(range(0, length, block)):
        scores = masked_scores(query[start:start + block], keys, start, segments, slopes)
        probs = jnp.exp(scores - totals[number])
        probs_low = rounded(probs)
        grad_block = dcontext[start:start + block].reshape(block, heads, HEAD_DIM).astype(jnp.float32)
        dvalues = dvalues + jnp.einsum('hqk,qhd->khd', probs_low, grad_block)
        dprob = jnp.einsum('qhd,khd->hqk', grad_block, values)
        delta = lax.optimization_barrier(jnp.sum(probs * dprob, axis=-1, keepdims=True))
        dscore = rounded(probs * (dprob - delta))
        dquery_parts.append(jnp.einsum('hqk,khd->qhd', dscore, keys) * scale)
        dkeys = dkeys + jnp.einsum('hqk,qhd->khd', dscore, query[start:start + block]) * scale
    dquery = jnp.concatenate(dquery_parts, axis=0)
    return jnp.stack([dquery, dkeys, dvalues], axis=2).reshape(length, heads * 3 * HEAD_DIM)

def query_value_slope(packed_triple_sensitivity, heads):
    split = packed_triple_sensitivity.reshape(packed_triple_sensitivity.shape[0], heads, 3, HEAD_DIM)
    pair = jnp.stack([split[:, :, 0], split[:, :, 2]], axis=2)
    return lax.optimization_barrier(jnp.sum(pair, axis=0)).reshape(heads * 2 * HEAD_DIM)

def sequence_pass(local_token_activations, seg_seq, local_tokens_sensitivity, lows, vectors):
    qkv_low, dense_low, up_low, down_low = lows
    qv_bias, dense_bias, up_bias, down_bias, mixer_multiplier, mixer_additive_offset, perceptron_multiplier, perceptron_additive_offset = vectors
    slopes = head_slopes(0, FOCUS_COUNT)
    mixer_standardised, mixer_unit_spread1, mixer_reciprocal_spread1 = standardise_features(local_token_activations, mixer_multiplier, mixer_additive_offset)
    qkv = (jnp.dot(mixer_standardised, qkv_low, preferred_element_type=jnp.float32) + full_bias(qv_bias, FOCUS_COUNT)).astype(jnp.bfloat16)
    context, totals = attention_forward(qkv, seg_seq, slopes)
    skip_path_sum = local_token_activations + grouped(context, dense_low) + dense_bias
    perceptron_standardised, perceptron_unit_spread2, perceptron_reciprocal_spread2 = standardise_features(skip_path_sum, perceptron_multiplier, perceptron_additive_offset)
    pre = jnp.dot(perceptron_standardised, up_low, preferred_element_type=jnp.float32) + up_bias
    act_val, act_slope = gelu_parts(pre)
    act = act_val.astype(jnp.bfloat16)
    block_out = skip_path_sum + grouped(act, down_low) + down_bias
    out_low = local_tokens_sensitivity.astype(jnp.bfloat16)
    contraction_sensitivity = jnp.dot(act.T, out_low, preferred_element_type=jnp.float32)
    hidden_activation_sensitivity = jnp.dot(out_low, down_low.T, preferred_element_type=jnp.float32) * act_slope
    dpre_low = hidden_activation_sensitivity.astype(jnp.bfloat16)
    expansion_sensitivity = jnp.dot(perceptron_standardised.T, dpre_low, preferred_element_type=jnp.float32)
    pre_perceptron_sensitivity = grouped(dpre_low, up_low.T)
    skip_path_sensitivity = local_tokens_sensitivity + standardise_features_reverse(pre_perceptron_sensitivity, perceptron_unit_spread2, perceptron_reciprocal_spread2, perceptron_multiplier)
    dresid_low = skip_path_sensitivity.astype(jnp.bfloat16)
    mixer_merge_sensitivity = jnp.dot(context.T, dresid_low, preferred_element_type=jnp.float32)
    dcontext = jnp.dot(dresid_low, dense_low.T, preferred_element_type=jnp.float32).astype(jnp.bfloat16)
    packed_triple_sensitivity = attention_backward(qkv, seg_seq, slopes, totals, dcontext)
    dqkv_low = packed_triple_sensitivity.astype(jnp.bfloat16)
    packed_triple_slope = jnp.dot(mixer_standardised.T, dqkv_low, preferred_element_type=jnp.float32)
    pre_mixer_sensitivity = grouped(dqkv_low, qkv_low.T)
    entering_sensitivity = skip_path_sensitivity + standardise_features_reverse(pre_mixer_sensitivity, mixer_unit_spread1, mixer_reciprocal_spread1, mixer_multiplier)
    parameter_slopes = (packed_triple_slope, query_value_slope(packed_triple_sensitivity, FOCUS_COUNT), mixer_merge_sensitivity, lax.optimization_barrier(jnp.sum(skip_path_sensitivity, axis=0)), expansion_sensitivity, lax.optimization_barrier(jnp.sum(hidden_activation_sensitivity, axis=0)), contraction_sensitivity, lax.optimization_barrier(jnp.sum(local_tokens_sensitivity, axis=0)), lax.optimization_barrier(jnp.sum(pre_mixer_sensitivity * mixer_unit_spread1, axis=0)), lax.optimization_barrier(jnp.sum(pre_mixer_sensitivity, axis=0)), lax.optimization_barrier(jnp.sum(pre_perceptron_sensitivity * perceptron_unit_spread2, axis=0)), lax.optimization_barrier(jnp.sum(pre_perceptron_sensitivity, axis=0)))
    return (block_out, entering_sensitivity, parameter_slopes)

def adamw(param, loss_slope, first, second, rate, decay):
    first_new = beta_first * first + (1.0 - beta_first) * loss_slope
    second_new = beta_second * second + (1.0 - beta_second) * loss_slope * loss_slope
    update = first_new / (1.0 - beta_first ** ADAM_STEP) / (jnp.sqrt(second_new / (1.0 - beta_second ** ADAM_STEP)) + 1e-08)
    return (param - rate * (update + decay * param), first_new, second_new)

def reference(entering_activations, segment_ids, leaving_activation_slope, qkv_weight, qv_bias, dense_weight, dense_bias, up_weight, up_bias, down_weight, down_bias, mixer_scale_factor, mixer_offset_term, perceptron_scale_factor, perceptron_offset_term, first_qkv_weight, first_qv_bias, first_dense_weight, first_dense_bias, first_up_weight, first_up_bias, first_down_weight, first_down_bias, first_norm1_gain, first_norm1_bias, first_norm2_gain, first_norm2_bias, second_qkv_weight, second_qv_bias, second_dense_weight, second_dense_bias, second_up_weight, second_up_bias, second_down_weight, second_down_bias, second_norm1_gain, second_norm1_bias, second_norm2_gain, second_norm2_bias):
    params = (qkv_weight, qv_bias, dense_weight, dense_bias, up_weight, up_bias, down_weight, down_bias, mixer_scale_factor, mixer_offset_term, perceptron_scale_factor, perceptron_offset_term)
    firsts = (first_qkv_weight, first_qv_bias, first_dense_weight, first_dense_bias, first_up_weight, first_up_bias, first_down_weight, first_down_bias, first_norm1_gain, first_norm1_bias, first_norm2_gain, first_norm2_bias)
    seconds = (second_qkv_weight, second_qv_bias, second_dense_weight, second_dense_bias, second_up_weight, second_up_bias, second_down_weight, second_down_bias, second_norm1_gain, second_norm1_bias, second_norm2_gain, second_norm2_bias)
    lows = (qkv_weight.astype(jnp.bfloat16), dense_weight.astype(jnp.bfloat16), up_weight.astype(jnp.bfloat16), down_weight.astype(jnp.bfloat16))
    vectors = (qv_bias, dense_bias, up_bias, down_bias, mixer_scale_factor, mixer_offset_term, perceptron_scale_factor, perceptron_offset_term)
    inputs = entering_activations.reshape(SEQS, SEQ_LEN, D)
    cotangents = leaving_activation_slope.reshape(SEQS, SEQ_LEN, D)

    def one_sequence(carry, item):
        local_token_activations, seg_seq, local_tokens_sensitivity = item
        block_out, entering_sensitivity, parameter_slopes = sequence_pass(local_token_activations, seg_seq, local_tokens_sensitivity, lows, vectors)
        return (tuple((total + part for total, part in zip(carry, parameter_slopes))), (block_out, entering_sensitivity))
    start = tuple((jnp.zeros(p.shape, jnp.float32) for p in params))
    sums, (outs, grad_ins) = lax.scan(one_sequence, start, (inputs, segment_ids, cotangents))
    results = []
    for index in range(12):
        matrix = index in (0, 2, 4, 6)
        results.append(adamw(params[index], sums[index], firsts[index], seconds[index], 0.01 if matrix else 0.1, 0.1 if matrix else 0.0))
    news = [r[0] for r in results]
    moments_one = [r[1] for r in results]
    moments_two = [r[2] for r in results]
    return (outs.reshape(TOKENS, D), grad_ins.reshape(TOKENS, D), *sums, *news, *moments_one, *moments_two)
```

```python
import functools

import jax
import jax.numpy as jnp
from jax import lax
from jax.experimental import pallas as pl
from jax.experimental.pallas import tpu as pltpu
from jax.sharding import PartitionSpec as P

D = 1024
FOCUS_COUNT = 16
FF = 4096
ADAM_STEP = 4
HEAD_DIM = 64
MAX_SPAN = 512


beta_first = 0.9
beta_second = 0.95


def standardise_features(values, elementwise_multiplier, additive_offset):
    feature_midpoint = jnp.mean(values, axis=-1, keepdims=True)
    demeaned_entries = values - feature_midpoint
    reciprocal_spread = lax.rsqrt(
        jnp.mean(demeaned_entries * demeaned_entries, axis=-1, keepdims=True) + 1e-05
    )
    unit_spread_entries = demeaned_entries * reciprocal_spread
    return (
        (unit_spread_entries * elementwise_multiplier + additive_offset).astype(jnp.bfloat16),
        unit_spread_entries,
        reciprocal_spread,
    )


def standardise_features_reverse(
    loss_slope, unit_spread_entries, reciprocal_spread, elementwise_multiplier
):
    multiplied_entries = loss_slope * elementwise_multiplier
    return reciprocal_spread * (
        multiplied_entries
        - jnp.mean(multiplied_entries, axis=-1, keepdims=True)
        - unit_spread_entries
        * jnp.mean(multiplied_entries * unit_spread_entries, axis=-1, keepdims=True)
    )


def gelu_parts(pre):
    inner = 0.7978845608 * (pre + 0.044715 * pre * pre * pre)
    tanh_val = jnp.tanh(inner)
    value = 0.5 * pre * (1.0 + tanh_val)
    slope = 0.5 * (1.0 + tanh_val) + 0.5 * pre * (1.0 - tanh_val * tanh_val) * 0.7978845608 * (
        1.0 + 3.0 * 0.044715 * pre * pre
    )
    return (value, slope)


def inner_rows(left, right):
    return lax.dot_general(
        left, right, (((0,), (0,)), ((), ())), preferred_element_type=jnp.float32
    )


def times_transposed(left, right):
    return lax.dot_general(
        left, right, (((1,), (1,)), ((), ())), preferred_element_type=jnp.float32
    )


def head_slopes(first, count):
    index = (first + jnp.arange(count)).astype(jnp.float32)
    return jnp.exp2(-8.0 * (index + 1.0) / FOCUS_COUNT)


def full_bias(qv_bias, heads):
    pair = qv_bias.reshape(heads, 2, HEAD_DIM)
    return jnp.stack([pair[:, 0], jnp.zeros_like(pair[:, 0]), pair[:, 1]], axis=1).reshape(
        heads * 3 * HEAD_DIM
    )


def window(start, block, length):
    return (max(0, start - MAX_SPAN), min(length, start + block))


def fill_offsets(offsets, rows_seg, cols_seg, rows_first, length, block):
    for start in range(0, length, block):
        low, high = window(start, block, length)
        shape = (block, high - low) if rows_first else (high - low, block)
        axis = 0 if rows_first else 1
        row = start + lax.broadcasted_iota(jnp.int32, shape, axis)
        col = low + lax.broadcasted_iota(jnp.int32, shape, 1 - axis)
        if rows_first:
            same = rows_seg[start : start + block, :] == cols_seg[:, low:high]
        else:
            same = rows_seg[low:high, :] == cols_seg[:, start : start + block]
        allowed = (col <= row) & same
        value = jnp.where(allowed, (col - row).astype(jnp.float32), -1e30)
        if rows_first:
            offsets[start : start + block, 0 : high - low] = value
        else:
            offsets[0 : high - low, start : start + block] = value


def forward_kernel(block, slopes, x, rows_seg, cols_seg, out, offsets):
    length = x.shape[0]
    step = pl.program_id(0)

    @pl.when(step == 0)
    def _():
        fill_offsets(offsets, rows_seg, cols_seg, True, length, block)

    for i in range(2):
        base = 3 * HEAD_DIM * i
        slope = slopes[2 * step + i]
        query = x[:, base : base + HEAD_DIM] * HEAD_DIM ** (-0.5)
        keys = x[:, base + HEAD_DIM : base + 2 * HEAD_DIM]
        values = x[:, base + 2 * HEAD_DIM : base + 3 * HEAD_DIM]
        for start in range(0, length, block):
            low, high = window(start, block, length)
            scores = (
                times_transposed(query[start : start + block], keys[low:high])
                + slope * offsets[start : start + block, 0 : high - low]
            )
            peak = jnp.max(scores, axis=1, keepdims=True)
            raised = jnp.exp(scores - peak)
            total = jnp.sum(raised, axis=1, keepdims=True)
            probs = (raised * (1.0 / total)).astype(jnp.bfloat16)
            context = jnp.dot(probs, values[low:high], preferred_element_type=jnp.float32)
            out[start : start + block, HEAD_DIM * i : HEAD_DIM * (i + 1)] = context.astype(
                jnp.bfloat16
            )


def backward_kernel(
    block, slopes, x, grad, rows_seg, cols_seg, out, sums, offsets, dkeys, dvalues, dquery
):
    length = x.shape[0]
    step = pl.program_id(0)
    scale = HEAD_DIM ** (-0.5)

    @pl.when(step == 0)
    def _():
        fill_offsets(offsets, rows_seg, cols_seg, False, length, block)

    for i in range(2):
        base = 3 * HEAD_DIM * i
        slope = slopes[2 * step + i]
        query = x[:, base : base + HEAD_DIM] * scale
        keys = x[:, base + HEAD_DIM : base + 2 * HEAD_DIM]
        values = x[:, base + 2 * HEAD_DIM : base + 3 * HEAD_DIM]
        slopes_out = grad[:, HEAD_DIM * i : HEAD_DIM * (i + 1)]
        dkeys[...] = jnp.zeros_like(dkeys)
        dvalues[...] = jnp.zeros_like(dvalues)
        for start in range(0, length, block):
            low, high = window(start, block, length)
            query_block = query[start : start + block]
            grad_block = slopes_out[start : start + block]
            scores = (
                times_transposed(keys[low:high], query_block)
                + slope * offsets[0 : high - low, start : start + block]
            )
            peak = jnp.max(scores, axis=0, keepdims=True)
            raised = jnp.exp(scores - peak)
            total = jnp.sum(raised, axis=0, keepdims=True)
            probs = raised * (1.0 / total)
            dprob = times_transposed(values[low:high], grad_block)
            delta = jnp.sum(probs * dprob, axis=0, keepdims=True)
            dscore = (probs * (dprob - delta)).astype(jnp.bfloat16)
            dvalues[low:high, :] += jnp.dot(
                probs.astype(jnp.bfloat16), grad_block, preferred_element_type=jnp.float32
            )
            dkeys[low:high, :] += jnp.dot(dscore, query_block, preferred_element_type=jnp.float32)
            dquery[start : start + block, :] = inner_rows(dscore, keys[low:high]) * scale
        for place, part in enumerate((dquery, dkeys, dvalues)):
            first = base + HEAD_DIM * place
            out[:, first : first + HEAD_DIM] = part[...].astype(jnp.bfloat16)
            sums[:, first : first + HEAD_DIM] = jnp.sum(part[...], axis=0, keepdims=True)


def attention_forward(qkv, segments, slopes):
    length, width = qkv.shape
    pairs = width // (6 * HEAD_DIM)
    block = min(256, length)
    span = min(length, block + MAX_SPAN)
    return pl.pallas_call(
        functools.partial(forward_kernel, block),
        grid=(pairs,),
        out_shape=jax.ShapeDtypeStruct((length, width // 3), jnp.bfloat16),
        in_specs=[
            pl.BlockSpec(memory_space=pltpu.SMEM),
            pl.BlockSpec((length, 6 * HEAD_DIM), lambda p: (0, p)),
            pl.BlockSpec((length, 1), lambda p: (0, 0)),
            pl.BlockSpec((1, length), lambda p: (0, 0)),
        ],
        out_specs=pl.BlockSpec((length, 2 * HEAD_DIM), lambda p: (0, p)),
        scratch_shapes=[pltpu.VMEM((length, span), jnp.float32)],
        cost_estimate=pl.CostEstimate(
            flops=4 * length * span * width // 3,
            bytes_accessed=8 * length * width // 3,
            transcendentals=length * span * pairs * 2,
        ),
        compiler_params=pltpu.CompilerParams(vmem_limit_bytes=40 * 1024 * 1024),
        name="attention_forward",
    )(slopes, qkv, segments[:, None], segments[None, :])


def attention_backward(qkv, segments, slopes, dcontext):
    length, width = qkv.shape
    pairs = width // (6 * HEAD_DIM)
    block = min(256, length)
    span = min(length, block + MAX_SPAN)
    return pl.pallas_call(
        functools.partial(backward_kernel, block),
        grid=(pairs,),
        out_shape=(
            jax.ShapeDtypeStruct((length, width), jnp.bfloat16),
            jax.ShapeDtypeStruct((1, width), jnp.float32),
        ),
        in_specs=[
            pl.BlockSpec(memory_space=pltpu.SMEM),
            pl.BlockSpec((length, 6 * HEAD_DIM), lambda p: (0, p)),
            pl.BlockSpec((length, 2 * HEAD_DIM), lambda p: (0, p)),
            pl.BlockSpec((length, 1), lambda p: (0, 0)),
            pl.BlockSpec((1, length), lambda p: (0, 0)),
        ],
        out_specs=(
            pl.BlockSpec((length, 6 * HEAD_DIM), lambda p: (0, p)),
            pl.BlockSpec((1, 6 * HEAD_DIM), lambda p: (0, p)),
        ),
        scratch_shapes=[
            pltpu.VMEM((span, length), jnp.float32),
            pltpu.VMEM((length, HEAD_DIM), jnp.float32),
            pltpu.VMEM((length, HEAD_DIM), jnp.float32),
            pltpu.VMEM((length, HEAD_DIM), jnp.float32),
        ],
        cost_estimate=pl.CostEstimate(
            flops=10 * length * span * width // 3,
            bytes_accessed=14 * length * width // 3,
            transcendentals=length * span * pairs * 2,
        ),
        compiler_params=pltpu.CompilerParams(vmem_limit_bytes=40 * 1024 * 1024),
        name="attention_backward",
    )(slopes, qkv, dcontext, segments[:, None], segments[None, :])


def swap(values):
    return lax.ppermute(values, "tensor", [(0, 1), (1, 0)])


def spread(values, count):
    if count == 2:
        return [values, swap(values)]
    return [lax.all_gather(values, "tensor", axis=0, tiled=True)]


def fold(parts, count):
    if count == 2:
        return swap(parts[1]).astype(jnp.float32) + parts[0].astype(jnp.float32)
    return lax.psum_scatter(parts[0], "tensor", scatter_dimension=0, tiled=True).astype(
        jnp.float32
    )


def to_order(parts, rank):
    if len(parts) == 2:
        own, other = parts
        return jnp.concatenate(
            [jnp.where(rank == 0, own, other), jnp.where(rank == 0, other, own)], axis=0
        )
    return parts[0]


def from_order(values, rank, count):
    if count == 2:
        half = values.shape[0] // 2
        return [
            lax.dynamic_slice_in_dim(values, rank * half, half, 0),
            lax.dynamic_slice_in_dim(values, (1 - rank) * half, half, 0),
        ]
    return [values]


def product(left, right):
    return jnp.dot(left, right, preferred_element_type=jnp.float32)


def add_up(lefts, rights):
    total = inner_rows(lefts[0], rights[0])
    for left, right in zip(lefts[1:], rights[1:]):
        total = total + inner_rows(left, right)
    return total


def total_over_all(vector, shared, rank):
    rows = lax.all_gather(vector[None], ("dp", "tensor"), axis=0, tiled=True)
    everyone = jnp.sum(rows[:, :shared], axis=0)
    count = lax.axis_size("tensor")
    split = rows[:, shared:].reshape(rows.shape[0] // count, count, -1)
    mine = lax.dynamic_index_in_dim(jnp.sum(split, axis=0), rank, 0, keepdims=False)
    return everyone, mine


def adamw(param, loss_slope, first, second, rate, decay):
    first_new = beta_first * first + (1.0 - beta_first) * loss_slope
    second_new = beta_second * second + (1.0 - beta_second) * loss_slope * loss_slope
    update = (
        first_new
        / (1.0 - beta_first**ADAM_STEP)
        / (jnp.sqrt(second_new / (1.0 - beta_second**ADAM_STEP)) + 1e-08)
    )
    return (param - rate * (update + decay * param), first_new, second_new)


MESH = pl.DeviceIdType.MESH
CHUNK = 64
MIB = 1024 * 1024


class Spot:
    def __init__(self, depth):
        dp = lax.axis_index("dp")
        self.depth = depth
        self.t = lax.axis_index("tensor")
        self.c = lax.rem(dp, 2)
        self.x = lax.rem(lax.div(dp, 2), 2)
        self.z = lax.div(dp, 4)
        self.twin = self.at(self.z, self.x, 1 - self.c)
        self.cross = self.at(self.z, 1 - self.x, self.c)
        self.pair = (dp, 1 - self.t)

    def index(self, z, x, c):
        return (z * 2 + x) * 2 + c

    def at(self, z, x, c):
        return (self.index(z, x, c), self.t)

    def farthest(self, i):
        n = self.depth
        if i == n - 1:
            return self.z
        down = jnp.where(n - 1 - i > self.z, n - 1 - i, n - 2 - i)
        up = jnp.where(i < self.z, i, i + 1)
        return jnp.where(2 * self.z < n, down, up)

    def greet(self):
        barrier = pltpu.get_barrier_semaphore()
        others = [self.twin, self.cross, self.pair]
        for step in range(1, self.depth):
            others.append(self.at(lax.rem(self.z + step, self.depth), self.x, self.c))
        for other in others:
            pl.semaphore_signal(barrier, inc=1, device_id=other, device_id_type=MESH)
        pl.semaphore_wait(barrier, len(others))


def push(source, target, send, arrive, to):
    return pltpu.make_async_remote_copy(
        src_ref=source,
        dst_ref=target,
        send_sem=send,
        recv_sem=arrive,
        device_id=to,
        device_id_type=MESH,
    )


def rows_of(ref, first, size):
    return ref.at[pl.ds(pl.multiple_of(first, size), size)]


class Gather:
    def __init__(self, spot, shards, fulls, zs, zr, xs, xr, cs, cr, ls):
        self.spot, self.shards, self.fulls = spot, shards, fulls
        self.zs, self.zr, self.xs, self.xr, self.cs, self.cr, self.ls = zs, zr, xs, xr, cs, cr, ls
        self.count = len(shards)

    @staticmethod
    def semaphores(count, depth):
        dma = pltpu.SemaphoreType.DMA
        return [
            dma((count, depth, 2)),
            dma((count, depth)),
            dma((count, depth)),
            dma((count, depth)),
            dma((count, 2 * depth)),
            dma((count, 2 * depth)),
            dma((count,)),
        ]

    def block(self, a, z, x, c):
        size = self.shards[a].shape[0]
        return rows_of(self.fulls[a], self.spot.index(z, x, c) * size, size)

    def along(self, a, bz, way, own=False):
        s = self.spot
        region = self.block(a, bz, s.x, s.c)
        to = s.at(s.z + (1 if way == 0 else -1), s.x, s.c)
        return push(
            self.shards[a] if own else region, region, self.zs.at[a, bz, way], self.zr.at[a, bz], to
        )

    def over(self, a, bz, own=False):
        s = self.spot
        region = self.block(a, bz, s.x, s.c)
        return push(
            self.shards[a] if own else region, region, self.xs.at[a, bz], self.xr.at[a, bz], s.cross
        )

    def across(self, a, bz, bx, own=False):
        s = self.spot
        region = self.block(a, bz, bx, s.c)
        k = bz * 2 + bx
        return push(
            self.shards[a] if own else region, region, self.cs.at[a, k], self.cr.at[a, k], s.twin
        )

    def keep(self, a):
        s = self.spot
        return pltpu.make_async_copy(
            self.shards[a], self.block(a, s.z, s.x, s.c), self.ls.at[a]
        )

    def start(self):
        s = self.spot
        for a in range(self.count):
            pl.when(s.z + 1 < s.depth)(lambda a=a: self.along(a, s.z, 0, True).start())
            pl.when(s.z > 0)(lambda a=a: self.along(a, s.z, 1, True).start())
            self.over(a, s.z, True).start()
        for a in range(self.count):
            self.across(a, s.z, s.x, True).start()
            self.keep(a).start()

    def z_step(self, a, step):
        s = self.spot
        for way in (0, 1):
            bz = s.z - step if way == 0 else s.z + step
            here = bz >= 0 if way == 0 else bz < s.depth
            onward = s.z + 1 < s.depth if way == 0 else s.z > 0

            @pl.when(here)
            def _():
                self.along(a, bz, way).wait_recv()
                pl.when(onward)(lambda: self.along(a, bz, way).start())
                self.over(a, bz).start()
                self.across(a, bz, s.x).start()

    def x_step(self, a, step):
        s = self.spot

        def take(bz):
            self.over(a, bz).wait_recv()
            self.across(a, bz, 1 - s.x).start()

        if step == 0:
            take(s.z)
            return
        pl.when(s.z - step >= 0)(lambda: take(s.z - step))
        pl.when(s.z + step < s.depth)(lambda: take(s.z + step))

    def finish(self):
        s = self.spot
        for a in range(self.count):
            self.keep(a).wait()
            for bz in range(s.depth):
                for bx in range(2):
                    self.across(a, bz, bx).wait()
                self.over(a, bz).wait_send()
                pl.when((bz <= s.z) & (s.z + 1 < s.depth))(
                    lambda a=a, bz=bz: self.along(a, bz, 0).wait_send()
                )
                pl.when((bz >= s.z) & (s.z > 0))(
                    lambda a=a, bz=bz: self.along(a, bz, 1).wait_send()
                )


STRIP = 16


def strips(size, step, body):
    def one(i, carry):
        body(pl.multiple_of(i * step, step))
        return carry

    lax.fori_loop(0, size // step, one, 0)


class Scatter:
    def __init__(self, spot, grads, sums, keeps, cins, xins, zins, ls, cs, cr, xs, xr, zs, zr):
        self.spot, self.grads, self.sums = spot, grads, sums
        self.keeps, self.cins, self.xins, self.zins = keeps, cins, xins, zins
        self.ls, self.cs, self.cr, self.xs, self.xr, self.zs, self.zr = ls, cs, cr, xs, xr, zs, zr
        self.count = len(grads)

    @staticmethod
    def scratch(shapes, depth):
        count, low = len(shapes), jnp.bfloat16
        dma = pltpu.SemaphoreType.DMA
        buffers = []
        for slots in (2 * depth, 2 * depth, depth, depth):
            for rows, width in shapes:
                buffers.append(pltpu.VMEM((slots, rows, width), low))
        return buffers + [
            dma((count, 2 * depth)),
            dma((count, 2 * depth)),
            dma((count, 2 * depth)),
            dma((count, depth)),
            dma((count, depth)),
            dma((count, depth)),
            dma((count, depth)),
        ]

    def block(self, a, z, x, c):
        size = self.sums[a].shape[0]
        return rows_of(self.grads[a], self.spot.index(z, x, c) * size, size)

    def across(self, a, bz, bx):
        s = self.spot
        k = bz * 2 + bx
        return push(
            self.block(a, bz, bx, 1 - s.c),
            self.cins[a].at[k],
            self.cs.at[a, k],
            self.cr.at[a, k],
            s.twin,
        )

    def keep(self, a, bz, bx):
        k = bz * 2 + bx
        return pltpu.make_async_copy(
            self.block(a, bz, bx, self.spot.c), self.keeps[a].at[k], self.ls.at[a, k]
        )

    def over(self, a, bz):
        s = self.spot
        return push(
            self.keeps[a].at[bz * 2 + 1 - s.x],
            self.xins[a].at[bz],
            self.xs.at[a, bz],
            self.xr.at[a, bz],
            s.cross,
        )

    def along(self, a, bz, arriving=False):
        s = self.spot
        slot = bz if arriving else s.z
        return push(
            self.keeps[a].at[bz * 2 + s.x],
            self.zins[a].at[slot],
            self.zs.at[a, bz],
            self.zr.at[a, slot],
            s.at(bz, s.x, s.c),
        )

    def start(self):
        s = self.spot
        for bx in (1 - s.x, s.x):
            for i in range(s.depth):
                for a in range(self.count):
                    bz = s.farthest(i)
                    self.across(a, bz, bx).start()
                    self.keep(a, bz, bx).start()

    def c_step(self, a, i):
        s = self.spot
        bz = s.farthest(i)
        k = bz * 2 + 1 - s.x
        self.keep(a, bz, 1 - s.x).wait()
        self.across(a, bz, 1 - s.x).wait_recv()
        keep, cin = self.keeps[a], self.cins[a]

        def add(r):
            part = pl.ds(r, STRIP)
            keep[k, part, :] = (
                keep[k, part, :].astype(jnp.float32) + cin[k, part, :].astype(jnp.float32)
            ).astype(jnp.bfloat16)

        strips(keep.shape[1], STRIP, add)
        self.over(a, bz).start()

    def x_step(self, a, i):
        s = self.spot
        bz = s.farthest(i)
        k = bz * 2 + s.x
        self.keep(a, bz, s.x).wait()
        self.across(a, bz, s.x).wait_recv()
        self.over(a, bz).wait_recv()
        keep, cin, xin, out = self.keeps[a], self.cins[a], self.xins[a], self.sums[a]

        def add(r):
            part = pl.ds(r, STRIP)
            total = (
                keep[k, part, :].astype(jnp.float32)
                + cin[k, part, :].astype(jnp.float32)
                + xin[bz, part, :].astype(jnp.float32)
            )
            if i < s.depth - 1:
                keep[k, part, :] = total.astype(jnp.bfloat16)
            else:
                out[part, :] = total

        strips(keep.shape[1], STRIP, add)
        if i < s.depth - 1:
            self.along(a, bz).start()

    def last_step(self, a):
        s = self.spot
        zin, out = self.zins[a], self.sums[a]
        slots = [lax.rem(s.z + step, s.depth) for step in range(1, s.depth)]
        for slot in slots:
            self.along(a, slot, True).wait_recv()

        def add(r):
            part = pl.ds(r, STRIP)
            total = out[part, :]
            for slot in slots:
                total = total + zin[slot, part, :].astype(jnp.float32)
            out[part, :] = total

        strips(out.shape[0], STRIP, add)

    def finish(self):
        s = self.spot
        for a in range(self.count):
            for i in range(s.depth):
                bz = s.farthest(i)
                for bx in range(2):
                    self.across(a, bz, bx).wait_send()
                self.over(a, bz).wait_send()
                if i < s.depth - 1:
                    self.along(a, bz).wait_send()


class Swap:
    def __init__(self, spot, source, target, send, arrive):
        self.spot, self.source, self.target, self.send, self.arrive = (
            spot,
            source,
            target,
            send,
            arrive,
        )

    def chunk(self, i, source_first=0, target_first=0):
        return push(
            rows_of(self.source, source_first + i * CHUNK, CHUNK),
            rows_of(self.target, target_first + i * CHUNK, CHUNK),
            self.send.at[i],
            self.arrive.at[i],
            self.spot.pair,
        )


def loop(first, last, body):
    def one(i, carry):
        body(i)
        return carry

    lax.fori_loop(first, last, one, 0)


def cast_into(source, target):
    def one(r):
        part = pl.ds(r, STRIP)
        target[part, :] = source[part, :].astype(target.dtype)

    strips(source.shape[0], STRIP, one)


def spread_kernel(depth, x, gain, shift, wide0, wide1, normed, full0, full1, own, low0, low1, ys, yr, yl, *sems):
    spot = Spot(depth)
    half = x.shape[0]
    base = spot.t * half
    cast_into(wide0, low0)
    cast_into(wide1, low1)
    spot.greet()
    gather = Gather(spot, (low0, low1), (full0, full1), *sems)
    gather.start()
    swap = Swap(spot, own, normed, ys, yr)

    def keep(i):
        return pltpu.make_async_copy(
            rows_of(own, i * CHUNK, CHUNK), rows_of(normed, base + i * CHUNK, CHUNK), yl.at[i]
        )

    def work(i):
        def one(r):
            part = pl.ds(i * CHUNK + r, STRIP)
            own[part, :] = standardise_features(x[part, :], gain[...], shift[...])[0]

        strips(CHUNK, STRIP, one)
        swap.chunk(i, 0, base).start()
        keep(i).start()

    loop(0, half // CHUNK, work)
    for step in range(1, depth):
        for a in range(2):
            gather.z_step(a, step)
        for a in range(2):
            gather.x_step(a, step - 1)
    for a in range(2):
        gather.x_step(a, depth - 1)

    def done(i):
        keep(i).wait()
        swap.chunk(i, 0, base).wait_send()
        swap.chunk(i, 0, half - base).wait_recv()

    loop(0, half // CHUNK, done)
    gather.finish()


def middle_kernel(depth, part, x, bias, gain, shift, wide0, wide1, resid, normed, full0, full1, own, low0, low1, inbox, ps, pr, ys, yr, yl, *sems):
    spot = Spot(depth)
    half = x.shape[0]
    base = spot.t * half
    cast_into(wide0, low0)
    cast_into(wide1, low1)
    spot.greet()
    first = Swap(spot, part, inbox, ps, pr)
    second = Swap(spot, own, normed, ys, yr)
    chunks = half // CHUNK
    loop(0, chunks, lambda i: first.chunk(i, half - base, 0).start())
    gather = Gather(spot, (low0, low1), (full0, full1), *sems)
    gather.start()

    def keep(i):
        return pltpu.make_async_copy(
            rows_of(own, i * CHUNK, CHUNK), rows_of(normed, base + i * CHUNK, CHUNK), yl.at[i]
        )

    def work(i):
        first.chunk(i, half - base, 0).wait_recv()

        def one(r):
            here = pl.ds(i * CHUNK + r, STRIP)
            there = pl.ds(base + i * CHUNK + r, STRIP)
            total = (
                x[here, :]
                + (inbox[here, :].astype(jnp.float32) + part[there, :].astype(jnp.float32))
                + bias[...]
            )
            resid[here, :] = total
            own[here, :] = standardise_features(total, gain[...], shift[...])[0]

        strips(CHUNK, STRIP, one)
        second.chunk(i, 0, base).start()
        keep(i).start()

    todo = []
    for step in range(1, depth):
        todo += [(gather.z_step, 0, step), (gather.z_step, 1, step)]
        todo += [(gather.x_step, 0, step - 1), (gather.x_step, 1, step - 1)]
    todo += [(gather.x_step, 0, depth - 1), (gather.x_step, 1, depth - 1)]
    lead = chunks // 2
    loop(0, lead, work)
    for i in range(lead, chunks):
        work(i)
        if todo:
            act, a, step = todo.pop(0)
            act(a, step)
    for act, a, step in todo:
        act(a, step)

    def done(i):
        keep(i).wait()
        first.chunk(i, half - base, 0).wait_send()
        second.chunk(i, 0, base).wait_send()
        second.chunk(i, 0, half - base).wait_recv()

    loop(0, chunks, done)
    gather.finish()


def fold_rows(values):
    return jnp.sum(values.reshape(-1, 8, values.shape[-1]), axis=0)


def turn_kernel(depth, part, slope, resid, gain, grad0, grad1, dresid, low, sum0, sum1, sums, own, inbox, totals, ps, pr, ys, yr, yl, *rest):
    spot = Spot(depth)
    half = slope.shape[0]
    base = spot.t * half
    spot.greet()
    first = Swap(spot, part, inbox, ps, pr)
    second = Swap(spot, own, low, ys, yr)
    chunks = half // CHUNK
    loop(0, chunks, lambda i: first.chunk(i, half - base, 0).start())
    scatter = Scatter(
        spot, (grad0, grad1), (sum0, sum1), rest[0:2], rest[2:4], rest[4:6], rest[6:8], *rest[8:]
    )
    scatter.start()
    totals[...] = jnp.zeros_like(totals)

    def keep(i):
        return pltpu.make_async_copy(
            rows_of(own, i * CHUNK, CHUNK), rows_of(low, base + i * CHUNK, CHUNK), yl.at[i]
        )

    def work(i):
        first.chunk(i, half - base, 0).wait_recv()

        def one(r):
            here = pl.ds(i * CHUNK + r, STRIP)
            there = pl.ds(base + i * CHUNK + r, STRIP)
            grad = inbox[here, :].astype(jnp.float32) + part[there, :].astype(jnp.float32)
            values = resid[here, :]
            centred = values - jnp.mean(values, axis=-1, keepdims=True)
            spread = lax.rsqrt(jnp.mean(centred * centred, axis=-1, keepdims=True) + 1e-05)
            unit = centred * spread
            out = slope[here, :]
            total = out + standardise_features_reverse(grad, unit, spread, gain[...])
            dresid[here, :] = total
            own[here, :] = total.astype(jnp.bfloat16)
            for place, term in enumerate((total, out, grad * unit, grad)):
                totals[place] += fold_rows(term)

        strips(CHUNK, STRIP, one)
        second.chunk(i, 0, base).start()
        keep(i).start()

    for i in range(depth):
        for a in range(2):
            scatter.c_step(a, i)
    todo = [(scatter.x_step, a, i) for i in range(depth) for a in range(2)]
    lead = chunks // 2
    loop(0, lead, work)
    for i in range(lead, chunks):
        work(i)
        act, a, step = todo.pop(0)
        act(a, step)
    for act, a, step in todo:
        act(a, step)
    sums[...] = jnp.zeros_like(sums)
    for place in range(4):
        sums[place : place + 1, :] = jnp.sum(totals[place], axis=0, keepdims=True)

    for a in range(2):
        scatter.last_step(a)

    def done(i):
        keep(i).wait()
        first.chunk(i, half - base, 0).wait_send()
        second.chunk(i, 0, base).wait_send()
        second.chunk(i, 0, half - base).wait_recv()

    loop(0, chunks, done)
    scatter.finish()


def leave_kernel(depth, part, dresid, x, gain, early, split, grad0, grad1, slope, sum0, sum1, vector, inbox, totals, stage, vin, vs, vr, ps, pr, *rest):
    spot = Spot(depth)
    half = x.shape[0]
    base = spot.t * half
    spot.greet()
    first = Swap(spot, part, inbox, ps, pr)
    chunks = half // CHUNK
    loop(0, chunks, lambda i: first.chunk(i, half - base, 0).start())
    scatter = Scatter(
        spot, (grad0, grad1), (sum0, sum1), rest[0:2], rest[2:4], rest[4:6], rest[6:8], *rest[8:]
    )
    scatter.start()
    totals[...] = jnp.zeros_like(totals)

    def work(i):
        first.chunk(i, half - base, 0).wait_recv()

        def one(r):
            here = pl.ds(i * CHUNK + r, STRIP)
            there = pl.ds(base + i * CHUNK + r, STRIP)
            grad = inbox[here, :].astype(jnp.float32) + part[there, :].astype(jnp.float32)
            values = x[here, :]
            centred = values - jnp.mean(values, axis=-1, keepdims=True)
            spread = lax.rsqrt(jnp.mean(centred * centred, axis=-1, keepdims=True) + 1e-05)
            unit = centred * spread
            slope[here, :] = dresid[here, :] + standardise_features_reverse(
                grad, unit, spread, gain[...]
            )
            for place, term in enumerate((grad * unit, grad)):
                totals[place] += fold_rows(term)

        strips(CHUNK, STRIP, one)

    for i in range(depth):
        for a in range(2):
            scatter.c_step(a, i)
    todo = [(scatter.x_step, a, i) for i in range(depth) for a in range(2)]
    for i in range(chunks):
        work(i)
        if i % 2 == 1 and todo:
            act, a, step = todo.pop(0)
            act(a, step)

    stage[0, 0:8, :] = early[...]
    stage[0, 8:16, :] = split[...]
    for place in range(2):
        stage[0, 4 + place : 5 + place, :] = jnp.sum(totals[place], axis=0, keepdims=True)

    hops = [spot.twin, spot.cross]
    for number, to in enumerate(hops):
        copy = push(stage.at[number], vin.at[number], vs.at[number], vr.at[number], to)
        copy.start()
        copy.wait_recv()
        stage[number + 1] = stage[number] + vin[number]
        if todo:
            act, a, step = todo.pop(0)
            act(a, step)
    z_copies = []
    for step in range(1, depth):
        to = lax.rem(spot.z + step, depth)
        copy = push(
            stage.at[2], vin.at[2 + spot.z], vs.at[2 + to], vr.at[2 + spot.z], spot.at(to, spot.x, spot.c)
        )
        copy.start()
        z_copies.append(copy)
    for act, a, step in todo:
        act(a, step)
    vin[2 + spot.z] = stage[2]
    for step in range(1, depth):
        source = lax.rem(spot.z + step, depth)
        push(
            stage.at[2], vin.at[2 + source], vs.at[2 + source], vr.at[2 + source], spot.at(source, spot.x, spot.c)
        ).wait_recv()
    total = vin[2]
    for number in range(1, depth):
        total = total + vin[2 + number]
    stage[3] = total
    last = 2 + depth
    pair_copy = push(
        stage.at[3, pl.ds(0, 8)], vin.at[last, pl.ds(0, 8)], vs.at[last], vr.at[last], spot.pair
    )
    pair_copy.start()
    for a in range(2):
        scatter.last_step(a)
    pair_copy.wait_recv()
    vector[0:8, :] = stage[3, 0:8, :] + vin[last, 0:8, :]
    vector[8:16, :] = stage[3, 8:16, :]
    for number, to in enumerate(hops):
        push(stage.at[number], vin.at[number], vs.at[number], vr.at[number], to).wait_send()
    for copy in z_copies:
        copy.wait_send()
    pair_copy.wait_send()
    loop(0, chunks, lambda i: first.chunk(i, half - base, 0).wait_send())
    scatter.finish()


def vmem(count=1):
    return [pl.BlockSpec(memory_space=pltpu.VMEM)] * count


def anywhere(count=1):
    return [pl.BlockSpec(memory_space=pl.ANY)] * count


def call(body, number, name, depth, outs, in_specs, out_specs, scratch, args):
    size = sum(a.size * a.dtype.itemsize for a in args) + sum(
        o.size * jnp.dtype(o.dtype).itemsize for o in outs
    )
    return pl.pallas_call(
        functools.partial(body, depth),
        out_shape=outs,
        in_specs=in_specs,
        out_specs=out_specs,
        scratch_shapes=scratch,
        cost_estimate=pl.CostEstimate(flops=0, bytes_accessed=size, transcendentals=0),
        compiler_params=pltpu.CompilerParams(
            collective_id=number, has_side_effects=True, vmem_limit_bytes=48 * MIB
        ),
        name=name,
    )(*args)


def shaped(shape, dtype=jnp.bfloat16):
    return jax.ShapeDtypeStruct(shape, dtype)


def spread_call(depth, x, gain, shift, shards):
    half, width = x.shape
    dma = pltpu.SemaphoreType.DMA
    chunks = half // CHUNK
    outs = [shaped((2 * half, width))]
    outs += [shaped((4 * depth * s.shape[0], s.shape[1])) for s in shards]
    scratch = [pltpu.VMEM((half, width), jnp.bfloat16)]
    scratch += [pltpu.VMEM(s.shape, jnp.bfloat16) for s in shards]
    scratch += [dma((chunks,))] * 3 + Gather.semaphores(2, depth)
    return call(
        spread_kernel, 0, "spread", depth, outs, vmem(5), anywhere(3), scratch,
        (x, gain[None], shift[None], *shards),
    )


def middle_call(depth, part, x, bias, gain, shift, shards):
    half, width = x.shape
    dma = pltpu.SemaphoreType.DMA
    chunks = half // CHUNK
    outs = [shaped((half, width), jnp.float32), shaped((2 * half, width))]
    outs += [shaped((4 * depth * s.shape[0], s.shape[1])) for s in shards]
    scratch = [pltpu.VMEM((half, width), jnp.bfloat16)]
    scratch += [pltpu.VMEM(s.shape, jnp.bfloat16) for s in shards]
    scratch += [pltpu.VMEM((half, width), jnp.bfloat16)]
    scratch += [dma((chunks,))] * 5 + Gather.semaphores(2, depth)
    return call(
        middle_kernel, 1, "middle", depth, outs, vmem(7), vmem() + anywhere(3), scratch,
        (part, x, bias[None], gain[None], shift[None], *shards),
    )


def turn_call(depth, part, slope, resid, gain, grads):
    half, width = slope.shape
    dma = pltpu.SemaphoreType.DMA
    chunks = half // CHUNK
    shapes = [(g.shape[0] // (4 * depth), g.shape[1]) for g in grads]
    outs = [shaped((half, width), jnp.float32), shaped((2 * half, width))]
    outs += [shaped(s, jnp.float32) for s in shapes] + [shaped((8, width), jnp.float32)]
    scratch = [pltpu.VMEM((half, width), jnp.bfloat16)] * 2
    scratch += [pltpu.VMEM((4, 8, width), jnp.float32)]
    scratch += [dma((chunks,))] * 5 + Scatter.scratch(shapes, depth)
    return call(
        turn_kernel, 2, "turn", depth, outs, vmem(4) + anywhere(2),
        vmem() + anywhere() + vmem(3), scratch, (part, slope, resid, gain[None], *grads),
    )


def leave_call(depth, part, dresid, x, gain, early, split, grads):
    half, width = x.shape
    dma = pltpu.SemaphoreType.DMA
    chunks = half // CHUNK
    shapes = [(g.shape[0] // (4 * depth), g.shape[1]) for g in grads]
    outs = [shaped((half, width), jnp.float32)]
    outs += [shaped(s, jnp.float32) for s in shapes] + [shaped((16, width), jnp.float32)]
    scratch = [pltpu.VMEM((half, width), jnp.bfloat16)]
    scratch += [pltpu.VMEM((2, 8, width), jnp.float32)]
    scratch += [pltpu.VMEM((4, 16, width), jnp.float32)]
    scratch += [pltpu.VMEM((3 + depth, 16, width), jnp.float32)]
    scratch += [dma((3 + depth,))] * 2 + [dma((chunks,))] * 2 + Scatter.scratch(shapes, depth)
    return call(
        leave_kernel, 3, "leave", depth, outs, vmem(6) + anywhere(2), vmem(4), scratch,
        (part, dresid, x, gain[None], early, split, *grads),
    )


def linked(
    entering_activations,
    segment_ids,
    leaving_activation_slope,
    qkv_weight,
    qv_bias,
    dense_weight,
    dense_bias,
    up_weight,
    up_bias,
    down_weight,
    down_bias,
    mixer_scale_factor,
    mixer_offset_term,
    perceptron_scale_factor,
    perceptron_offset_term,
):
    depth = lax.axis_size("dp") // 4
    rank = lax.axis_index("tensor")
    local_heads = qkv_weight.shape[1] // (3 * HEAD_DIM)
    slopes = head_slopes(rank * local_heads, local_heads)
    segments = segment_ids[0]
    ones, qkv_low, dense_low = spread_call(
        depth,
        entering_activations,
        mixer_scale_factor,
        mixer_offset_term,
        (qkv_weight, dense_weight.T),
    )
    out_own, ones = lax.optimization_barrier(
        (leaving_activation_slope.astype(jnp.bfloat16), ones)
    )
    outs = to_order([out_own, swap(out_own)], rank)
    qkv = (product(ones, qkv_low) + full_bias(qv_bias, local_heads)).astype(jnp.bfloat16)
    context = attention_forward(qkv, segments, slopes)
    dense_part = times_transposed(context, dense_low).astype(jnp.bfloat16)
    resid, twos, up_low, down_low = middle_call(
        depth,
        dense_part,
        entering_activations,
        dense_bias,
        perceptron_scale_factor,
        perceptron_offset_term,
        (up_weight, down_weight.T),
    )
    act_val, act_slope = gelu_parts(product(twos, up_low) + up_bias)
    act = act_val.astype(jnp.bfloat16)
    dpre = product(outs, down_low) * act_slope
    up_bias_part = jnp.sum(dpre, axis=0)
    dpre_low = dpre.astype(jnp.bfloat16)
    norm_part = times_transposed(dpre_low, up_low).astype(jnp.bfloat16)
    down_part = times_transposed(act, down_low).astype(jnp.bfloat16)
    grad_down = inner_rows(outs, act).astype(jnp.bfloat16)
    grad_up = inner_rows(twos, dpre_low).astype(jnp.bfloat16)
    dresid, resid_low, grad_up, grad_down, early = turn_call(
        depth,
        norm_part,
        leaving_activation_slope,
        resid,
        perceptron_scale_factor,
        (grad_up, grad_down),
    )
    down_part, resid_low = lax.optimization_barrier((down_part, resid_low))
    block_out = resid + fold(from_order(down_part, rank, 2), 2) + down_bias
    dcontext = times_transposed(resid_low, jnp.swapaxes(dense_low, 0, 1)).astype(jnp.bfloat16)
    grad_dense = inner_rows(resid_low, context).astype(jnp.bfloat16)
    dqkv_low, dqkv_sums = attention_backward(qkv, segments, slopes, dcontext)
    grad_qkv = inner_rows(ones, dqkv_low).astype(jnp.bfloat16)
    triple = dqkv_sums.reshape(local_heads, 3, HEAD_DIM)
    qv_part = jnp.stack([triple[:, 0], triple[:, 2]], axis=1).reshape(-1)
    mixer_part = times_transposed(dqkv_low, qkv_low).astype(jnp.bfloat16)
    split = jnp.concatenate([up_bias_part, qv_part]).reshape(-1, D)
    split = jnp.pad(split, ((0, 8 - split.shape[0]), (0, 0)))
    entering_slope, grad_qkv, grad_dense, vector = leave_call(
        depth,
        mixer_part,
        dresid,
        entering_activations,
        mixer_scale_factor,
        early,
        split,
        (grad_qkv, grad_dense),
    )
    ups = up_bias.size
    rest = vector[8:].reshape(-1)
    return (
        block_out,
        entering_slope,
        (
            grad_qkv,
            rest[ups : ups + qv_bias.size],
            grad_dense.T,
            vector[0],
            grad_up,
            rest[:ups],
            grad_down.T,
            vector[1],
            vector[4],
            vector[5],
            vector[2],
            vector[3],
        ),
    )


def general(
    entering_activations,
    segment_ids,
    leaving_activation_slope,
    qkv_weight,
    qv_bias,
    dense_weight,
    dense_bias,
    up_weight,
    up_bias,
    down_weight,
    down_bias,
    mixer_scale_factor,
    mixer_offset_term,
    perceptron_scale_factor,
    perceptron_offset_term,
):
    qkv_low, dense_low, up_low, down_low = (
        lax.all_gather(qkv_weight.astype(jnp.bfloat16), "dp", axis=0, tiled=True),
        lax.all_gather(dense_weight.astype(jnp.bfloat16), "dp", axis=1, tiled=True),
        lax.all_gather(up_weight.astype(jnp.bfloat16), "dp", axis=0, tiled=True),
        lax.all_gather(down_weight.astype(jnp.bfloat16), "dp", axis=1, tiled=True),
    )
    local_heads = qkv_low.shape[1] // (3 * HEAD_DIM)
    tensor_rank = lax.axis_index("tensor")
    count = lax.axis_size("tensor")
    slopes = head_slopes(tensor_rank * local_heads, local_heads)
    segments = segment_ids[0]
    mixer_standardised, mixer_unit_spread1, mixer_reciprocal_spread1 = standardise_features(
        entering_activations, mixer_scale_factor, mixer_offset_term
    )
    ones = spread(mixer_standardised, count)
    outs = spread(leaving_activation_slope.astype(jnp.bfloat16), count)
    qkv_bias = full_bias(qv_bias, local_heads)
    qkv = to_order([(product(one, qkv_low) + qkv_bias).astype(jnp.bfloat16) for one in ones], tensor_rank)
    context = attention_forward(qkv, segments, slopes)
    contexts = from_order(context, tensor_rank, count)
    skip_path_sum = (
        entering_activations
        + fold([product(part, dense_low).astype(jnp.bfloat16) for part in contexts], count)
        + dense_bias
    )
    perceptron_standardised, perceptron_unit_spread2, perceptron_reciprocal_spread2 = (
        standardise_features(skip_path_sum, perceptron_scale_factor, perceptron_offset_term)
    )
    twos = spread(perceptron_standardised, count)
    acts, dpres, dpre_lows, pre_parts = [], [], [], []
    for two, out in zip(twos, outs):
        act_val, act_slope = gelu_parts(product(two, up_low) + up_bias)
        acts.append(act_val.astype(jnp.bfloat16))
        dpres.append(times_transposed(out, down_low) * act_slope)
        dpre_lows.append(dpres[-1].astype(jnp.bfloat16))
        pre_parts.append(times_transposed(dpre_lows[-1], up_low).astype(jnp.bfloat16))
    pre_perceptron_sensitivity = fold(pre_parts, count)
    block_out = (
        skip_path_sum
        + fold([product(act, down_low).astype(jnp.bfloat16) for act in acts], count)
        + down_bias
    )
    contraction_sensitivity = add_up(acts, outs).astype(jnp.bfloat16)
    expansion_sensitivity = add_up(twos, dpre_lows).astype(jnp.bfloat16)
    up_bias_part = sum(jnp.sum(dpre, axis=0) for dpre in dpres)
    skip_path_sensitivity = leaving_activation_slope + standardise_features_reverse(
        pre_perceptron_sensitivity,
        perceptron_unit_spread2,
        perceptron_reciprocal_spread2,
        perceptron_scale_factor,
    )
    resids = spread(skip_path_sensitivity.astype(jnp.bfloat16), count)
    mixer_merge_sensitivity = add_up(contexts, resids).astype(jnp.bfloat16)
    dcontext = to_order(
        [times_transposed(resid, dense_low).astype(jnp.bfloat16) for resid in resids], tensor_rank
    )
    dqkv_low, dqkv_sums = attention_backward(qkv, segments, slopes, dcontext)
    dqkv_lows = from_order(dqkv_low, tensor_rank, count)
    packed_triple_slope = add_up(ones, dqkv_lows).astype(jnp.bfloat16)
    triple = dqkv_sums.reshape(local_heads, 3, HEAD_DIM)
    qv_part = jnp.stack([triple[:, 0], triple[:, 2]], axis=1).reshape(-1)
    pre_mixer_sensitivity = fold(
        [times_transposed(part, qkv_low).astype(jnp.bfloat16) for part in dqkv_lows], count
    )
    entering_activation_slope = skip_path_sensitivity + standardise_features_reverse(
        pre_mixer_sensitivity, mixer_unit_spread1, mixer_reciprocal_spread1, mixer_scale_factor
    )
    early, up_bias_grad = total_over_all(
        jnp.concatenate(
            [
                jnp.sum(skip_path_sensitivity, axis=0),
                jnp.sum(leaving_activation_slope, axis=0),
                jnp.sum(pre_perceptron_sensitivity * perceptron_unit_spread2, axis=0),
                jnp.sum(pre_perceptron_sensitivity, axis=0),
                up_bias_part,
            ]
        ),
        4 * D,
        tensor_rank,
    )
    dense_bias_grad, down_bias_grad, gain_two_grad, shift_two_grad = jnp.split(early, 4)
    late, qv_bias_grad = total_over_all(
        jnp.concatenate(
            [
                jnp.sum(pre_mixer_sensitivity * mixer_unit_spread1, axis=0),
                jnp.sum(pre_mixer_sensitivity, axis=0),
                qv_part,
            ]
        ),
        2 * D,
        tensor_rank,
    )
    gain_one_grad, shift_one_grad = jnp.split(late, 2)
    packed_triple_slope, mixer_merge_sensitivity, expansion_sensitivity, contraction_sensitivity = (
        part.astype(jnp.float32)
        for part in (
            lax.psum_scatter(packed_triple_slope, "dp", scatter_dimension=0, tiled=True),
            lax.psum_scatter(mixer_merge_sensitivity, "dp", scatter_dimension=1, tiled=True),
            lax.psum_scatter(expansion_sensitivity, "dp", scatter_dimension=0, tiled=True),
            lax.psum_scatter(contraction_sensitivity, "dp", scatter_dimension=1, tiled=True),
        )
    )
    return block_out, entering_activation_slope, (
        packed_triple_slope,
        qv_bias_grad,
        mixer_merge_sensitivity,
        dense_bias_grad,
        expansion_sensitivity,
        up_bias_grad,
        contraction_sensitivity,
        down_bias_grad,
        gain_one_grad,
        shift_one_grad,
        gain_two_grad,
        shift_two_grad,
    )


def local(
    entering_activations,
    segment_ids,
    leaving_activation_slope,
    qkv_weight,
    qv_bias,
    dense_weight,
    dense_bias,
    up_weight,
    up_bias,
    down_weight,
    down_bias,
    mixer_scale_factor,
    mixer_offset_term,
    perceptron_scale_factor,
    perceptron_offset_term,
    first_qkv_weight,
    first_qv_bias,
    first_dense_weight,
    first_dense_bias,
    first_up_weight,
    first_up_bias,
    first_down_weight,
    first_down_bias,
    first_norm1_gain,
    first_norm1_bias,
    first_norm2_gain,
    first_norm2_bias,
    second_qkv_weight,
    second_qv_bias,
    second_dense_weight,
    second_dense_bias,
    second_up_weight,
    second_up_bias,
    second_down_weight,
    second_down_bias,
    second_norm1_gain,
    second_norm1_bias,
    second_norm2_gain,
    second_norm2_bias,
):
    params = (
        qkv_weight,
        qv_bias,
        dense_weight,
        dense_bias,
        up_weight,
        up_bias,
        down_weight,
        down_bias,
        mixer_scale_factor,
        mixer_offset_term,
        perceptron_scale_factor,
        perceptron_offset_term,
    )
    firsts = (
        first_qkv_weight,
        first_qv_bias,
        first_dense_weight,
        first_dense_bias,
        first_up_weight,
        first_up_bias,
        first_down_weight,
        first_down_bias,
        first_norm1_gain,
        first_norm1_bias,
        first_norm2_gain,
        first_norm2_bias,
    )
    seconds = (
        second_qkv_weight,
        second_qv_bias,
        second_dense_weight,
        second_dense_bias,
        second_up_weight,
        second_up_bias,
        second_down_weight,
        second_down_bias,
        second_norm1_gain,
        second_norm1_bias,
        second_norm2_gain,
        second_norm2_bias,
    )
    whole_line = lax.axis_size("tensor") == 2 and lax.axis_size("dp") % 4 == 0
    route = linked if whole_line and segment_ids.shape[0] == 1 else general
    block_out, entering_activation_slope, parameter_slopes = route(
        entering_activations,
        segment_ids,
        leaving_activation_slope,
        qkv_weight,
        qv_bias,
        dense_weight,
        dense_bias,
        up_weight,
        up_bias,
        down_weight,
        down_bias,
        mixer_scale_factor,
        mixer_offset_term,
        perceptron_scale_factor,
        perceptron_offset_term,
    )
    results = []
    for index in range(12):
        matrix = index in (0, 2, 4, 6)
        results.append(
            adamw(
                params[index],
                parameter_slopes[index],
                firsts[index],
                seconds[index],
                0.01 if matrix else 0.1,
                0.1 if matrix else 0.0,
            )
        )
    news = [r[0] for r in results]
    moments_one = [r[1] for r in results]
    moments_two = [r[2] for r in results]
    return (
        block_out,
        entering_activation_slope,
        *parameter_slopes,
        *news,
        *moments_one,
        *moments_two,
    )


def solution(mesh):
    in_specs = (
        P(("dp", "tensor"), None),
        P("dp", None),
        P(("dp", "tensor"), None),
        P("dp", "tensor"),
        P("tensor"),
        P("tensor", "dp"),
        P(),
        P("dp", "tensor"),
        P("tensor"),
        P("tensor", "dp"),
        P(),
        P(),
        P(),
        P(),
        P(),
        P("dp", "tensor"),
        P("tensor"),
        P("tensor", "dp"),
        P(),
        P("dp", "tensor"),
        P("tensor"),
        P("tensor", "dp"),
        P(),
        P(),
        P(),
        P(),
        P(),
        P("dp", "tensor"),
        P("tensor"),
        P("tensor", "dp"),
        P(),
        P("dp", "tensor"),
        P("tensor"),
        P("tensor", "dp"),
        P(),
        P(),
        P(),
        P(),
        P(),
    )
    out_specs = (
        P(("dp", "tensor"), None),
        P(("dp", "tensor"), None),
        P("dp", "tensor"),
        P("tensor"),
        P("tensor", "dp"),
        P(),
        P("dp", "tensor"),
        P("tensor"),
        P("tensor", "dp"),
        P(),
        P(),
        P(),
        P(),
        P(),
        P("dp", "tensor"),
        P("tensor"),
        P("tensor", "dp"),
        P(),
        P("dp", "tensor"),
        P("tensor"),
        P("tensor", "dp"),
        P(),
        P(),
        P(),
        P(),
        P(),
        P("dp", "tensor"),
        P("tensor"),
        P("tensor", "dp"),
        P(),
        P("dp", "tensor"),
        P("tensor"),
        P("tensor", "dp"),
        P(),
        P(),
        P(),
        P(),
        P(),
        P("dp", "tensor"),
        P("tensor"),
        P("tensor", "dp"),
        P(),
        P("dp", "tensor"),
        P("tensor"),
        P("tensor", "dp"),
        P(),
        P(),
        P(),
        P(),
        P(),
    )
    return jax.shard_map(local, mesh=mesh, in_specs=in_specs, out_specs=out_specs, check_vma=False)
```

```python
import functools

import jax
import jax.numpy as jnp
from jax import lax
from jax.experimental import pallas as pl
from jax.experimental.pallas import tpu as pltpu
from jax.sharding import PartitionSpec as P

D = 1024
FOCUS_COUNT = 16
FF = 4096
ADAM_STEP = 4
HEAD_DIM = 64
MAX_SPAN = 512


beta_first = 0.9
beta_second = 0.95


def standardise_features(values, elementwise_multiplier, additive_offset):
    feature_midpoint = jnp.mean(values, axis=-1, keepdims=True)
    demeaned_entries = values - feature_midpoint
    reciprocal_spread = lax.rsqrt(
        jnp.mean(demeaned_entries * demeaned_entries, axis=-1, keepdims=True) + 1e-05
    )
    unit_spread_entries = demeaned_entries * reciprocal_spread
    return (
        (unit_spread_entries * elementwise_multiplier + additive_offset).astype(jnp.bfloat16),
        unit_spread_entries,
        reciprocal_spread,
    )


def standardise_features_reverse(
    loss_slope, unit_spread_entries, reciprocal_spread, elementwise_multiplier
):
    multiplied_entries = loss_slope * elementwise_multiplier
    return reciprocal_spread * (
        multiplied_entries
        - jnp.mean(multiplied_entries, axis=-1, keepdims=True)
        - unit_spread_entries
        * jnp.mean(multiplied_entries * unit_spread_entries, axis=-1, keepdims=True)
    )


def gelu_parts(pre):
    inner = 0.7978845608 * (pre + 0.044715 * pre * pre * pre)
    tanh_val = jnp.tanh(inner)
    value = 0.5 * pre * (1.0 + tanh_val)
    slope = 0.5 * (1.0 + tanh_val) + 0.5 * pre * (1.0 - tanh_val * tanh_val) * 0.7978845608 * (
        1.0 + 3.0 * 0.044715 * pre * pre
    )
    return (value, slope)


def inner_rows(left, right):
    return lax.dot_general(
        left, right, (((0,), (0,)), ((), ())), preferred_element_type=jnp.float32
    )


def times_transposed(left, right):
    return lax.dot_general(
        left, right, (((1,), (1,)), ((), ())), preferred_element_type=jnp.float32
    )


def head_slopes(first, count):
    index = (first + jnp.arange(count)).astype(jnp.float32)
    return jnp.exp2(-8.0 * (index + 1.0) / FOCUS_COUNT)


def full_bias(qv_bias, heads):
    pair = qv_bias.reshape(heads, 2, HEAD_DIM)
    return jnp.stack([pair[:, 0], jnp.zeros_like(pair[:, 0]), pair[:, 1]], axis=1).reshape(
        heads * 3 * HEAD_DIM
    )


def window(start, block, length):
    return (max(0, start - MAX_SPAN), min(length, start + block))


def fill_offsets(offsets, rows_seg, cols_seg, rows_first, length, block):
    for start in range(0, length, block):
        low, high = window(start, block, length)
        shape = (block, high - low) if rows_first else (high - low, block)
        axis = 0 if rows_first else 1
        row = start + lax.broadcasted_iota(jnp.int32, shape, axis)
        col = low + lax.broadcasted_iota(jnp.int32, shape, 1 - axis)
        if rows_first:
            same = rows_seg[start : start + block, :] == cols_seg[:, low:high]
        else:
            same = rows_seg[low:high, :] == cols_seg[:, start : start + block]
        allowed = (col <= row) & same
        value = jnp.where(allowed, (col - row).astype(jnp.float32), -1e30)
        if rows_first:
            offsets[start : start + block, 0 : high - low] = value
        else:
            offsets[0 : high - low, start : start + block] = value


def forward_kernel(block, slopes, x, rows_seg, cols_seg, out, offsets):
    length = x.shape[0]
    step = pl.program_id(0)

    @pl.when(step == 0)
    def _():
        fill_offsets(offsets, rows_seg, cols_seg, True, length, block)

    for i in range(2):
        base = 3 * HEAD_DIM * i
        slope = slopes[2 * step + i]
        query = x[:, base : base + HEAD_DIM] * HEAD_DIM ** (-0.5)
        keys = x[:, base + HEAD_DIM : base + 2 * HEAD_DIM]
        values = x[:, base + 2 * HEAD_DIM : base + 3 * HEAD_DIM]
        for start in range(0, length, block):
            low, high = window(start, block, length)
            scores = (
                times_transposed(query[start : start + block], keys[low:high])
                + slope * offsets[start : start + block, 0 : high - low]
            )
            peak = jnp.max(scores, axis=1, keepdims=True)
            raised = jnp.exp(scores - peak)
            total = jnp.sum(raised, axis=1, keepdims=True)
            probs = (raised * (1.0 / total)).astype(jnp.bfloat16)
            context = jnp.dot(probs, values[low:high], preferred_element_type=jnp.float32)
            out[start : start + block, HEAD_DIM * i : HEAD_DIM * (i + 1)] = context.astype(
                jnp.bfloat16
            )


def backward_kernel(
    block, slopes, x, grad, rows_seg, cols_seg, out, sums, offsets, dkeys, dvalues, dquery
):
    length = x.shape[0]
    step = pl.program_id(0)
    scale = HEAD_DIM ** (-0.5)

    @pl.when(step == 0)
    def _():
        fill_offsets(offsets, rows_seg, cols_seg, False, length, block)

    for i in range(2):
        base = 3 * HEAD_DIM * i
        slope = slopes[2 * step + i]
        query = x[:, base : base + HEAD_DIM] * scale
        keys = x[:, base + HEAD_DIM : base + 2 * HEAD_DIM]
        values = x[:, base + 2 * HEAD_DIM : base + 3 * HEAD_DIM]
        slopes_out = grad[:, HEAD_DIM * i : HEAD_DIM * (i + 1)]
        dkeys[...] = jnp.zeros_like(dkeys)
        dvalues[...] = jnp.zeros_like(dvalues)
        for start in range(0, length, block):
            low, high = window(start, block, length)
            query_block = query[start : start + block]
            grad_block = slopes_out[start : start + block]
            scores = (
                times_transposed(keys[low:high], query_block)
                + slope * offsets[0 : high - low, start : start + block]
            )
            peak = jnp.max(scores, axis=0, keepdims=True)
            raised = jnp.exp(scores - peak)
            total = jnp.sum(raised, axis=0, keepdims=True)
            probs = raised * (1.0 / total)
            dprob = times_transposed(values[low:high], grad_block)
            delta = jnp.sum(probs * dprob, axis=0, keepdims=True)
            dscore = (probs * (dprob - delta)).astype(jnp.bfloat16)
            dvalues[low:high, :] += jnp.dot(
                probs.astype(jnp.bfloat16), grad_block, preferred_element_type=jnp.float32
            )
            dkeys[low:high, :] += jnp.dot(dscore, query_block, preferred_element_type=jnp.float32)
            dquery[start : start + block, :] = inner_rows(dscore, keys[low:high]) * scale
        for place, part in enumerate((dquery, dkeys, dvalues)):
            first = base + HEAD_DIM * place
            out[:, first : first + HEAD_DIM] = part[...].astype(jnp.bfloat16)
            sums[:, first : first + HEAD_DIM] = jnp.sum(part[...], axis=0, keepdims=True)


def attention_forward(qkv, segments, slopes):
    length, width = qkv.shape
    pairs = width // (6 * HEAD_DIM)
    block = min(256, length)
    span = min(length, block + MAX_SPAN)
    return pl.pallas_call(
        functools.partial(forward_kernel, block),
        grid=(pairs,),
        out_shape=jax.ShapeDtypeStruct((length, width // 3), jnp.bfloat16),
        in_specs=[
            pl.BlockSpec(memory_space=pltpu.SMEM),
            pl.BlockSpec((length, 6 * HEAD_DIM), lambda p: (0, p)),
            pl.BlockSpec((length, 1), lambda p: (0, 0)),
            pl.BlockSpec((1, length), lambda p: (0, 0)),
        ],
        out_specs=pl.BlockSpec((length, 2 * HEAD_DIM), lambda p: (0, p)),
        scratch_shapes=[pltpu.VMEM((length, span), jnp.float32)],
        cost_estimate=pl.CostEstimate(
            flops=4 * length * span * width // 3,
            bytes_accessed=8 * length * width // 3,
            transcendentals=length * span * pairs * 2,
        ),
        compiler_params=pltpu.CompilerParams(vmem_limit_bytes=40 * 1024 * 1024),
        name="attention_forward",
    )(slopes, qkv, segments[:, None], segments[None, :])


def attention_backward(qkv, segments, slopes, dcontext):
    length, width = qkv.shape
    pairs = width // (6 * HEAD_DIM)
    block = min(256, length)
    span = min(length, block + MAX_SPAN)
    return pl.pallas_call(
        functools.partial(backward_kernel, block),
        grid=(pairs,),
        out_shape=(
            jax.ShapeDtypeStruct((length, width), jnp.bfloat16),
            jax.ShapeDtypeStruct((1, width), jnp.float32),
        ),
        in_specs=[
            pl.BlockSpec(memory_space=pltpu.SMEM),
            pl.BlockSpec((length, 6 * HEAD_DIM), lambda p: (0, p)),
            pl.BlockSpec((length, 2 * HEAD_DIM), lambda p: (0, p)),
            pl.BlockSpec((length, 1), lambda p: (0, 0)),
            pl.BlockSpec((1, length), lambda p: (0, 0)),
        ],
        out_specs=(
            pl.BlockSpec((length, 6 * HEAD_DIM), lambda p: (0, p)),
            pl.BlockSpec((1, 6 * HEAD_DIM), lambda p: (0, p)),
        ),
        scratch_shapes=[
            pltpu.VMEM((span, length), jnp.float32),
            pltpu.VMEM((length, HEAD_DIM), jnp.float32),
            pltpu.VMEM((length, HEAD_DIM), jnp.float32),
            pltpu.VMEM((length, HEAD_DIM), jnp.float32),
        ],
        cost_estimate=pl.CostEstimate(
            flops=10 * length * span * width // 3,
            bytes_accessed=14 * length * width // 3,
            transcendentals=length * span * pairs * 2,
        ),
        compiler_params=pltpu.CompilerParams(vmem_limit_bytes=40 * 1024 * 1024),
        name="attention_backward",
    )(slopes, qkv, dcontext, segments[:, None], segments[None, :])


def swap(values):
    return lax.ppermute(values, "tensor", [(0, 1), (1, 0)])


def spread(values, count):
    if count == 2:
        return [values, swap(values)]
    return [lax.all_gather(values, "tensor", axis=0, tiled=True)]


def fold(parts, count):
    if count == 2:
        return swap(parts[1]).astype(jnp.float32) + parts[0].astype(jnp.float32)
    return lax.psum_scatter(parts[0], "tensor", scatter_dimension=0, tiled=True).astype(
        jnp.float32
    )


def to_order(parts, rank):
    if len(parts) == 2:
        own, other = parts
        return jnp.concatenate(
            [jnp.where(rank == 0, own, other), jnp.where(rank == 0, other, own)], axis=0
        )
    return parts[0]


def from_order(values, rank, count):
    if count == 2:
        half = values.shape[0] // 2
        return [
            lax.dynamic_slice_in_dim(values, rank * half, half, 0),
            lax.dynamic_slice_in_dim(values, (1 - rank) * half, half, 0),
        ]
    return [values]


def product(left, right):
    return jnp.dot(left, right, preferred_element_type=jnp.float32)


def add_up(lefts, rights):
    total = inner_rows(lefts[0], rights[0])
    for left, right in zip(lefts[1:], rights[1:]):
        total = total + inner_rows(left, right)
    return total


def total_over_all(vector, shared, rank):
    rows = lax.all_gather(vector[None], ("dp", "tensor"), axis=0, tiled=True)
    everyone = jnp.sum(rows[:, :shared], axis=0)
    count = lax.axis_size("tensor")
    split = rows[:, shared:].reshape(rows.shape[0] // count, count, -1)
    mine = lax.dynamic_index_in_dim(jnp.sum(split, axis=0), rank, 0, keepdims=False)
    return everyone, mine


def adamw(param, loss_slope, first, second, rate, decay):
    first_new = beta_first * first + (1.0 - beta_first) * loss_slope
    second_new = beta_second * second + (1.0 - beta_second) * loss_slope * loss_slope
    update = (
        first_new
        / (1.0 - beta_first**ADAM_STEP)
        / (jnp.sqrt(second_new / (1.0 - beta_second**ADAM_STEP)) + 1e-08)
    )
    return (param - rate * (update + decay * param), first_new, second_new)


MESH = pl.DeviceIdType.MESH
CHUNK = 64
MIB = 1024 * 1024


class Spot:
    def __init__(self, depth):
        dp = lax.axis_index("dp")
        self.depth = depth
        self.t = lax.axis_index("tensor")
        self.c = lax.rem(dp, 2)
        self.x = lax.rem(lax.div(dp, 2), 2)
        self.z = lax.div(dp, 4)
        self.twin = self.at(self.z, self.x, 1 - self.c)
        self.cross = self.at(self.z, 1 - self.x, self.c)
        self.pair = (dp, 1 - self.t)

    def index(self, z, x, c):
        return (z * 2 + x) * 2 + c

    def at(self, z, x, c):
        return (self.index(z, x, c), self.t)

    def farthest(self, i):
        n = self.depth
        if i == n - 1:
            return self.z
        down = jnp.where(n - 1 - i > self.z, n - 1 - i, n - 2 - i)
        up = jnp.where(i < self.z, i, i + 1)
        return jnp.where(2 * self.z < n, down, up)

    def greet(self, everyone=True):
        barrier = pltpu.get_barrier_semaphore()
        others = [self.twin, self.cross, self.pair] if everyone else [self.pair]
        for step in range(1, self.depth if everyone else 1):
            others.append(self.at(lax.rem(self.z + step, self.depth), self.x, self.c))
        for other in others:
            pl.semaphore_signal(barrier, inc=1, device_id=other, device_id_type=MESH)
        pl.semaphore_wait(barrier, len(others))


def push(source, target, send, arrive, to):
    return pltpu.make_async_remote_copy(
        src_ref=source,
        dst_ref=target,
        send_sem=send,
        recv_sem=arrive,
        device_id=to,
        device_id_type=MESH,
    )


def rows_of(ref, first, size):
    return ref.at[pl.ds(pl.multiple_of(first, size), size)]


class Gather:
    def __init__(self, spot, shards, fulls, zs, zr, xs, xr, cs, cr, ls):
        self.spot, self.shards, self.fulls = spot, shards, fulls
        self.zs, self.zr, self.xs, self.xr, self.cs, self.cr, self.ls = zs, zr, xs, xr, cs, cr, ls
        self.count = len(shards)

    @staticmethod
    def semaphores(count, depth):
        dma = pltpu.SemaphoreType.DMA
        return [
            dma((count, depth, 2)),
            dma((count, depth)),
            dma((count, depth)),
            dma((count, depth)),
            dma((count, 2 * depth)),
            dma((count, 2 * depth)),
            dma((count,)),
        ]

    def block(self, a, z, x, c):
        size = self.shards[a].shape[0]
        return rows_of(self.fulls[a], self.spot.index(z, x, c) * size, size)

    def along(self, a, bz, way, own=False):
        s = self.spot
        region = self.block(a, bz, s.x, s.c)
        to = s.at(s.z + (1 if way == 0 else -1), s.x, s.c)
        return push(
            self.shards[a] if own else region, region, self.zs.at[a, bz, way], self.zr.at[a, bz], to
        )

    def over(self, a, bz, own=False):
        s = self.spot
        region = self.block(a, bz, s.x, s.c)
        return push(
            self.shards[a] if own else region, region, self.xs.at[a, bz], self.xr.at[a, bz], s.cross
        )

    def across(self, a, bz, bx, own=False):
        s = self.spot
        region = self.block(a, bz, bx, s.c)
        k = bz * 2 + bx
        return push(
            self.shards[a] if own else region, region, self.cs.at[a, k], self.cr.at[a, k], s.twin
        )

    def keep(self, a):
        s = self.spot
        return pltpu.make_async_copy(
            self.shards[a], self.block(a, s.z, s.x, s.c), self.ls.at[a]
        )

    def start(self):
        s = self.spot
        for a in range(self.count):
            pl.when(s.z + 1 < s.depth)(lambda a=a: self.along(a, s.z, 0, True).start())
            pl.when(s.z > 0)(lambda a=a: self.along(a, s.z, 1, True).start())
            self.over(a, s.z, True).start()
        for a in range(self.count):
            self.across(a, s.z, s.x, True).start()
            self.keep(a).start()

    def z_step(self, a, step):
        s = self.spot
        for way in (0, 1):
            bz = s.z - step if way == 0 else s.z + step
            here = bz >= 0 if way == 0 else bz < s.depth
            onward = s.z + 1 < s.depth if way == 0 else s.z > 0

            @pl.when(here)
            def _():
                self.along(a, bz, way).wait_recv()
                pl.when(onward)(lambda: self.along(a, bz, way).start())
                self.over(a, bz).start()
                self.across(a, bz, s.x).start()

    def x_step(self, a, step):
        s = self.spot

        def take(bz):
            self.over(a, bz).wait_recv()
            self.across(a, bz, 1 - s.x).start()

        if step == 0:
            take(s.z)
            return
        pl.when(s.z - step >= 0)(lambda: take(s.z - step))
        pl.when(s.z + step < s.depth)(lambda: take(s.z + step))

    def finish(self):
        s = self.spot
        for a in range(self.count):
            self.keep(a).wait()
            for bz in range(s.depth):
                for bx in range(2):
                    self.across(a, bz, bx).wait()
                self.over(a, bz).wait_send()
                pl.when((bz <= s.z) & (s.z + 1 < s.depth))(
                    lambda a=a, bz=bz: self.along(a, bz, 0).wait_send()
                )
                pl.when((bz >= s.z) & (s.z > 0))(
                    lambda a=a, bz=bz: self.along(a, bz, 1).wait_send()
                )


STRIP = 16
BAND = 64


def strips(size, step, body):
    def one(i, carry):
        body(pl.multiple_of(i * step, step))
        return carry

    lax.fori_loop(0, size // step, one, 0)


class Scatter:
    def __init__(self, spot, grads, sums, cins, xins, zins, cs, cr, xs, xr, zs, zr):
        self.spot, self.grads, self.sums = spot, grads, sums
        self.cins, self.xins, self.zins = cins, xins, zins
        self.cs, self.cr, self.xs, self.xr, self.zs, self.zr = cs, cr, xs, xr, zs, zr
        self.count = len(grads)

    @staticmethod
    def scratch(shapes, depth):
        count, low = len(shapes), jnp.bfloat16
        dma = pltpu.SemaphoreType.DMA
        buffers = []
        for slots in (2 * depth, depth, depth):
            for rows, width in shapes:
                buffers.append(pltpu.VMEM((slots, rows, width), low))
        return buffers + [
            dma((count, 2 * depth)),
            dma((count, 2 * depth)),
            dma((count, depth)),
            dma((count, depth)),
            dma((count, depth)),
            dma((count, depth)),
        ]

    def first(self, a, z, x, c):
        return self.spot.index(z, x, c) * self.sums[a].shape[0]

    def across(self, a, bz, bx):
        s = self.spot
        k = bz * 2 + bx
        return push(
            rows_of(self.grads[a], self.first(a, bz, bx, 1 - s.c), self.sums[a].shape[0]),
            self.cins[a].at[k],
            self.cs.at[a, k],
            self.cr.at[a, k],
            s.twin,
        )

    def over(self, a, bz):
        s = self.spot
        return push(
            self.cins[a].at[bz * 2 + 1 - s.x],
            self.xins[a].at[bz],
            self.xs.at[a, bz],
            self.xr.at[a, bz],
            s.cross,
        )

    def along(self, a, bz, arriving=False):
        s = self.spot
        slot = bz if arriving else s.z
        return push(
            self.cins[a].at[bz * 2 + s.x],
            self.zins[a].at[slot],
            self.zs.at[a, bz],
            self.zr.at[a, slot],
            s.at(bz, s.x, s.c),
        )

    def start(self):
        s = self.spot
        for bx in (1 - s.x, s.x):
            for i in range(s.depth):
                for a in range(self.count):
                    self.across(a, s.farthest(i), bx).start()

    def own(self, a, bz, bx, r):
        here = pl.multiple_of(self.first(a, bz, bx, self.spot.c) + r, STRIP)
        return self.grads[a][pl.ds(here, STRIP), :].astype(jnp.float32)

    def c_step(self, a, i):
        s = self.spot
        bz = s.farthest(i)
        k = bz * 2 + 1 - s.x
        self.across(a, bz, 1 - s.x).wait_recv()
        cin = self.cins[a]

        def add(r):
            part = pl.ds(r, STRIP)
            total = self.own(a, bz, 1 - s.x, r) + cin[k, part, :].astype(jnp.float32)
            cin[k, part, :] = total.astype(jnp.bfloat16)

        strips(cin.shape[1], STRIP, add)
        self.over(a, bz).start()

    def x_step(self, a, i):
        s = self.spot
        bz = s.farthest(i)
        k = bz * 2 + s.x
        self.across(a, bz, s.x).wait_recv()
        self.over(a, bz).wait_recv()
        cin, xin, out = self.cins[a], self.xins[a], self.sums[a]

        def add(r):
            part = pl.ds(r, STRIP)
            total = (
                self.own(a, bz, s.x, r)
                + cin[k, part, :].astype(jnp.float32)
                + xin[bz, part, :].astype(jnp.float32)
            )
            if i < s.depth - 1:
                cin[k, part, :] = total.astype(jnp.bfloat16)
            else:
                out[part, :] = total

        strips(cin.shape[1], STRIP, add)
        if i < s.depth - 1:
            self.along(a, bz).start()

    def last_step(self, a):
        s = self.spot
        zin, out = self.zins[a], self.sums[a]
        slots = [lax.rem(s.z + step, s.depth) for step in range(1, s.depth)]
        for slot in slots:
            self.along(a, slot, True).wait_recv()

        def add(r):
            part = pl.ds(r, STRIP)
            total = out[part, :]
            for slot in slots:
                total = total + zin[slot, part, :].astype(jnp.float32)
            out[part, :] = total

        strips(out.shape[0], STRIP, add)

    def finish(self):
        s = self.spot
        for a in range(self.count):
            for i in range(s.depth):
                bz = s.farthest(i)
                for bx in range(2):
                    self.across(a, bz, bx).wait_send()
                self.over(a, bz).wait_send()
                if i < s.depth - 1:
                    self.along(a, bz).wait_send()


class Totals:
    def __init__(self, spot, stage, inbox, send, arrive, shared):
        self.spot, self.stage, self.inbox, self.send, self.arrive, self.shared = (
            spot, stage, inbox, send, arrive, shared,
        )

    @staticmethod
    def scratch(shape, depth):
        dma = pltpu.SemaphoreType.DMA
        return [
            pltpu.VMEM((4, *shape), jnp.float32),
            pltpu.VMEM((3 + depth, *shape), jnp.float32),
            dma((3 + depth,)),
            dma((3 + depth,)),
        ]

    def hop(self, number):
        to = (self.spot.twin, self.spot.cross)[number]
        return push(
            self.stage.at[number], self.inbox.at[number], self.send.at[number], self.arrive.at[number], to
        )

    def along(self, z, arriving=False):
        s = self.spot
        slot = 2 + (z if arriving else s.z)
        return push(
            self.stage.at[2], self.inbox.at[slot], self.send.at[2 + z], self.arrive.at[slot], s.at(z, s.x, s.c)
        )

    def pair(self):
        last = 2 + self.spot.depth
        part = pl.ds(0, self.shared)
        return push(
            self.stage.at[3, part], self.inbox.at[last, part], self.send.at[last], self.arrive.at[last], self.spot.pair
        )

    def others(self):
        s = self.spot
        return [lax.rem(s.z + step, s.depth) for step in range(1, s.depth)]

    def step(self, number):
        s = self.spot
        if number == 0:
            self.hop(0).start()
        elif number < 3:
            self.hop(number - 1).wait_recv()
            self.stage[number] = self.stage[number - 1] + self.inbox[number - 1]
            if number == 1:
                self.hop(1).start()
            else:
                for z in self.others():
                    self.along(z).start()
                self.inbox[2 + s.z] = self.stage[2]
        elif number == 3:
            for z in self.others():
                self.along(z, True).wait_recv()
            total = self.inbox[2]
            for z in range(1, s.depth):
                total = total + self.inbox[2 + z]
            self.stage[3] = total
            self.pair().start()
        else:
            self.pair().wait_recv()

    def result(self):
        part = slice(0, self.shared)
        return self.stage[3, part, :] + self.inbox[2 + self.spot.depth, part, :]

    def finish(self):
        self.hop(0).wait_send()
        self.hop(1).wait_send()
        for z in self.others():
            self.along(z).wait_send()
        self.pair().wait_send()


class Swap:
    def __init__(self, spot, source, target, send, arrive):
        self.spot, self.source, self.target, self.send, self.arrive = (
            spot,
            source,
            target,
            send,
            arrive,
        )

    def chunk(self, i, source_first=0, target_first=0):
        return push(
            rows_of(self.source, source_first + i * CHUNK, CHUNK),
            rows_of(self.target, target_first + i * CHUNK, CHUNK),
            self.send.at[i],
            self.arrive.at[i],
            self.spot.pair,
        )


def loop(first, last, body):
    def one(i, carry):
        body(i)
        return carry

    lax.fori_loop(first, last, one, 0)


def cast_into(source, target):
    def one(r):
        part = pl.ds(r, STRIP)
        target[part, :] = source[part, :].astype(target.dtype)

    strips(source.shape[0], STRIP, one)


def spread_kernel(depth, x, gain, shift, wide0, wide1, normed, full0, full1, own, low0, low1, ys, yr, yl, *sems):
    spot = Spot(depth)
    half = x.shape[0]
    base = spot.t * half
    cast_into(wide0, low0)
    cast_into(wide1, low1)
    spot.greet()
    gather = Gather(spot, (low0, low1), (full0, full1), *sems)
    gather.start()
    swap = Swap(spot, own, normed, ys, yr)

    def keep(i):
        return pltpu.make_async_copy(
            rows_of(own, i * CHUNK, CHUNK), rows_of(normed, base + i * CHUNK, CHUNK), yl.at[i]
        )

    def work(i):
        def one(r):
            part = pl.ds(i * CHUNK + r, BAND)
            own[part, :] = standardise_features(x[part, :], gain[...], shift[...])[0]

        strips(CHUNK, BAND, one)
        swap.chunk(i, 0, base).start()
        keep(i).start()

    loop(0, half // CHUNK, work)
    for step in range(1, depth):
        for a in range(2):
            gather.z_step(a, step)
        for a in range(2):
            gather.x_step(a, step - 1)
    for a in range(2):
        gather.x_step(a, depth - 1)

    def done(i):
        keep(i).wait()
        swap.chunk(i, 0, base).wait_send()
        swap.chunk(i, 0, half - base).wait_recv()

    loop(0, half // CHUNK, done)
    gather.finish()


def fold_rows(values):
    return jnp.sum(values.reshape(-1, 8, values.shape[-1]), axis=0)


def core_kernel(depth, part, x, bias, gain, shift, slope, other, shard, down, up_bias, resid, dresid, low, gup, contracted, sum0, sums, ups, up, shard_low, gdown, twos, outs, act, dpre, twos_t, outs_t, normed, own, inbox, inbox2, totals, ps, pr, ys, yr, ns, nr, ls, lr, lk, *rest):
    spot = Spot(depth)
    half, model = x.shape
    hidden = down.shape[1]
    width = min(512, hidden)
    side = min(256, half)
    blocks = hidden // width
    base = pl.multiple_of(spot.t * half, half)
    away = pl.multiple_of(half - base, half)
    chunks = half // CHUNK
    cast_into(shard, shard_low)
    spot.greet()
    gather = Gather(spot, (shard_low,), (up,), *rest[9:])
    gather.start()
    first = Swap(spot, part, inbox, ps, pr)
    second = Swap(spot, twos, twos, ys, yr)
    third = Swap(spot, normed, inbox2, ns, nr)
    fourth = Swap(spot, own, low, ls, lr)
    loop(0, chunks, lambda i: first.chunk(i, away, 0).start())

    def place(i):
        here = pl.ds(pl.multiple_of(base + i * side, side), side)
        there = pl.ds(pl.multiple_of(away + i * side, side), side)
        piece = pl.ds(pl.multiple_of(i * side, side), side)
        outs[here, :] = slope[piece, :].astype(jnp.bfloat16)
        outs[there, :] = other[piece, :]
        outs_t[:, here] = outs[here, :].T
        outs_t[:, there] = outs[there, :].T

    loop(0, half // side, place)

    def enter(i):
        first.chunk(i, away, 0).wait_recv()

        def one(r):
            here = pl.ds(i * CHUNK + r, BAND)
            there = pl.ds(pl.multiple_of(base + i * CHUNK + r, BAND), BAND)
            total = (
                x[here, :]
                + (inbox[here, :].astype(jnp.float32) + part[there, :].astype(jnp.float32))
                + bias[...]
            )
            resid[here, :] = total
            twos[there, :] = standardise_features(total, gain[...], shift[...])[0]

        strips(CHUNK, BAND, one)
        second.chunk(i, base, base).start()

    todo = []
    for step in range(depth):
        if step + 1 < depth:
            todo.append((gather.z_step, step + 1))
        todo.append((gather.x_step, step))
    for i in range(chunks):
        enter(i)
        if i > 0 and todo:
            act_on, step = todo.pop(0)
            act_on(0, step)
    for act_on, step in todo:
        act_on(0, step)
    gather.finish()

    def forward(start, again):
        here = pl.ds(start, half)
        twos_t[:, here] = twos[here, :].T

        def block(n):
            cols = pl.ds(pl.multiple_of(n * width, width), width)
            pre = product(twos[here, :], up[:, cols]) + up_bias[:, cols]
            square = pre * pre
            inner = 0.7978845608 * pre * (1.0 + 0.044715 * square)
            gate = 0.5 + 0.5 * jnp.tanh(inner)
            value = pre * gate
            act[here, cols] = value.astype(jnp.bfloat16)
            tilt = gate + value * (1.0 - gate) * (
                2.0 * 0.7978845608 + (6.0 * 0.7978845608 * 0.044715) * square
            )
            grad = product(outs[here, :], down[:, cols]) * tilt
            dpre[here, cols] = grad.astype(jnp.bfloat16)
            total = jnp.sum(fold_rows(grad), axis=0, keepdims=True)
            ups[:, cols] = ups[:, cols] + total if again else total

        loop(0, blocks, block)

    def contract(start, target):
        def one(i):
            here = pl.ds(pl.multiple_of(start + i * side, side), side)
            there = pl.ds(pl.multiple_of(target + i * side, side), side)
            contracted[there, :] = times_transposed(act[here, :], down[...]).astype(
                jnp.bfloat16
            )

        loop(0, half // side, one)

    def reduce_norm(i, start):
        here = pl.ds(pl.multiple_of(start + i * side, side), side)
        normed[here, :] = times_transposed(dpre[here, :], up[...]).astype(jnp.bfloat16)

    forward(base, False)
    contract(base, 0)
    loop(0, chunks, lambda i: second.chunk(i, away, away).wait_recv())
    forward(away, True)

    def send_norm(i):
        reduce_norm(i, away)
        for j in range(side // CHUNK):
            third.chunk(i * (side // CHUNK) + j, away, 0).start()

    loop(0, half // side, send_norm)
    loop(0, half // side, lambda i: reduce_norm(i, base))

    def weights(target, left, right):
        def one(n):
            cols = pl.ds(pl.multiple_of(n * width, width), width)
            target[:, cols] = product(left[...], right[:, cols]).astype(jnp.bfloat16)

        loop(0, blocks, one)

    weights(gdown, outs_t, act)
    scatter = Scatter(spot, (gdown,), (sum0,), rest[0:1], rest[1:2], rest[2:3], *rest[3:9])
    scatter.start()
    totals[...] = jnp.zeros_like(totals)
    weights(gup, twos_t, dpre)
    for i in range(depth):
        scatter.c_step(0, i)

    def keep(i):
        return pltpu.make_async_copy(
            rows_of(own, i * CHUNK, CHUNK), rows_of(low, base + i * CHUNK, CHUNK), lk.at[i]
        )

    def leave(i):
        third.chunk(i, away, 0).wait_recv()

        def one(r):
            here = pl.ds(i * CHUNK + r, BAND)
            there = pl.ds(pl.multiple_of(base + i * CHUNK + r, BAND), BAND)
            grad = inbox2[here, :].astype(jnp.float32) + normed[there, :].astype(jnp.float32)
            values = resid[here, :]
            centred = values - jnp.mean(values, axis=-1, keepdims=True)
            spread = lax.rsqrt(jnp.mean(centred * centred, axis=-1, keepdims=True) + 1e-05)
            unit = centred * spread
            out = slope[here, :]
            total = out + standardise_features_reverse(grad, unit, spread, gain[...])
            dresid[here, :] = total
            own[here, :] = total.astype(jnp.bfloat16)
            for spot_in, term in enumerate((total, out, grad * unit, grad)):
                totals[spot_in] += fold_rows(term)

        strips(CHUNK, BAND, one)
        fourth.chunk(i, 0, base).start()
        keep(i).start()

    loop(0, chunks, leave)
    contract(away, half)
    for i in range(depth):
        scatter.x_step(0, i)
    sums[...] = jnp.zeros_like(sums)
    for number in range(4):
        sums[number : number + 1, :] = jnp.sum(totals[number], axis=0, keepdims=True)
    scatter.last_step(0)

    def done(i):
        keep(i).wait()
        first.chunk(i, away, 0).wait_send()
        second.chunk(i, base, base).wait_send()
        third.chunk(i, away, 0).wait_send()
        fourth.chunk(i, 0, base).wait_send()
        fourth.chunk(i, 0, away).wait_recv()

    loop(0, chunks, done)
    scatter.finish()


def leave_kernel(depth, part, dresid, x, gain, early, split, grad0, grad1, slope, sum0, sum1, vector, inbox, totals, ps, pr, *rest):
    spot = Spot(depth)
    half = x.shape[0]
    base = spot.t * half
    spot.greet()
    first = Swap(spot, part, inbox, ps, pr)
    chunks = half // CHUNK
    loop(0, chunks, lambda i: first.chunk(i, half - base, 0).start())
    scatter = Scatter(spot, (grad0, grad1), (sum0, sum1), rest[0:2], rest[2:4], rest[4:6], *rest[6:12])
    scatter.start()
    every = Totals(spot, *rest[12:16], 8)
    totals[...] = jnp.zeros_like(totals)
    every.stage[0, 0:8, :] = early[...]
    every.stage[0, 8:16, :] = split[...]

    def work(i):
        first.chunk(i, half - base, 0).wait_recv()

        def one(r):
            here = pl.ds(i * CHUNK + r, BAND)
            there = pl.ds(pl.multiple_of(base + i * CHUNK + r, BAND), BAND)
            grad = inbox[here, :].astype(jnp.float32) + part[there, :].astype(jnp.float32)
            values = x[here, :]
            centred = values - jnp.mean(values, axis=-1, keepdims=True)
            spread = lax.rsqrt(jnp.mean(centred * centred, axis=-1, keepdims=True) + 1e-05)
            unit = centred * spread
            slope[here, :] = dresid[here, :] + standardise_features_reverse(
                grad, unit, spread, gain[...]
            )
            for place, term in enumerate((grad * unit, grad)):
                totals[place] += fold_rows(term)

        strips(CHUNK, BAND, one)

    for i in range(depth):
        for a in range(2):
            scatter.c_step(a, i)
    todo = [(scatter.x_step, a, i) for i in range(depth) for a in range(2)]
    for i in range(chunks):
        work(i)
        if todo:
            act, a, step = todo.pop(0)
            act(a, step)
    for place in range(2):
        every.stage[0, 4 + place : 5 + place, :] = jnp.sum(totals[place], axis=0, keepdims=True)
    every.step(0)
    for act, a, step in todo:
        act(a, step)
    for number in range(1, 4):
        every.step(number)
    for a in range(2):
        scatter.last_step(a)
    every.step(4)
    vector[0:8, :] = every.result()
    vector[8:16, :] = every.stage[3, 8:16, :]
    loop(0, chunks, lambda i: first.chunk(i, half - base, 0).wait_send())
    every.finish()
    scatter.finish()


def vmem(count=1):
    return [pl.BlockSpec(memory_space=pltpu.VMEM)] * count


def anywhere(count=1):
    return [pl.BlockSpec(memory_space=pl.ANY)] * count


def call(body, number, name, depth, outs, in_specs, out_specs, scratch, args, mib=48):
    size = sum(a.size * a.dtype.itemsize for a in args) + sum(
        o.size * jnp.dtype(o.dtype).itemsize for o in outs
    )
    return pl.pallas_call(
        functools.partial(body, depth),
        out_shape=outs,
        in_specs=in_specs,
        out_specs=out_specs,
        scratch_shapes=scratch,
        cost_estimate=pl.CostEstimate(flops=0, bytes_accessed=size, transcendentals=0),
        compiler_params=pltpu.CompilerParams(
            collective_id=number, has_side_effects=True, vmem_limit_bytes=mib * MIB
        ),
        name=name,
    )(*args)


def shaped(shape, dtype=jnp.bfloat16):
    return jax.ShapeDtypeStruct(shape, dtype)


def spread_call(depth, x, gain, shift, shards):
    half, width = x.shape
    dma = pltpu.SemaphoreType.DMA
    chunks = half // CHUNK
    outs = [shaped((2 * half, width))]
    outs += [shaped((4 * depth * s.shape[0], s.shape[1])) for s in shards]
    scratch = [pltpu.VMEM((half, width), jnp.bfloat16)]
    scratch += [pltpu.VMEM(s.shape, jnp.bfloat16) for s in shards]
    scratch += [dma((chunks,))] * 3 + Gather.semaphores(2, depth)
    return call(
        spread_kernel, 0, "spread", depth, outs, vmem(5), anywhere(3), scratch,
        (x, gain[None], shift[None], *shards),
    )


def core_call(depth, part, x, bias, gain, shift, slope, other, shard, down, up_bias):
    half, model = x.shape
    tokens, hidden = 2 * half, down.shape[1]
    low, full, dma = jnp.bfloat16, jnp.float32, pltpu.SemaphoreType.DMA
    chunks = half // CHUNK
    shapes = [(model // (4 * depth), hidden)]
    outs = [
        shaped((half, model), full),
        shaped((half, model), full),
        shaped((tokens, model)),
        shaped((model, hidden)),
        shaped((tokens, model)),
        shaped(shapes[0], full),
        shaped((8, model), full),
        shaped((1, hidden), full),
    ]
    scratch = [
        pltpu.VMEM((model, hidden), low),
        pltpu.VMEM(shard.shape, low),
        pltpu.VMEM((model, hidden), low),
        pltpu.VMEM((tokens, model), low),
        pltpu.VMEM((tokens, model), low),
        pltpu.VMEM((tokens, hidden), low),
        pltpu.VMEM((tokens, hidden), low),
        pltpu.VMEM((model, tokens), low),
        pltpu.VMEM((model, tokens), low),
        pltpu.VMEM((tokens, model), low),
        pltpu.VMEM((half, model), low),
        pltpu.VMEM((half, model), low),
        pltpu.VMEM((half, model), low),
        pltpu.VMEM((4, 8, model), full),
    ]
    scratch += [dma((chunks,))] * 9 + Scatter.scratch(shapes, depth)
    scratch += Gather.semaphores(1, depth)
    return call(
        core_kernel, 1, "core", depth, outs, vmem(10),
        vmem(2) + anywhere() + vmem(5), scratch,
        (part, x, bias[None], gain[None], shift[None], slope, other, shard, down, up_bias[None]),
        60,
    )


def leave_call(depth, part, dresid, x, gain, early, split, grads):
    half, width = x.shape
    dma = pltpu.SemaphoreType.DMA
    chunks = half // CHUNK
    shapes = [(g.shape[0] // (4 * depth), g.shape[1]) for g in grads]
    outs = [shaped((half, width), jnp.float32)]
    outs += [shaped(s, jnp.float32) for s in shapes] + [shaped((16, width), jnp.float32)]
    scratch = [pltpu.VMEM((half, width), jnp.bfloat16)]
    scratch += [pltpu.VMEM((2, 8, width), jnp.float32)]
    scratch += [dma((chunks,))] * 2 + Scatter.scratch(shapes, depth)
    scratch += Totals.scratch((16, width), depth)
    return call(
        leave_kernel, 2, "leave", depth, outs, vmem(8), vmem(4), scratch,
        (part, dresid, x, gain[None], early, split, *grads),
    )


def reverse_kernel(
    depth, block, slopes, x, grad, rows_seg, cols_seg, gup, contracted, out, sums, sum0, arrived,
    offsets, dkeys, dvalues, dquery, ds, dr, *rest
):
    step = pl.program_id(0)
    last = pl.num_programs(0) - 1
    spot = Spot(depth)
    chunks, half = arrived.shape[0] // CHUNK, arrived.shape[0]
    swap = Swap(spot, contracted, arrived, ds, dr)
    scatter = Scatter(spot, (gup,), (sum0,), rest[0:1], rest[1:2], rest[2:3], *rest[3:])

    @pl.when(step == 0)
    def _():
        spot.greet()
        scatter.start()
        loop(0, chunks, lambda i: swap.chunk(i, half, 0).start())

    backward_kernel(
        block, slopes, x, grad, rows_seg, cols_seg, out, sums, offsets, dkeys, dvalues, dquery
    )

    @pl.when(step == 0)
    def _():
        for i in range(depth):
            scatter.c_step(0, i)

    for i in range(depth - 1):
        @pl.when(step == jnp.minimum(i + 1, last))
        def _():
            scatter.x_step(0, i)

    @pl.when(step == last)
    def _():
        scatter.x_step(0, depth - 1)
        scatter.last_step(0)
        loop(0, chunks, lambda i: swap.chunk(i, half, 0).wait())
        scatter.finish()


def reverse_call(depth, qkv, segments, slopes, dcontext, gup, contracted):
    length, width = qkv.shape
    model, hidden = gup.shape
    pairs = width // (6 * HEAD_DIM)
    block = min(256, length)
    span = min(length, block + MAX_SPAN)
    half = length // 2
    dma = pltpu.SemaphoreType.DMA
    shapes = [(model // (4 * depth), hidden)]
    return pl.pallas_call(
        functools.partial(reverse_kernel, depth, block),
        grid=(pairs,),
        out_shape=(
            shaped((length, width)),
            shaped((1, width), jnp.float32),
            shaped(shapes[0], jnp.float32),
            shaped((half, model)),
        ),
        in_specs=[
            pl.BlockSpec(memory_space=pltpu.SMEM),
            pl.BlockSpec((length, 6 * HEAD_DIM), lambda p: (0, p)),
            pl.BlockSpec((length, 2 * HEAD_DIM), lambda p: (0, p)),
            pl.BlockSpec((length, 1), lambda p: (0, 0)),
            pl.BlockSpec((1, length), lambda p: (0, 0)),
            pl.BlockSpec(memory_space=pltpu.VMEM),
            pl.BlockSpec(memory_space=pl.ANY),
        ],
        out_specs=(
            pl.BlockSpec((length, 6 * HEAD_DIM), lambda p: (0, p)),
            pl.BlockSpec((1, 6 * HEAD_DIM), lambda p: (0, p)),
            pl.BlockSpec(memory_space=pltpu.VMEM),
            pl.BlockSpec(memory_space=pl.ANY),
        ),
        scratch_shapes=[
            pltpu.VMEM((span, length), jnp.float32),
            pltpu.VMEM((length, HEAD_DIM), jnp.float32),
            pltpu.VMEM((length, HEAD_DIM), jnp.float32),
            pltpu.VMEM((length, HEAD_DIM), jnp.float32),
        ]
        + [dma((half // CHUNK,))] * 2
        + Scatter.scratch(shapes, depth),
        cost_estimate=pl.CostEstimate(
            flops=10 * length * span * width // 3,
            bytes_accessed=14 * length * width // 3,
            transcendentals=length * span * pairs * 2,
        ),
        compiler_params=pltpu.CompilerParams(
            collective_id=3, has_side_effects=True, vmem_limit_bytes=48 * MIB
        ),
        name="attention_backward",
    )(slopes, qkv, dcontext, segments[:, None], segments[None, :], gup, contracted)


def direct_kernel(
    depth, block, slopes, x, rows_seg, cols_seg, shard, out, full, offsets, shard_low, *sems
):
    step = pl.program_id(0)
    last = pl.num_programs(0) - 1
    spot = Spot(depth)
    gather = Gather(spot, (shard_low,), (full,), *sems)

    @pl.when(step == 0)
    def _():
        cast_into(shard, shard_low)
        spot.greet()
        gather.start()

    forward_kernel(block, slopes, x, rows_seg, cols_seg, out, offsets)

    for i in range(depth):

        @pl.when(step == jnp.minimum(i, last))
        def _():
            if i + 1 < depth:
                gather.z_step(0, i + 1)
            if i > 0:
                gather.x_step(0, i - 1)

    @pl.when(step == last)
    def _():
        gather.x_step(0, depth - 1)
        gather.finish()


def direct_call(depth, qkv, segments, slopes, shard):
    length, width = qkv.shape
    pairs = width // (6 * HEAD_DIM)
    block = min(256, length)
    span = min(length, block + MAX_SPAN)
    return pl.pallas_call(
        functools.partial(direct_kernel, depth, block),
        grid=(pairs,),
        out_shape=(
            shaped((length, width // 3)),
            shaped((4 * depth * shard.shape[0], shard.shape[1])),
        ),
        in_specs=[
            pl.BlockSpec(memory_space=pltpu.SMEM),
            pl.BlockSpec((length, 6 * HEAD_DIM), lambda p: (0, p)),
            pl.BlockSpec((length, 1), lambda p: (0, 0)),
            pl.BlockSpec((1, length), lambda p: (0, 0)),
            pl.BlockSpec(memory_space=pltpu.VMEM),
        ],
        out_specs=(
            pl.BlockSpec((length, 2 * HEAD_DIM), lambda p: (0, p)),
            pl.BlockSpec(memory_space=pl.ANY),
        ),
        scratch_shapes=[
            pltpu.VMEM((length, span), jnp.float32),
            pltpu.VMEM(shard.shape, jnp.bfloat16),
        ]
        + Gather.semaphores(1, depth),
        cost_estimate=pl.CostEstimate(
            flops=4 * length * span * width // 3,
            bytes_accessed=8 * length * width // 3,
            transcendentals=length * span * pairs * 2,
        ),
        compiler_params=pltpu.CompilerParams(
            collective_id=4, has_side_effects=True, vmem_limit_bytes=40 * MIB
        ),
        name="attention_forward",
    )(slopes, qkv, segments[:, None], segments[None, :], shard)


def linked(
    entering_activations,
    segment_ids,
    leaving_activation_slope,
    qkv_weight,
    qv_bias,
    dense_weight,
    dense_bias,
    up_weight,
    up_bias,
    down_weight,
    down_bias,
    mixer_scale_factor,
    mixer_offset_term,
    perceptron_scale_factor,
    perceptron_offset_term,
):
    depth = lax.axis_size("dp") // 4
    rank = lax.axis_index("tensor")
    local_heads = qkv_weight.shape[1] // (3 * HEAD_DIM)
    slopes = head_slopes(rank * local_heads, local_heads)
    segments = segment_ids[0]
    ones, qkv_low, dense_low = spread_call(
        depth,
        entering_activations,
        mixer_scale_factor,
        mixer_offset_term,
        (qkv_weight, dense_weight.T),
    )
    out_own, ones = lax.optimization_barrier(
        (leaving_activation_slope.astype(jnp.bfloat16), ones)
    )
    out_other = swap(out_own)
    qkv = (product(ones, qkv_low) + full_bias(qv_bias, local_heads)).astype(jnp.bfloat16)
    context, down_low = direct_call(depth, qkv, segments, slopes, down_weight.T)
    dense_part = times_transposed(context, dense_low).astype(jnp.bfloat16)
    resid, dresid, resid_low, grad_up, down_part, grad_down, early, up_bias_part = core_call(
        depth,
        dense_part,
        entering_activations,
        dense_bias,
        perceptron_scale_factor,
        perceptron_offset_term,
        leaving_activation_slope,
        out_other,
        up_weight,
        down_low,
        up_bias,
    )
    dcontext = times_transposed(resid_low, jnp.swapaxes(dense_low, 0, 1)).astype(jnp.bfloat16)
    grad_dense = inner_rows(resid_low, context).astype(jnp.bfloat16)
    dqkv_low, dqkv_sums, grad_up, arrived = reverse_call(
        depth, qkv, segments, slopes, dcontext, grad_up, down_part
    )
    half = resid.shape[0]
    block_out = (
        resid + (arrived.astype(jnp.float32) + down_part[:half].astype(jnp.float32)) + down_bias
    )
    grad_qkv = inner_rows(ones, dqkv_low).astype(jnp.bfloat16)
    triple = dqkv_sums.reshape(local_heads, 3, HEAD_DIM)
    qv_part = jnp.stack([triple[:, 0], triple[:, 2]], axis=1).reshape(-1)
    mixer_part = times_transposed(dqkv_low, qkv_low).astype(jnp.bfloat16)
    split = jnp.concatenate([up_bias_part[0], qv_part]).reshape(-1, D)
    split = jnp.pad(split, ((0, 8 - split.shape[0]), (0, 0)))
    entering_slope, grad_qkv, grad_dense, vector = leave_call(
        depth,
        mixer_part,
        dresid,
        entering_activations,
        mixer_scale_factor,
        early,
        split,
        (grad_qkv, grad_dense),
    )
    ups = up_bias.size
    rest = vector[8:].reshape(-1)
    return (
        block_out,
        entering_slope,
        (
            grad_qkv,
            rest[ups : ups + qv_bias.size],
            grad_dense.T,
            vector[0],
            grad_up,
            rest[:ups],
            grad_down.T,
            vector[1],
            vector[4],
            vector[5],
            vector[2],
            vector[3],
        ),
    )


def general(
    entering_activations,
    segment_ids,
    leaving_activation_slope,
    qkv_weight,
    qv_bias,
    dense_weight,
    dense_bias,
    up_weight,
    up_bias,
    down_weight,
    down_bias,
    mixer_scale_factor,
    mixer_offset_term,
    perceptron_scale_factor,
    perceptron_offset_term,
):
    qkv_low, dense_low, up_low, down_low = (
        lax.all_gather(qkv_weight.astype(jnp.bfloat16), "dp", axis=0, tiled=True),
        lax.all_gather(dense_weight.astype(jnp.bfloat16), "dp", axis=1, tiled=True),
        lax.all_gather(up_weight.astype(jnp.bfloat16), "dp", axis=0, tiled=True),
        lax.all_gather(down_weight.astype(jnp.bfloat16), "dp", axis=1, tiled=True),
    )
    local_heads = qkv_low.shape[1] // (3 * HEAD_DIM)
    tensor_rank = lax.axis_index("tensor")
    count = lax.axis_size("tensor")
    slopes = head_slopes(tensor_rank * local_heads, local_heads)
    segments = segment_ids[0]
    mixer_standardised, mixer_unit_spread1, mixer_reciprocal_spread1 = standardise_features(
        entering_activations, mixer_scale_factor, mixer_offset_term
    )
    ones = spread(mixer_standardised, count)
    outs = spread(leaving_activation_slope.astype(jnp.bfloat16), count)
    qkv_bias = full_bias(qv_bias, local_heads)
    qkv = to_order([(product(one, qkv_low) + qkv_bias).astype(jnp.bfloat16) for one in ones], tensor_rank)
    context = attention_forward(qkv, segments, slopes)
    contexts = from_order(context, tensor_rank, count)
    skip_path_sum = (
        entering_activations
        + fold([product(part, dense_low).astype(jnp.bfloat16) for part in contexts], count)
        + dense_bias
    )
    perceptron_standardised, perceptron_unit_spread2, perceptron_reciprocal_spread2 = (
        standardise_features(skip_path_sum, perceptron_scale_factor, perceptron_offset_term)
    )
    twos = spread(perceptron_standardised, count)
    acts, dpres, dpre_lows, pre_parts = [], [], [], []
    for two, out in zip(twos, outs):
        act_val, act_slope = gelu_parts(product(two, up_low) + up_bias)
        acts.append(act_val.astype(jnp.bfloat16))
        dpres.append(times_transposed(out, down_low) * act_slope)
        dpre_lows.append(dpres[-1].astype(jnp.bfloat16))
        pre_parts.append(times_transposed(dpre_lows[-1], up_low).astype(jnp.bfloat16))
    pre_perceptron_sensitivity = fold(pre_parts, count)
    block_out = (
        skip_path_sum
        + fold([product(act, down_low).astype(jnp.bfloat16) for act in acts], count)
        + down_bias
    )
    contraction_sensitivity = add_up(acts, outs).astype(jnp.bfloat16)
    expansion_sensitivity = add_up(twos, dpre_lows).astype(jnp.bfloat16)
    up_bias_part = sum(jnp.sum(dpre, axis=0) for dpre in dpres)
    skip_path_sensitivity = leaving_activation_slope + standardise_features_reverse(
        pre_perceptron_sensitivity,
        perceptron_unit_spread2,
        perceptron_reciprocal_spread2,
        perceptron_scale_factor,
    )
    resids = spread(skip_path_sensitivity.astype(jnp.bfloat16), count)
    mixer_merge_sensitivity = add_up(contexts, resids).astype(jnp.bfloat16)
    dcontext = to_order(
        [times_transposed(resid, dense_low).astype(jnp.bfloat16) for resid in resids], tensor_rank
    )
    dqkv_low, dqkv_sums = attention_backward(qkv, segments, slopes, dcontext)
    dqkv_lows = from_order(dqkv_low, tensor_rank, count)
    packed_triple_slope = add_up(ones, dqkv_lows).astype(jnp.bfloat16)
    triple = dqkv_sums.reshape(local_heads, 3, HEAD_DIM)
    qv_part = jnp.stack([triple[:, 0], triple[:, 2]], axis=1).reshape(-1)
    pre_mixer_sensitivity = fold(
        [times_transposed(part, qkv_low).astype(jnp.bfloat16) for part in dqkv_lows], count
    )
    entering_activation_slope = skip_path_sensitivity + standardise_features_reverse(
        pre_mixer_sensitivity, mixer_unit_spread1, mixer_reciprocal_spread1, mixer_scale_factor
    )
    early, up_bias_grad = total_over_all(
        jnp.concatenate(
            [
                jnp.sum(skip_path_sensitivity, axis=0),
                jnp.sum(leaving_activation_slope, axis=0),
                jnp.sum(pre_perceptron_sensitivity * perceptron_unit_spread2, axis=0),
                jnp.sum(pre_perceptron_sensitivity, axis=0),
                up_bias_part,
            ]
        ),
        4 * D,
        tensor_rank,
    )
    dense_bias_grad, down_bias_grad, gain_two_grad, shift_two_grad = jnp.split(early, 4)
    late, qv_bias_grad = total_over_all(
        jnp.concatenate(
            [
                jnp.sum(pre_mixer_sensitivity * mixer_unit_spread1, axis=0),
                jnp.sum(pre_mixer_sensitivity, axis=0),
                qv_part,
            ]
        ),
        2 * D,
        tensor_rank,
    )
    gain_one_grad, shift_one_grad = jnp.split(late, 2)
    packed_triple_slope, mixer_merge_sensitivity, expansion_sensitivity, contraction_sensitivity = (
        part.astype(jnp.float32)
        for part in (
            lax.psum_scatter(packed_triple_slope, "dp", scatter_dimension=0, tiled=True),
            lax.psum_scatter(mixer_merge_sensitivity, "dp", scatter_dimension=1, tiled=True),
            lax.psum_scatter(expansion_sensitivity, "dp", scatter_dimension=0, tiled=True),
            lax.psum_scatter(contraction_sensitivity, "dp", scatter_dimension=1, tiled=True),
        )
    )
    return block_out, entering_activation_slope, (
        packed_triple_slope,
        qv_bias_grad,
        mixer_merge_sensitivity,
        dense_bias_grad,
        expansion_sensitivity,
        up_bias_grad,
        contraction_sensitivity,
        down_bias_grad,
        gain_one_grad,
        shift_one_grad,
        gain_two_grad,
        shift_two_grad,
    )


def local(
    entering_activations,
    segment_ids,
    leaving_activation_slope,
    qkv_weight,
    qv_bias,
    dense_weight,
    dense_bias,
    up_weight,
    up_bias,
    down_weight,
    down_bias,
    mixer_scale_factor,
    mixer_offset_term,
    perceptron_scale_factor,
    perceptron_offset_term,
    first_qkv_weight,
    first_qv_bias,
    first_dense_weight,
    first_dense_bias,
    first_up_weight,
    first_up_bias,
    first_down_weight,
    first_down_bias,
    first_norm1_gain,
    first_norm1_bias,
    first_norm2_gain,
    first_norm2_bias,
    second_qkv_weight,
    second_qv_bias,
    second_dense_weight,
    second_dense_bias,
    second_up_weight,
    second_up_bias,
    second_down_weight,
    second_down_bias,
    second_norm1_gain,
    second_norm1_bias,
    second_norm2_gain,
    second_norm2_bias,
):
    params = (
        qkv_weight,
        qv_bias,
        dense_weight,
        dense_bias,
        up_weight,
        up_bias,
        down_weight,
        down_bias,
        mixer_scale_factor,
        mixer_offset_term,
        perceptron_scale_factor,
        perceptron_offset_term,
    )
    firsts = (
        first_qkv_weight,
        first_qv_bias,
        first_dense_weight,
        first_dense_bias,
        first_up_weight,
        first_up_bias,
        first_down_weight,
        first_down_bias,
        first_norm1_gain,
        first_norm1_bias,
        first_norm2_gain,
        first_norm2_bias,
    )
    seconds = (
        second_qkv_weight,
        second_qv_bias,
        second_dense_weight,
        second_dense_bias,
        second_up_weight,
        second_up_bias,
        second_down_weight,
        second_down_bias,
        second_norm1_gain,
        second_norm1_bias,
        second_norm2_gain,
        second_norm2_bias,
    )
    whole_line = lax.axis_size("tensor") == 2 and lax.axis_size("dp") % 4 == 0
    route = linked if whole_line and segment_ids.shape[0] == 1 else general
    block_out, entering_activation_slope, parameter_slopes = route(
        entering_activations,
        segment_ids,
        leaving_activation_slope,
        qkv_weight,
        qv_bias,
        dense_weight,
        dense_bias,
        up_weight,
        up_bias,
        down_weight,
        down_bias,
        mixer_scale_factor,
        mixer_offset_term,
        perceptron_scale_factor,
        perceptron_offset_term,
    )
    results = []
    for index in range(12):
        matrix = index in (0, 2, 4, 6)
        results.append(
            adamw(
                params[index],
                parameter_slopes[index],
                firsts[index],
                seconds[index],
                0.01 if matrix else 0.1,
                0.1 if matrix else 0.0,
            )
        )
    news = [r[0] for r in results]
    moments_one = [r[1] for r in results]
    moments_two = [r[2] for r in results]
    return (
        block_out,
        entering_activation_slope,
        *parameter_slopes,
        *news,
        *moments_one,
        *moments_two,
    )


def solution(mesh):
    in_specs = (
        P(("dp", "tensor"), None),
        P("dp", None),
        P(("dp", "tensor"), None),
        P("dp", "tensor"),
        P("tensor"),
        P("tensor", "dp"),
        P(),
        P("dp", "tensor"),
        P("tensor"),
        P("tensor", "dp"),
        P(),
        P(),
        P(),
        P(),
        P(),
        P("dp", "tensor"),
        P("tensor"),
        P("tensor", "dp"),
        P(),
        P("dp", "tensor"),
        P("tensor"),
        P("tensor", "dp"),
        P(),
        P(),
        P(),
        P(),
        P(),
        P("dp", "tensor"),
        P("tensor"),
        P("tensor", "dp"),
        P(),
        P("dp", "tensor"),
        P("tensor"),
        P("tensor", "dp"),
        P(),
        P(),
        P(),
        P(),
        P(),
    )
    out_specs = (
        P(("dp", "tensor"), None),
        P(("dp", "tensor"), None),
        P("dp", "tensor"),
        P("tensor"),
        P("tensor", "dp"),
        P(),
        P("dp", "tensor"),
        P("tensor"),
        P("tensor", "dp"),
        P(),
        P(),
        P(),
        P(),
        P(),
        P("dp", "tensor"),
        P("tensor"),
        P("tensor", "dp"),
        P(),
        P("dp", "tensor"),
        P("tensor"),
        P("tensor", "dp"),
        P(),
        P(),
        P(),
        P(),
        P(),
        P("dp", "tensor"),
        P("tensor"),
        P("tensor", "dp"),
        P(),
        P("dp", "tensor"),
        P("tensor"),
        P("tensor", "dp"),
        P(),
        P(),
        P(),
        P(),
        P(),
        P("dp", "tensor"),
        P("tensor"),
        P("tensor", "dp"),
        P(),
        P("dp", "tensor"),
        P("tensor"),
        P("tensor", "dp"),
        P(),
        P(),
        P(),
        P(),
        P(),
    )
    return jax.shard_map(local, mesh=mesh, in_specs=in_specs, out_specs=out_specs, check_vma=False)
```

```python
import functools

import jax
import jax.numpy as jnp
from jax import lax
from jax.experimental import pallas as pl
from jax.experimental.pallas import tpu as pltpu
from jax.sharding import PartitionSpec as P

D = 1024
FOCUS_COUNT = 16
FF = 4096
ADAM_STEP = 4
HEAD_DIM = 64
MAX_SPAN = 512


beta_first = 0.9
beta_second = 0.95


def standardise_features(values, elementwise_multiplier, additive_offset):
    feature_midpoint = jnp.mean(values, axis=-1, keepdims=True)
    demeaned_entries = values - feature_midpoint
    reciprocal_spread = lax.rsqrt(
        jnp.mean(demeaned_entries * demeaned_entries, axis=-1, keepdims=True) + 1e-05
    )
    unit_spread_entries = demeaned_entries * reciprocal_spread
    return (
        (unit_spread_entries * elementwise_multiplier + additive_offset).astype(jnp.bfloat16),
        unit_spread_entries,
        reciprocal_spread,
    )


def standardise_features_reverse(
    loss_slope, unit_spread_entries, reciprocal_spread, elementwise_multiplier
):
    multiplied_entries = loss_slope * elementwise_multiplier
    return reciprocal_spread * (
        multiplied_entries
        - jnp.mean(multiplied_entries, axis=-1, keepdims=True)
        - unit_spread_entries
        * jnp.mean(multiplied_entries * unit_spread_entries, axis=-1, keepdims=True)
    )


def gelu_parts(pre):
    inner = 0.7978845608 * (pre + 0.044715 * pre * pre * pre)
    tanh_val = jnp.tanh(inner)
    value = 0.5 * pre * (1.0 + tanh_val)
    slope = 0.5 * (1.0 + tanh_val) + 0.5 * pre * (1.0 - tanh_val * tanh_val) * 0.7978845608 * (
        1.0 + 3.0 * 0.044715 * pre * pre
    )
    return (value, slope)


def inner_rows(left, right):
    return lax.dot_general(
        left, right, (((0,), (0,)), ((), ())), preferred_element_type=jnp.float32
    )


def times_transposed(left, right):
    return lax.dot_general(
        left, right, (((1,), (1,)), ((), ())), preferred_element_type=jnp.float32
    )


def head_slopes(first, count):
    index = (first + jnp.arange(count)).astype(jnp.float32)
    return jnp.exp2(-8.0 * (index + 1.0) / FOCUS_COUNT)


def full_bias(qv_bias, heads):
    pair = qv_bias.reshape(heads, 2, HEAD_DIM)
    return jnp.stack([pair[:, 0], jnp.zeros_like(pair[:, 0]), pair[:, 1]], axis=1).reshape(
        heads * 3 * HEAD_DIM
    )


def window(start, block, length):
    return (max(0, start - MAX_SPAN), min(length, start + block))


def fill_offsets(offsets, rows_seg, cols_seg, rows_first, length, block):
    for start in range(0, length, block):
        low, high = window(start, block, length)
        shape = (block, high - low) if rows_first else (high - low, block)
        axis = 0 if rows_first else 1
        row = start + lax.broadcasted_iota(jnp.int32, shape, axis)
        col = low + lax.broadcasted_iota(jnp.int32, shape, 1 - axis)
        if rows_first:
            same = rows_seg[start : start + block, :] == cols_seg[:, low:high]
        else:
            same = rows_seg[low:high, :] == cols_seg[:, start : start + block]
        allowed = (col <= row) & same
        value = jnp.where(allowed, (col - row).astype(jnp.float32), -1e30)
        if rows_first:
            offsets[start : start + block, 0 : high - low] = value
        else:
            offsets[0 : high - low, start : start + block] = value


def forward_kernel(block, slopes, x, rows_seg, cols_seg, out, offsets):
    length = x.shape[0]
    step = pl.program_id(0)

    @pl.when(step == 0)
    def _():
        fill_offsets(offsets, rows_seg, cols_seg, True, length, block)

    for i in range(2):
        base = 3 * HEAD_DIM * i
        slope = slopes[2 * step + i]
        query = x[:, base : base + HEAD_DIM] * HEAD_DIM ** (-0.5)
        keys = x[:, base + HEAD_DIM : base + 2 * HEAD_DIM]
        values = x[:, base + 2 * HEAD_DIM : base + 3 * HEAD_DIM]
        for start in range(0, length, block):
            low, high = window(start, block, length)
            scores = (
                times_transposed(query[start : start + block], keys[low:high])
                + slope * offsets[start : start + block, 0 : high - low]
            )
            peak = jnp.max(scores, axis=1, keepdims=True)
            raised = jnp.exp(scores - peak)
            total = jnp.sum(raised, axis=1, keepdims=True)
            probs = (raised * (1.0 / total)).astype(jnp.bfloat16)
            context = jnp.dot(probs, values[low:high], preferred_element_type=jnp.float32)
            out[start : start + block, HEAD_DIM * i : HEAD_DIM * (i + 1)] = context.astype(
                jnp.bfloat16
            )


def backward_kernel(
    block, slopes, x, grad, rows_seg, cols_seg, out, sums, offsets, dkeys, dvalues, dquery,
    compact=False,
):
    length = x.shape[0]
    step = pl.program_id(0)
    scale = HEAD_DIM ** (-0.5)

    @pl.when(step == 0)
    def _():
        fill_offsets(offsets, rows_seg, cols_seg, False, length, block)

    for i in range(2):
        base = 3 * HEAD_DIM * i
        slope = slopes[2 * step + i]
        query = x[:, base : base + HEAD_DIM] * scale
        keys = x[:, base + HEAD_DIM : base + 2 * HEAD_DIM]
        values = x[:, base + 2 * HEAD_DIM : base + 3 * HEAD_DIM]
        slopes_out = grad[:, HEAD_DIM * i : HEAD_DIM * (i + 1)]
        dkeys[...] = jnp.zeros_like(dkeys)
        dvalues[...] = jnp.zeros_like(dvalues)
        for start in range(0, length, block):
            low, high = window(start, block, length)
            query_block = query[start : start + block]
            grad_block = slopes_out[start : start + block]
            scores = (
                times_transposed(keys[low:high], query_block)
                + slope * offsets[0 : high - low, start : start + block]
            )
            peak = jnp.max(scores, axis=0, keepdims=True)
            raised = jnp.exp(scores - peak)
            total = jnp.sum(raised, axis=0, keepdims=True)
            probs = raised * (1.0 / total)
            dprob = times_transposed(values[low:high], grad_block)
            delta = jnp.sum(probs * dprob, axis=0, keepdims=True)
            dscore = (probs * (dprob - delta)).astype(jnp.bfloat16)
            dvalues[low:high, :] += jnp.dot(
                probs.astype(jnp.bfloat16), grad_block, preferred_element_type=jnp.float32
            )
            dkeys[low:high, :] += jnp.dot(dscore, query_block, preferred_element_type=jnp.float32)
            dquery[start : start + block, :] = inner_rows(dscore, keys[low:high]) * scale
        for place, part in enumerate((dquery, dkeys, dvalues)):
            first = base + HEAD_DIM * place
            out[:, first : first + HEAD_DIM] = part[...].astype(jnp.bfloat16)
            if compact and place == 1:
                continue
            if compact:
                first = HEAD_DIM * (2 * i + place // 2)
            sums[:, first : first + HEAD_DIM] = jnp.sum(part[...], axis=0, keepdims=True)


def attention_forward(qkv, segments, slopes):
    length, width = qkv.shape
    pairs = width // (6 * HEAD_DIM)
    block = min(256, length)
    span = min(length, block + MAX_SPAN)
    return pl.pallas_call(
        functools.partial(forward_kernel, block),
        grid=(pairs,),
        out_shape=jax.ShapeDtypeStruct((length, width // 3), jnp.bfloat16),
        in_specs=[
            pl.BlockSpec(memory_space=pltpu.SMEM),
            pl.BlockSpec((length, 6 * HEAD_DIM), lambda p: (0, p)),
            pl.BlockSpec((length, 1), lambda p: (0, 0)),
            pl.BlockSpec((1, length), lambda p: (0, 0)),
        ],
        out_specs=pl.BlockSpec((length, 2 * HEAD_DIM), lambda p: (0, p)),
        scratch_shapes=[pltpu.VMEM((length, span), jnp.float32)],
        cost_estimate=pl.CostEstimate(
            flops=4 * length * span * width // 3,
            bytes_accessed=8 * length * width // 3,
            transcendentals=length * span * pairs * 2,
        ),
        compiler_params=pltpu.CompilerParams(vmem_limit_bytes=40 * 1024 * 1024),
        name="attention_forward",
    )(slopes, qkv, segments[:, None], segments[None, :])


def attention_backward(qkv, segments, slopes, dcontext):
    length, width = qkv.shape
    pairs = width // (6 * HEAD_DIM)
    block = min(256, length)
    span = min(length, block + MAX_SPAN)
    return pl.pallas_call(
        functools.partial(backward_kernel, block),
        grid=(pairs,),
        out_shape=(
            jax.ShapeDtypeStruct((length, width), jnp.bfloat16),
            jax.ShapeDtypeStruct((1, width), jnp.float32),
        ),
        in_specs=[
            pl.BlockSpec(memory_space=pltpu.SMEM),
            pl.BlockSpec((length, 6 * HEAD_DIM), lambda p: (0, p)),
            pl.BlockSpec((length, 2 * HEAD_DIM), lambda p: (0, p)),
            pl.BlockSpec((length, 1), lambda p: (0, 0)),
            pl.BlockSpec((1, length), lambda p: (0, 0)),
        ],
        out_specs=(
            pl.BlockSpec((length, 6 * HEAD_DIM), lambda p: (0, p)),
            pl.BlockSpec((1, 6 * HEAD_DIM), lambda p: (0, p)),
        ),
        scratch_shapes=[
            pltpu.VMEM((span, length), jnp.float32),
            pltpu.VMEM((length, HEAD_DIM), jnp.float32),
            pltpu.VMEM((length, HEAD_DIM), jnp.float32),
            pltpu.VMEM((length, HEAD_DIM), jnp.float32),
        ],
        cost_estimate=pl.CostEstimate(
            flops=10 * length * span * width // 3,
            bytes_accessed=14 * length * width // 3,
            transcendentals=length * span * pairs * 2,
        ),
        compiler_params=pltpu.CompilerParams(vmem_limit_bytes=40 * 1024 * 1024),
        name="attention_backward",
    )(slopes, qkv, dcontext, segments[:, None], segments[None, :])


def swap(values):
    return lax.ppermute(values, "tensor", [(0, 1), (1, 0)])


def spread(values, count):
    if count == 2:
        return [values, swap(values)]
    return [lax.all_gather(values, "tensor", axis=0, tiled=True)]


def fold(parts, count):
    if count == 2:
        return swap(parts[1]).astype(jnp.float32) + parts[0].astype(jnp.float32)
    return lax.psum_scatter(parts[0], "tensor", scatter_dimension=0, tiled=True).astype(
        jnp.float32
    )


def to_order(parts, rank):
    if len(parts) == 2:
        own, other = parts
        return jnp.concatenate(
            [jnp.where(rank == 0, own, other), jnp.where(rank == 0, other, own)], axis=0
        )
    return parts[0]


def from_order(values, rank, count):
    if count == 2:
        half = values.shape[0] // 2
        return [
            lax.dynamic_slice_in_dim(values, rank * half, half, 0),
            lax.dynamic_slice_in_dim(values, (1 - rank) * half, half, 0),
        ]
    return [values]


def product(left, right):
    return jnp.dot(left, right, preferred_element_type=jnp.float32)


def add_up(lefts, rights):
    total = inner_rows(lefts[0], rights[0])
    for left, right in zip(lefts[1:], rights[1:]):
        total = total + inner_rows(left, right)
    return total


def total_over_all(vector, shared, rank):
    rows = lax.all_gather(vector[None], ("dp", "tensor"), axis=0, tiled=True)
    everyone = jnp.sum(rows[:, :shared], axis=0)
    count = lax.axis_size("tensor")
    split = rows[:, shared:].reshape(rows.shape[0] // count, count, -1)
    mine = lax.dynamic_index_in_dim(jnp.sum(split, axis=0), rank, 0, keepdims=False)
    return everyone, mine


def adamw(param, loss_slope, first, second, rate, decay):
    first_new = beta_first * first + (1.0 - beta_first) * loss_slope
    second_new = beta_second * second + (1.0 - beta_second) * loss_slope * loss_slope
    update = (
        first_new
        / (1.0 - beta_first**ADAM_STEP)
        / (jnp.sqrt(second_new / (1.0 - beta_second**ADAM_STEP)) + 1e-08)
    )
    return (param - rate * (update + decay * param), first_new, second_new)


MESH = pl.DeviceIdType.MESH
CHUNK = 64
MIB = 1024 * 1024


class Spot:
    def __init__(self, depth):
        dp = lax.axis_index("dp")
        self.depth = depth
        self.t = lax.axis_index("tensor")
        self.c = lax.rem(dp, 2)
        self.x = lax.rem(lax.div(dp, 2), 2)
        self.z = lax.div(dp, 4)
        self.twin = self.at(self.z, self.x, 1 - self.c)
        self.cross = self.at(self.z, 1 - self.x, self.c)
        self.pair = (dp, 1 - self.t)

    def index(self, z, x, c):
        return (z * 2 + x) * 2 + c

    def at(self, z, x, c):
        return (self.index(z, x, c), self.t)

    def farthest(self, i):
        n = self.depth
        if i == n - 1:
            return self.z
        down = jnp.where(n - 1 - i > self.z, n - 1 - i, n - 2 - i)
        up = jnp.where(i < self.z, i, i + 1)
        return jnp.where(2 * self.z < n, down, up)

    def greet(self, everyone=True):
        barrier = pltpu.get_barrier_semaphore()
        others = [self.twin, self.cross, self.pair] if everyone else [self.pair]
        for step in range(1, self.depth if everyone else 1):
            others.append(self.at(lax.rem(self.z + step, self.depth), self.x, self.c))
        for other in others:
            pl.semaphore_signal(barrier, inc=1, device_id=other, device_id_type=MESH)
        pl.semaphore_wait(barrier, len(others))


def push(source, target, send, arrive, to):
    return pltpu.make_async_remote_copy(
        src_ref=source,
        dst_ref=target,
        send_sem=send,
        recv_sem=arrive,
        device_id=to,
        device_id_type=MESH,
    )


def rows_of(ref, first, size):
    return ref.at[pl.ds(pl.multiple_of(first, size), size)]


class Gather:
    def __init__(self, spot, shards, fulls, zs, zr, xs, xr, cs, cr, ls):
        self.spot, self.shards, self.fulls = spot, shards, fulls
        self.zs, self.zr, self.xs, self.xr, self.cs, self.cr, self.ls = zs, zr, xs, xr, cs, cr, ls
        self.count = len(shards)

    @staticmethod
    def semaphores(count, depth):
        dma = pltpu.SemaphoreType.DMA
        return [
            dma((count, depth, 2)),
            dma((count, depth)),
            dma((count, depth)),
            dma((count, depth)),
            dma((count, 2 * depth)),
            dma((count, 2 * depth)),
            dma((count,)),
        ]

    def block(self, a, z, x, c):
        size = self.shards[a].shape[0]
        return rows_of(self.fulls[a], self.spot.index(z, x, c) * size, size)

    def along(self, a, bz, way, own=False):
        s = self.spot
        region = self.block(a, bz, s.x, s.c)
        to = s.at(s.z + (1 if way == 0 else -1), s.x, s.c)
        return push(
            self.shards[a] if own else region, region, self.zs.at[a, bz, way], self.zr.at[a, bz], to
        )

    def over(self, a, bz, own=False):
        s = self.spot
        region = self.block(a, bz, s.x, s.c)
        return push(
            self.shards[a] if own else region, region, self.xs.at[a, bz], self.xr.at[a, bz], s.cross
        )

    def across(self, a, bz, bx, own=False):
        s = self.spot
        region = self.block(a, bz, bx, s.c)
        k = bz * 2 + bx
        return push(
            self.shards[a] if own else region, region, self.cs.at[a, k], self.cr.at[a, k], s.twin
        )

    def keep(self, a):
        s = self.spot
        return pltpu.make_async_copy(
            self.shards[a], self.block(a, s.z, s.x, s.c), self.ls.at[a]
        )

    def start(self):
        s = self.spot
        for a in range(self.count):
            pl.when(s.z + 1 < s.depth)(lambda a=a: self.along(a, s.z, 0, True).start())
            pl.when(s.z > 0)(lambda a=a: self.along(a, s.z, 1, True).start())
            self.over(a, s.z, True).start()
        for a in range(self.count):
            self.across(a, s.z, s.x, True).start()
            self.keep(a).start()

    def z_step(self, a, step):
        s = self.spot
        for way in (0, 1):
            bz = s.z - step if way == 0 else s.z + step
            here = bz >= 0 if way == 0 else bz < s.depth
            onward = s.z + 1 < s.depth if way == 0 else s.z > 0

            @pl.when(here)
            def _():
                self.along(a, bz, way).wait_recv()
                pl.when(onward)(lambda: self.along(a, bz, way).start())
                self.over(a, bz).start()
                self.across(a, bz, s.x).start()

    def x_step(self, a, step):
        s = self.spot

        def take(bz):
            self.over(a, bz).wait_recv()
            self.across(a, bz, 1 - s.x).start()

        if step == 0:
            take(s.z)
            return
        pl.when(s.z - step >= 0)(lambda: take(s.z - step))
        pl.when(s.z + step < s.depth)(lambda: take(s.z + step))

    def finish(self):
        s = self.spot
        for a in range(self.count):
            self.keep(a).wait()
            for bz in range(s.depth):
                for bx in range(2):
                    self.across(a, bz, bx).wait()
                self.over(a, bz).wait_send()
                pl.when((bz <= s.z) & (s.z + 1 < s.depth))(
                    lambda a=a, bz=bz: self.along(a, bz, 0).wait_send()
                )
                pl.when((bz >= s.z) & (s.z > 0))(
                    lambda a=a, bz=bz: self.along(a, bz, 1).wait_send()
                )


STRIP = 16
BAND = 64


def strips(size, step, body):
    def one(i, carry):
        body(pl.multiple_of(i * step, step))
        return carry

    lax.fori_loop(0, size // step, one, 0)


class Scatter:
    def __init__(self, spot, grads, sums, cins, xins, zins, cs, cr, xs, xr, zs, zr):
        self.spot, self.grads, self.sums = spot, grads, sums
        self.cins, self.xins, self.zins = cins, xins, zins
        self.cs, self.cr, self.xs, self.xr, self.zs, self.zr = cs, cr, xs, xr, zs, zr
        self.count = len(grads)

    @staticmethod
    def scratch(shapes, depth):
        count, low = len(shapes), jnp.bfloat16
        dma = pltpu.SemaphoreType.DMA
        buffers = []
        for slots in (2 * depth, depth, depth):
            for rows, width in shapes:
                buffers.append(pltpu.VMEM((slots, rows, width), low))
        return buffers + [
            dma((count, 2 * depth)),
            dma((count, 2 * depth)),
            dma((count, depth)),
            dma((count, depth)),
            dma((count, depth)),
            dma((count, depth)),
        ]

    def first(self, a, z, x, c):
        return self.spot.index(z, x, c) * self.sums[a].shape[0]

    def across(self, a, bz, bx):
        s = self.spot
        k = bz * 2 + bx
        return push(
            rows_of(self.grads[a], self.first(a, bz, bx, 1 - s.c), self.sums[a].shape[0]),
            self.cins[a].at[k],
            self.cs.at[a, k],
            self.cr.at[a, k],
            s.twin,
        )

    def over(self, a, bz):
        s = self.spot
        return push(
            self.cins[a].at[bz * 2 + 1 - s.x],
            self.xins[a].at[bz],
            self.xs.at[a, bz],
            self.xr.at[a, bz],
            s.cross,
        )

    def along(self, a, bz, arriving=False):
        s = self.spot
        slot = bz if arriving else s.z
        return push(
            self.cins[a].at[bz * 2 + s.x],
            self.zins[a].at[slot],
            self.zs.at[a, bz],
            self.zr.at[a, slot],
            s.at(bz, s.x, s.c),
        )

    def start(self, a):
        s = self.spot
        for bx in (1 - s.x, s.x):
            for i in range(s.depth):
                self.across(a, s.farthest(i), bx).start()

    def own(self, a, bz, bx, r):
        here = pl.multiple_of(self.first(a, bz, bx, self.spot.c) + r, STRIP)
        return self.grads[a][pl.ds(here, STRIP), :].astype(jnp.float32)

    def c_step(self, a, i):
        s = self.spot
        bz = s.farthest(i)
        k = bz * 2 + 1 - s.x
        self.across(a, bz, 1 - s.x).wait_recv()
        cin = self.cins[a]

        def add(r):
            part = pl.ds(r, STRIP)
            total = self.own(a, bz, 1 - s.x, r) + cin[k, part, :].astype(jnp.float32)
            cin[k, part, :] = total.astype(jnp.bfloat16)

        strips(cin.shape[1], STRIP, add)
        self.over(a, bz).start()

    def x_step(self, a, i):
        s = self.spot
        bz = s.farthest(i)
        k = bz * 2 + s.x
        self.across(a, bz, s.x).wait_recv()
        self.over(a, bz).wait_recv()
        cin, xin, out = self.cins[a], self.xins[a], self.sums[a]

        def add(r):
            part = pl.ds(r, STRIP)
            total = (
                self.own(a, bz, s.x, r)
                + cin[k, part, :].astype(jnp.float32)
                + xin[bz, part, :].astype(jnp.float32)
            )
            if i < s.depth - 1:
                cin[k, part, :] = total.astype(jnp.bfloat16)
            else:
                out[part, :] = total

        strips(cin.shape[1], STRIP, add)
        if i < s.depth - 1:
            self.along(a, bz).start()

    def last_step(self, a):
        s = self.spot
        zin, out = self.zins[a], self.sums[a]
        slots = [lax.rem(s.z + step, s.depth) for step in range(1, s.depth)]
        for slot in slots:
            self.along(a, slot, True).wait_recv()

        def add(r):
            part = pl.ds(r, STRIP)
            total = out[part, :]
            for slot in slots:
                total = total + zin[slot, part, :].astype(jnp.float32)
            out[part, :] = total

        strips(out.shape[0], STRIP, add)

    def finish(self):
        s = self.spot
        for a in range(self.count):
            for i in range(s.depth):
                bz = s.farthest(i)
                for bx in range(2):
                    self.across(a, bz, bx).wait_send()
                self.over(a, bz).wait_send()
                if i < s.depth - 1:
                    self.along(a, bz).wait_send()


class Totals:
    def __init__(self, spot, stage, inbox, send, arrive, shared):
        self.spot, self.stage, self.inbox, self.send, self.arrive, self.shared = (
            spot, stage, inbox, send, arrive, shared,
        )

    @staticmethod
    def scratch(shape, depth):
        dma = pltpu.SemaphoreType.DMA
        return [
            pltpu.VMEM((4, *shape), jnp.float32),
            pltpu.VMEM((3 + depth, *shape), jnp.float32),
            dma((3 + depth,)),
            dma((3 + depth,)),
        ]

    def hop(self, number):
        to = (self.spot.twin, self.spot.cross)[number]
        return push(
            self.stage.at[number], self.inbox.at[number], self.send.at[number], self.arrive.at[number], to
        )

    def along(self, z, arriving=False):
        s = self.spot
        slot = 2 + (z if arriving else s.z)
        return push(
            self.stage.at[2], self.inbox.at[slot], self.send.at[2 + z], self.arrive.at[slot], s.at(z, s.x, s.c)
        )

    def pair(self):
        last = 2 + self.spot.depth
        part = pl.ds(0, self.shared)
        return push(
            self.stage.at[3, part], self.inbox.at[last, part], self.send.at[last], self.arrive.at[last], self.spot.pair
        )

    def others(self):
        s = self.spot
        return [lax.rem(s.z + step, s.depth) for step in range(1, s.depth)]

    def step(self, number):
        s = self.spot
        if number == 0:
            self.hop(0).start()
        elif number < 3:
            self.hop(number - 1).wait_recv()
            self.stage[number] = self.stage[number - 1] + self.inbox[number - 1]
            if number == 1:
                self.hop(1).start()
            else:
                for z in self.others():
                    self.along(z).start()
                self.inbox[2 + s.z] = self.stage[2]
        elif number == 3:
            for z in self.others():
                self.along(z, True).wait_recv()
            total = self.inbox[2]
            for z in range(1, s.depth):
                total = total + self.inbox[2 + z]
            self.stage[3] = total
            self.pair().start()
        else:
            self.pair().wait_recv()

    def result(self):
        part = slice(0, self.shared)
        return self.stage[3, part, :] + self.inbox[2 + self.spot.depth, part, :]

    def finish(self):
        self.hop(0).wait_send()
        self.hop(1).wait_send()
        for z in self.others():
            self.along(z).wait_send()
        self.pair().wait_send()


class Swap:
    def __init__(self, spot, source, target, send, arrive):
        self.spot, self.source, self.target, self.send, self.arrive = (
            spot,
            source,
            target,
            send,
            arrive,
        )

    def chunk(self, i, source_first=0, target_first=0):
        return push(
            rows_of(self.source, source_first + i * CHUNK, CHUNK),
            rows_of(self.target, target_first + i * CHUNK, CHUNK),
            self.send.at[i],
            self.arrive.at[i],
            self.spot.pair,
        )


def loop(first, last, body):
    def one(i, carry):
        body(i)
        return carry

    lax.fori_loop(first, last, one, 0)


def cast_into(source, target):
    def one(r):
        part = pl.ds(r, STRIP)
        target[part, :] = source[part, :].astype(target.dtype)

    strips(source.shape[0], STRIP, one)


def spread_kernel(depth, x, gain, shift, wide0, wide1, normed, full0, full1, own, low0, low1, ys, yr, yl, *sems):
    spot = Spot(depth)
    half = x.shape[0]
    base = spot.t * half
    cast_into(wide0, low0)
    cast_into(wide1, low1)
    spot.greet()
    gather = Gather(spot, (low0, low1), (full0, full1), *sems)
    gather.start()
    swap = Swap(spot, own, normed, ys, yr)

    def keep(i):
        return pltpu.make_async_copy(
            rows_of(own, i * CHUNK, CHUNK), rows_of(normed, base + i * CHUNK, CHUNK), yl.at[i]
        )

    def work(i):
        def one(r):
            part = pl.ds(i * CHUNK + r, BAND)
            own[part, :] = standardise_features(x[part, :], gain[...], shift[...])[0]

        strips(CHUNK, BAND, one)
        swap.chunk(i, 0, base).start()
        keep(i).start()

    loop(0, half // CHUNK, work)
    for step in range(1, depth):
        for a in range(2):
            gather.z_step(a, step)
        for a in range(2):
            gather.x_step(a, step - 1)
    for a in range(2):
        gather.x_step(a, depth - 1)

    def done(i):
        keep(i).wait()
        swap.chunk(i, 0, base).wait_send()
        swap.chunk(i, 0, half - base).wait_recv()

    loop(0, half // CHUNK, done)
    gather.finish()


def fold_rows(values):
    return jnp.sum(values.reshape(-1, 8, values.shape[-1]), axis=0)


def core_kernel(depth, part, x, bias, gain, shift, slope, other, shard, down, up_bias, resid, dresid, low, gup, contracted, sum0, sums, ups, up, shard_low, gdown, twos, outs, act, dpre, twos_t, outs_t, normed, own, inbox, inbox2, totals, ps, pr, ys, yr, ns, nr, ls, lr, lk, *rest):
    spot = Spot(depth)
    half, model = x.shape
    hidden = down.shape[1]
    width = min(512, hidden)
    side = min(256, half)
    blocks = hidden // width
    base = pl.multiple_of(spot.t * half, half)
    away = pl.multiple_of(half - base, half)
    chunks = half // CHUNK
    cast_into(shard, shard_low)
    spot.greet()
    gather = Gather(spot, (shard_low,), (up,), *rest[9:])
    gather.start()
    first = Swap(spot, part, inbox, ps, pr)
    second = Swap(spot, twos, twos, ys, yr)
    third = Swap(spot, normed, inbox2, ns, nr)
    fourth = Swap(spot, own, low, ls, lr)
    loop(0, chunks, lambda i: first.chunk(i, away, 0).start())

    def place(i):
        here = pl.ds(pl.multiple_of(base + i * side, side), side)
        there = pl.ds(pl.multiple_of(away + i * side, side), side)
        piece = pl.ds(pl.multiple_of(i * side, side), side)
        outs[here, :] = slope[piece, :].astype(jnp.bfloat16)
        outs[there, :] = other[piece, :]
        outs_t[:, here] = outs[here, :].T
        outs_t[:, there] = outs[there, :].T

    loop(0, half // side, place)

    def enter(i):
        first.chunk(i, away, 0).wait_recv()

        def one(r):
            here = pl.ds(i * CHUNK + r, BAND)
            there = pl.ds(pl.multiple_of(base + i * CHUNK + r, BAND), BAND)
            total = (
                x[here, :]
                + (inbox[here, :].astype(jnp.float32) + part[there, :].astype(jnp.float32))
                + bias[...]
            )
            resid[here, :] = total
            twos[there, :] = standardise_features(total, gain[...], shift[...])[0]

        strips(CHUNK, BAND, one)
        second.chunk(i, base, base).start()

    todo = []
    for step in range(depth):
        if step + 1 < depth:
            todo.append((gather.z_step, step + 1))
        todo.append((gather.x_step, step))
    for i in range(chunks):
        enter(i)
        if i > 0 and todo:
            act_on, step = todo.pop(0)
            act_on(0, step)
    for act_on, step in todo:
        act_on(0, step)
    gather.finish()

    def forward(start, again):
        here = pl.ds(start, half)
        twos_t[:, here] = twos[here, :].T

        def block(n):
            cols = pl.ds(pl.multiple_of(n * width, width), width)
            pre = product(twos[here, :], up[:, cols]) + up_bias[:, cols]
            square = pre * pre
            inner = 0.7978845608 * pre * (1.0 + 0.044715 * square)
            gate = 0.5 + 0.5 * jnp.tanh(inner)
            value = pre * gate
            act[here, cols] = value.astype(jnp.bfloat16)
            tilt = gate + value * (1.0 - gate) * (
                2.0 * 0.7978845608 + (6.0 * 0.7978845608 * 0.044715) * square
            )
            grad = product(outs[here, :], down[:, cols]) * tilt
            dpre[here, cols] = grad.astype(jnp.bfloat16)
            total = jnp.sum(fold_rows(grad), axis=0, keepdims=True)
            ups[:, cols] = ups[:, cols] + total if again else total

        loop(0, blocks, block)

    def contract(start, target):
        def one(i):
            here = pl.ds(pl.multiple_of(start + i * side, side), side)
            there = pl.ds(pl.multiple_of(target + i * side, side), side)
            contracted[there, :] = times_transposed(act[here, :], down[...]).astype(
                jnp.bfloat16
            )

        loop(0, half // side, one)

    def reduce_norm(i, start):
        here = pl.ds(pl.multiple_of(start + i * side, side), side)
        normed[here, :] = times_transposed(dpre[here, :], up[...]).astype(jnp.bfloat16)

    forward(base, False)
    contract(base, 0)
    loop(0, chunks, lambda i: second.chunk(i, away, away).wait_recv())
    forward(away, True)

    def send_norm(i):
        reduce_norm(i, away)
        for j in range(side // CHUNK):
            third.chunk(i * (side // CHUNK) + j, away, 0).start()

    loop(0, half // side, send_norm)
    loop(0, half // side, lambda i: reduce_norm(i, base))

    def weights(target, left, right):
        def one(n):
            cols = pl.ds(pl.multiple_of(n * width, width), width)
            target[:, cols] = product(left[...], right[:, cols]).astype(jnp.bfloat16)

        loop(0, blocks, one)

    weights(gdown, outs_t, act)
    scatter = Scatter(spot, (gdown,), (sum0,), rest[0:1], rest[1:2], rest[2:3], *rest[3:9])
    scatter.start(0)
    totals[...] = jnp.zeros_like(totals)
    weights(gup, twos_t, dpre)
    for i in range(depth):
        scatter.c_step(0, i)

    def keep(i):
        return pltpu.make_async_copy(
            rows_of(own, i * CHUNK, CHUNK), rows_of(low, base + i * CHUNK, CHUNK), lk.at[i]
        )

    def leave(i):
        third.chunk(i, away, 0).wait_recv()

        def one(r):
            here = pl.ds(i * CHUNK + r, BAND)
            there = pl.ds(pl.multiple_of(base + i * CHUNK + r, BAND), BAND)
            grad = inbox2[here, :].astype(jnp.float32) + normed[there, :].astype(jnp.float32)
            values = resid[here, :]
            centred = values - jnp.mean(values, axis=-1, keepdims=True)
            spread = lax.rsqrt(jnp.mean(centred * centred, axis=-1, keepdims=True) + 1e-05)
            unit = centred * spread
            out = slope[here, :]
            total = out + standardise_features_reverse(grad, unit, spread, gain[...])
            dresid[here, :] = total
            own[here, :] = total.astype(jnp.bfloat16)
            for spot_in, term in enumerate((total, out, grad * unit, grad)):
                totals[spot_in] += fold_rows(term)

        strips(CHUNK, BAND, one)
        fourth.chunk(i, 0, base).start()
        keep(i).start()

    loop(0, chunks, leave)
    contract(away, half)
    for i in range(depth):
        scatter.x_step(0, i)
    sums[...] = jnp.zeros_like(sums)
    for number in range(4):
        sums[number : number + 1, :] = jnp.sum(totals[number], axis=0, keepdims=True)
    scatter.last_step(0)

    def done(i):
        keep(i).wait()
        first.chunk(i, away, 0).wait_send()
        second.chunk(i, base, base).wait_send()
        third.chunk(i, away, 0).wait_send()
        fourth.chunk(i, 0, base).wait_send()
        fourth.chunk(i, 0, away).wait_recv()

    loop(0, chunks, done)
    scatter.finish()


def leave_kernel(depth, ones, dqkv, low, dresid, x, gain, early, ups, qv, grad_dense, slope, sum0, sum1, vector, ups_sum, qv_sum, grad, ones_t, part, inbox, totals, ps, pr, *rest):
    spot = Spot(depth)
    half = x.shape[0]
    base = pl.multiple_of(spot.t * half, half)
    away = pl.multiple_of(half - base, half)
    first = Swap(spot, part, inbox, ps, pr)
    chunks = half // CHUNK
    side = min(256, half)
    width = min(512, dqkv.shape[1])

    def turn(i):
        here = pl.ds(pl.multiple_of(i * half, half), half)
        ones_t[:, here] = ones[here, :].T

    loop(0, 2, turn)
    spot.greet()
    scatter = Scatter(
        spot, (grad, grad_dense), (sum0, sum1), rest[0:2], rest[2:4], rest[4:6], *rest[6:12]
    )
    scatter.start(1)

    def weights(n):
        cols = pl.ds(pl.multiple_of(n * width, width), width)
        grad[:, cols] = product(ones_t[...], dqkv[:, cols]).astype(jnp.bfloat16)

    loop(0, dqkv.shape[1] // width, weights)
    scatter.start(0)

    def reduce_norm(i, start):
        here = pl.ds(pl.multiple_of(start + i * side, side), side)
        part[here, :] = times_transposed(dqkv[here, :], low[...]).astype(jnp.bfloat16)

    def send_norm(i):
        reduce_norm(i, away)
        for j in range(side // CHUNK):
            first.chunk(i * (side // CHUNK) + j, away, 0).start()

    loop(0, half // side, send_norm)
    for a in (1, 0):
        for i in range(depth):
            scatter.c_step(a, i)
    loop(0, half // side, lambda i: reduce_norm(i, base))
    model = x.shape[1]
    every = Totals(spot, *rest[12:16], 8)
    totals[...] = jnp.zeros_like(totals)
    every.stage[0] = jnp.zeros_like(every.stage[0])
    every.stage[0, 0:8, :] = early[...]
    row, pieces = 8, []
    for source, target in ((ups, ups_sum), (qv, qv_sum)):
        for start in range(0, source.shape[1], model):
            every.stage[0, row : row + 1, :] = source[:, start : start + model]
            pieces.append((target, start, row))
            row += 1

    def work(i):
        first.chunk(i, half - base, 0).wait_recv()

        def one(r):
            here = pl.ds(i * CHUNK + r, BAND)
            there = pl.ds(pl.multiple_of(base + i * CHUNK + r, BAND), BAND)
            grad = inbox[here, :].astype(jnp.float32) + part[there, :].astype(jnp.float32)
            values = x[here, :]
            centred = values - jnp.mean(values, axis=-1, keepdims=True)
            spread = lax.rsqrt(jnp.mean(centred * centred, axis=-1, keepdims=True) + 1e-05)
            unit = centred * spread
            slope[here, :] = dresid[here, :] + standardise_features_reverse(
                grad, unit, spread, gain[...]
            )
            for place, term in enumerate((grad * unit, grad)):
                totals[place] += fold_rows(term)

        strips(CHUNK, BAND, one)

    todo = [(scatter.x_step, a, i) for i in range(depth) for a in (1, 0)]
    for i in range(chunks):
        work(i)
        if todo:
            act, a, step = todo.pop(0)
            act(a, step)
    for place in range(2):
        every.stage[0, 4 + place : 5 + place, :] = jnp.sum(totals[place], axis=0, keepdims=True)
    every.step(0)
    for act, a, step in todo:
        act(a, step)
    for number in range(1, 4):
        every.step(number)
    for a in range(2):
        scatter.last_step(a)
    every.step(4)
    vector[...] = every.result()
    for target, start, row in pieces:
        target[:, start : start + model] = every.stage[3, row : row + 1, :]
    loop(0, chunks, lambda i: first.chunk(i, half - base, 0).wait_send())
    every.finish()
    scatter.finish()


def vmem(count=1):
    return [pl.BlockSpec(memory_space=pltpu.VMEM)] * count


def anywhere(count=1):
    return [pl.BlockSpec(memory_space=pl.ANY)] * count


def call(body, number, name, depth, outs, in_specs, out_specs, scratch, args, mib=48):
    size = sum(a.size * a.dtype.itemsize for a in args) + sum(
        o.size * jnp.dtype(o.dtype).itemsize for o in outs
    )
    return pl.pallas_call(
        functools.partial(body, depth),
        out_shape=outs,
        in_specs=in_specs,
        out_specs=out_specs,
        scratch_shapes=scratch,
        cost_estimate=pl.CostEstimate(flops=0, bytes_accessed=size, transcendentals=0),
        compiler_params=pltpu.CompilerParams(
            collective_id=number, has_side_effects=True, vmem_limit_bytes=mib * MIB
        ),
        name=name,
    )(*args)


def shaped(shape, dtype=jnp.bfloat16):
    return jax.ShapeDtypeStruct(shape, dtype)


def spread_call(depth, x, gain, shift, shards):
    half, width = x.shape
    dma = pltpu.SemaphoreType.DMA
    chunks = half // CHUNK
    outs = [shaped((2 * half, width))]
    outs += [shaped((4 * depth * s.shape[0], s.shape[1])) for s in shards]
    scratch = [pltpu.VMEM((half, width), jnp.bfloat16)]
    scratch += [pltpu.VMEM(s.shape, jnp.bfloat16) for s in shards]
    scratch += [dma((chunks,))] * 3 + Gather.semaphores(2, depth)
    return call(
        spread_kernel, 0, "spread", depth, outs, vmem(5), anywhere(3), scratch,
        (x, gain[None], shift[None], *shards),
    )


def core_call(depth, part, x, bias, gain, shift, slope, other, shard, down, up_bias):
    half, model = x.shape
    tokens, hidden = 2 * half, down.shape[1]
    low, full, dma = jnp.bfloat16, jnp.float32, pltpu.SemaphoreType.DMA
    chunks = half // CHUNK
    shapes = [(model // (4 * depth), hidden)]
    outs = [
        shaped((half, model), full),
        shaped((half, model), full),
        shaped((tokens, model)),
        shaped((model, hidden)),
        shaped((tokens, model)),
        shaped(shapes[0], full),
        shaped((8, model), full),
        shaped((1, hidden), full),
    ]
    scratch = [
        pltpu.VMEM((model, hidden), low),
        pltpu.VMEM(shard.shape, low),
        pltpu.VMEM((model, hidden), low),
        pltpu.VMEM((tokens, model), low),
        pltpu.VMEM((tokens, model), low),
        pltpu.VMEM((tokens, hidden), low),
        pltpu.VMEM((tokens, hidden), low),
        pltpu.VMEM((model, tokens), low),
        pltpu.VMEM((model, tokens), low),
        pltpu.VMEM((tokens, model), low),
        pltpu.VMEM((half, model), low),
        pltpu.VMEM((half, model), low),
        pltpu.VMEM((half, model), low),
        pltpu.VMEM((4, 8, model), full),
    ]
    scratch += [dma((chunks,))] * 9 + Scatter.scratch(shapes, depth)
    scratch += Gather.semaphores(1, depth)
    return call(
        core_kernel, 1, "core", depth, outs, vmem(10),
        vmem(2) + anywhere() + vmem(5), scratch,
        (part, x, bias[None], gain[None], shift[None], slope, other, shard, down, up_bias[None]),
        60,
    )


def leave_call(depth, ones, dqkv, low, dresid, x, gain, early, ups, qv, grad_dense):
    half, width = x.shape
    dma = pltpu.SemaphoreType.DMA
    chunks = half // CHUNK
    full = jnp.float32
    grads = ((width, dqkv.shape[1]), grad_dense.shape)
    shapes = [(g[0] // (4 * depth), g[1]) for g in grads]
    outs = [shaped((half, width), full)]
    outs += [shaped(s, full) for s in shapes]
    outs += [shaped((8, width), full), shaped(ups.shape, full), shaped(qv.shape, full)]
    scratch = [
        pltpu.VMEM(grads[0], jnp.bfloat16),
        pltpu.VMEM((width, 2 * half), jnp.bfloat16),
        pltpu.VMEM((2 * half, width), jnp.bfloat16),
        pltpu.VMEM((half, width), jnp.bfloat16),
        pltpu.VMEM((2, 8, width), full),
    ]
    scratch += [dma((chunks,))] * 2 + Scatter.scratch(shapes, depth)
    scratch += Totals.scratch((16, width), depth)
    return call(
        leave_kernel, 2, "leave", depth, outs, vmem(10), vmem(6), scratch,
        (ones, dqkv, low, dresid, x, gain[None], early, ups, qv, grad_dense),
    )


def reverse_kernel(
    depth, block, slopes, x, grad, rows_seg, cols_seg, gup, contracted, out, sums, sum0, arrived,
    offsets, dkeys, dvalues, dquery, ds, dr, *rest
):
    step = pl.program_id(0)
    last = pl.num_programs(0) - 1
    spot = Spot(depth)
    chunks, half = arrived.shape[0] // CHUNK, arrived.shape[0]
    swap = Swap(spot, contracted, arrived, ds, dr)
    scatter = Scatter(spot, (gup,), (sum0,), rest[0:1], rest[1:2], rest[2:3], *rest[3:])

    @pl.when(step == 0)
    def _():
        spot.greet()
        scatter.start(0)
        loop(0, chunks, lambda i: swap.chunk(i, half, 0).start())

    backward_kernel(
        block, slopes, x, grad, rows_seg, cols_seg, out, sums, offsets, dkeys, dvalues, dquery, True
    )

    @pl.when(step == 0)
    def _():
        for i in range(depth):
            scatter.c_step(0, i)

    for i in range(depth - 1):
        @pl.when(step == jnp.minimum(i + 1, last))
        def _():
            scatter.x_step(0, i)

    @pl.when(step == last)
    def _():
        scatter.x_step(0, depth - 1)
        scatter.last_step(0)
        loop(0, chunks, lambda i: swap.chunk(i, half, 0).wait())
        scatter.finish()


def reverse_call(depth, qkv, segments, slopes, dcontext, gup, contracted):
    length, width = qkv.shape
    model, hidden = gup.shape
    pairs = width // (6 * HEAD_DIM)
    block = min(256, length)
    span = min(length, block + MAX_SPAN)
    half = length // 2
    dma = pltpu.SemaphoreType.DMA
    shapes = [(model // (4 * depth), hidden)]
    return pl.pallas_call(
        functools.partial(reverse_kernel, depth, block),
        grid=(pairs,),
        out_shape=(
            shaped((length, width)),
            shaped((1, 4 * HEAD_DIM * pairs), jnp.float32),
            shaped(shapes[0], jnp.float32),
            shaped((half, model)),
        ),
        in_specs=[
            pl.BlockSpec(memory_space=pltpu.SMEM),
            pl.BlockSpec((length, 6 * HEAD_DIM), lambda p: (0, p)),
            pl.BlockSpec((length, 2 * HEAD_DIM), lambda p: (0, p)),
            pl.BlockSpec((length, 1), lambda p: (0, 0)),
            pl.BlockSpec((1, length), lambda p: (0, 0)),
            pl.BlockSpec(memory_space=pltpu.VMEM),
            pl.BlockSpec(memory_space=pl.ANY),
        ],
        out_specs=(
            pl.BlockSpec((length, 6 * HEAD_DIM), lambda p: (0, p)),
            pl.BlockSpec((1, 4 * HEAD_DIM), lambda p: (0, p)),
            pl.BlockSpec(memory_space=pltpu.VMEM),
            pl.BlockSpec(memory_space=pl.ANY),
        ),
        scratch_shapes=[
            pltpu.VMEM((span, length), jnp.float32),
            pltpu.VMEM((length, HEAD_DIM), jnp.float32),
            pltpu.VMEM((length, HEAD_DIM), jnp.float32),
            pltpu.VMEM((length, HEAD_DIM), jnp.float32),
        ]
        + [dma((half // CHUNK,))] * 2
        + Scatter.scratch(shapes, depth),
        cost_estimate=pl.CostEstimate(
            flops=10 * length * span * width // 3,
            bytes_accessed=14 * length * width // 3,
            transcendentals=length * span * pairs * 2,
        ),
        compiler_params=pltpu.CompilerParams(
            collective_id=3, has_side_effects=True, vmem_limit_bytes=48 * MIB
        ),
        name="attention_backward",
    )(slopes, qkv, dcontext, segments[:, None], segments[None, :], gup, contracted)


def direct_kernel(
    depth, block, slopes, x, rows_seg, cols_seg, shard, out, full, offsets, shard_low, *sems
):
    step = pl.program_id(0)
    last = pl.num_programs(0) - 1
    spot = Spot(depth)
    gather = Gather(spot, (shard_low,), (full,), *sems)

    @pl.when(step == 0)
    def _():
        cast_into(shard, shard_low)
        spot.greet()
        gather.start()

    forward_kernel(block, slopes, x, rows_seg, cols_seg, out, offsets)

    for i in range(depth):

        @pl.when(step == jnp.minimum(i, last))
        def _():
            if i + 1 < depth:
                gather.z_step(0, i + 1)
            if i > 0:
                gather.x_step(0, i - 1)

    @pl.when(step == last)
    def _():
        gather.x_step(0, depth - 1)
        gather.finish()


def direct_call(depth, qkv, segments, slopes, shard):
    length, width = qkv.shape
    pairs = width // (6 * HEAD_DIM)
    block = min(256, length)
    span = min(length, block + MAX_SPAN)
    return pl.pallas_call(
        functools.partial(direct_kernel, depth, block),
        grid=(pairs,),
        out_shape=(
            shaped((length, width // 3)),
            shaped((4 * depth * shard.shape[0], shard.shape[1])),
        ),
        in_specs=[
            pl.BlockSpec(memory_space=pltpu.SMEM),
            pl.BlockSpec((length, 6 * HEAD_DIM), lambda p: (0, p)),
            pl.BlockSpec((length, 1), lambda p: (0, 0)),
            pl.BlockSpec((1, length), lambda p: (0, 0)),
            pl.BlockSpec(memory_space=pltpu.VMEM),
        ],
        out_specs=(
            pl.BlockSpec((length, 2 * HEAD_DIM), lambda p: (0, p)),
            pl.BlockSpec(memory_space=pl.ANY),
        ),
        scratch_shapes=[
            pltpu.VMEM((length, span), jnp.float32),
            pltpu.VMEM(shard.shape, jnp.bfloat16),
        ]
        + Gather.semaphores(1, depth),
        cost_estimate=pl.CostEstimate(
            flops=4 * length * span * width // 3,
            bytes_accessed=8 * length * width // 3,
            transcendentals=length * span * pairs * 2,
        ),
        compiler_params=pltpu.CompilerParams(
            collective_id=4, has_side_effects=True, vmem_limit_bytes=40 * MIB
        ),
        name="attention_forward",
    )(slopes, qkv, segments[:, None], segments[None, :], shard)


def update_kernel(kinds, *refs):
    count = len(kinds)
    ins, outs = refs[: 4 * count], refs[4 * count :]
    for number, (rate, decay) in enumerate(kinds):
        given, made = ins[4 * number : 4 * number + 4], outs[4 * number : 4 * number + 4]

        def one(part, given=given, made=made, rate=rate, decay=decay):
            param, grad, first, second = (ref[part, :] for ref in given)
            made[0][part, :] = grad
            for target, value in zip(made[1:], adamw(param, grad, first, second, rate, decay)):
                target[part, :] = value

        rows = given[0].shape[0]
        if rows == 1:
            one(slice(0, 1))
        else:
            strips(rows, STRIP, lambda r, one=one: one(pl.ds(r, STRIP)))


def update_call(params, grads, firsts, seconds):
    kinds, args, outs, turned = [], [], [], (2, 6)
    for index in range(12):
        matrix = index in (0, 2, 4, 6)
        kinds.append((0.01, 0.1) if matrix else (0.1, 0.0))
        for value in (params[index], grads[index], firsts[index], seconds[index]):
            value = value.T if index in turned else value if matrix else value[None]
            args.append(value)
            outs.append(shaped(value.shape, jnp.float32))
    size = 8 * sum(a.size for a in args)
    made = pl.pallas_call(
        functools.partial(update_kernel, kinds),
        out_shape=outs,
        in_specs=vmem(48),
        out_specs=vmem(48),
        cost_estimate=pl.CostEstimate(flops=0, bytes_accessed=size, transcendentals=0),
        compiler_params=pltpu.CompilerParams(vmem_limit_bytes=32 * MIB),
        name="update",
    )(*args)
    groups = []
    for index in range(12):
        plain = index in (0, 4)
        groups.append(
            [
                v if plain else v.T if index in turned else v[0]
                for v in made[4 * index : 4 * index + 4]
            ]
        )
    return tuple([g[place] for g in groups] for place in range(4))


def linked(
    entering_activations,
    segment_ids,
    leaving_activation_slope,
    qkv_weight,
    qv_bias,
    dense_weight,
    dense_bias,
    up_weight,
    up_bias,
    down_weight,
    down_bias,
    mixer_scale_factor,
    mixer_offset_term,
    perceptron_scale_factor,
    perceptron_offset_term,
):
    depth = lax.axis_size("dp") // 4
    rank = lax.axis_index("tensor")
    local_heads = qkv_weight.shape[1] // (3 * HEAD_DIM)
    slopes = head_slopes(rank * local_heads, local_heads)
    segments = segment_ids[0]
    ones, qkv_low, dense_low = spread_call(
        depth,
        entering_activations,
        mixer_scale_factor,
        mixer_offset_term,
        (qkv_weight, dense_weight.T),
    )
    out_own, ones = lax.optimization_barrier(
        (leaving_activation_slope.astype(jnp.bfloat16), ones)
    )
    out_other = swap(out_own)
    qkv = (product(ones, qkv_low) + full_bias(qv_bias, local_heads)).astype(jnp.bfloat16)
    context, down_low = direct_call(depth, qkv, segments, slopes, down_weight.T)
    dense_part = times_transposed(context, dense_low).astype(jnp.bfloat16)
    resid, dresid, resid_low, grad_up, down_part, grad_down, early, up_bias_part = core_call(
        depth,
        dense_part,
        entering_activations,
        dense_bias,
        perceptron_scale_factor,
        perceptron_offset_term,
        leaving_activation_slope,
        out_other,
        up_weight,
        down_low,
        up_bias,
    )
    dcontext = times_transposed(resid_low, jnp.swapaxes(dense_low, 0, 1)).astype(jnp.bfloat16)
    grad_dense = inner_rows(resid_low, context).astype(jnp.bfloat16)
    dqkv_low, qv_part, grad_up, arrived = reverse_call(
        depth, qkv, segments, slopes, dcontext, grad_up, down_part
    )
    half = resid.shape[0]
    block_out = (
        resid + (arrived.astype(jnp.float32) + down_part[:half].astype(jnp.float32)) + down_bias
    )
    entering_slope, grad_qkv, grad_dense, vector, ups, qvs = leave_call(
        depth,
        ones,
        dqkv_low,
        qkv_low,
        dresid,
        entering_activations,
        mixer_scale_factor,
        early,
        up_bias_part,
        qv_part,
        grad_dense,
    )
    return (
        block_out,
        entering_slope,
        (
            grad_qkv,
            qvs[0],
            grad_dense.T,
            vector[0],
            grad_up,
            ups[0],
            grad_down.T,
            vector[1],
            vector[4],
            vector[5],
            vector[2],
            vector[3],
        ),
    )


def general(
    entering_activations,
    segment_ids,
    leaving_activation_slope,
    qkv_weight,
    qv_bias,
    dense_weight,
    dense_bias,
    up_weight,
    up_bias,
    down_weight,
    down_bias,
    mixer_scale_factor,
    mixer_offset_term,
    perceptron_scale_factor,
    perceptron_offset_term,
):
    qkv_low, dense_low, up_low, down_low = (
        lax.all_gather(qkv_weight.astype(jnp.bfloat16), "dp", axis=0, tiled=True),
        lax.all_gather(dense_weight.astype(jnp.bfloat16), "dp", axis=1, tiled=True),
        lax.all_gather(up_weight.astype(jnp.bfloat16), "dp", axis=0, tiled=True),
        lax.all_gather(down_weight.astype(jnp.bfloat16), "dp", axis=1, tiled=True),
    )
    local_heads = qkv_low.shape[1] // (3 * HEAD_DIM)
    tensor_rank = lax.axis_index("tensor")
    count = lax.axis_size("tensor")
    slopes = head_slopes(tensor_rank * local_heads, local_heads)
    segments = segment_ids[0]
    mixer_standardised, mixer_unit_spread1, mixer_reciprocal_spread1 = standardise_features(
        entering_activations, mixer_scale_factor, mixer_offset_term
    )
    ones = spread(mixer_standardised, count)
    outs = spread(leaving_activation_slope.astype(jnp.bfloat16), count)
    qkv_bias = full_bias(qv_bias, local_heads)
    qkv = to_order([(product(one, qkv_low) + qkv_bias).astype(jnp.bfloat16) for one in ones], tensor_rank)
    context = attention_forward(qkv, segments, slopes)
    contexts = from_order(context, tensor_rank, count)
    skip_path_sum = (
        entering_activations
        + fold([product(part, dense_low).astype(jnp.bfloat16) for part in contexts], count)
        + dense_bias
    )
    perceptron_standardised, perceptron_unit_spread2, perceptron_reciprocal_spread2 = (
        standardise_features(skip_path_sum, perceptron_scale_factor, perceptron_offset_term)
    )
    twos = spread(perceptron_standardised, count)
    acts, dpres, dpre_lows, pre_parts = [], [], [], []
    for two, out in zip(twos, outs):
        act_val, act_slope = gelu_parts(product(two, up_low) + up_bias)
        acts.append(act_val.astype(jnp.bfloat16))
        dpres.append(times_transposed(out, down_low) * act_slope)
        dpre_lows.append(dpres[-1].astype(jnp.bfloat16))
        pre_parts.append(times_transposed(dpre_lows[-1], up_low).astype(jnp.bfloat16))
    pre_perceptron_sensitivity = fold(pre_parts, count)
    block_out = (
        skip_path_sum
        + fold([product(act, down_low).astype(jnp.bfloat16) for act in acts], count)
        + down_bias
    )
    contraction_sensitivity = add_up(acts, outs).astype(jnp.bfloat16)
    expansion_sensitivity = add_up(twos, dpre_lows).astype(jnp.bfloat16)
    up_bias_part = sum(jnp.sum(dpre, axis=0) for dpre in dpres)
    skip_path_sensitivity = leaving_activation_slope + standardise_features_reverse(
        pre_perceptron_sensitivity,
        perceptron_unit_spread2,
        perceptron_reciprocal_spread2,
        perceptron_scale_factor,
    )
    resids = spread(skip_path_sensitivity.astype(jnp.bfloat16), count)
    mixer_merge_sensitivity = add_up(contexts, resids).astype(jnp.bfloat16)
    dcontext = to_order(
        [times_transposed(resid, dense_low).astype(jnp.bfloat16) for resid in resids], tensor_rank
    )
    dqkv_low, dqkv_sums = attention_backward(qkv, segments, slopes, dcontext)
    dqkv_lows = from_order(dqkv_low, tensor_rank, count)
    packed_triple_slope = add_up(ones, dqkv_lows).astype(jnp.bfloat16)
    triple = dqkv_sums.reshape(local_heads, 3, HEAD_DIM)
    qv_part = jnp.stack([triple[:, 0], triple[:, 2]], axis=1).reshape(-1)
    pre_mixer_sensitivity = fold(
        [times_transposed(part, qkv_low).astype(jnp.bfloat16) for part in dqkv_lows], count
    )
    entering_activation_slope = skip_path_sensitivity + standardise_features_reverse(
        pre_mixer_sensitivity, mixer_unit_spread1, mixer_reciprocal_spread1, mixer_scale_factor
    )
    early, up_bias_grad = total_over_all(
        jnp.concatenate(
            [
                jnp.sum(skip_path_sensitivity, axis=0),
                jnp.sum(leaving_activation_slope, axis=0),
                jnp.sum(pre_perceptron_sensitivity * perceptron_unit_spread2, axis=0),
                jnp.sum(pre_perceptron_sensitivity, axis=0),
                up_bias_part,
            ]
        ),
        4 * D,
        tensor_rank,
    )
    dense_bias_grad, down_bias_grad, gain_two_grad, shift_two_grad = jnp.split(early, 4)
    late, qv_bias_grad = total_over_all(
        jnp.concatenate(
            [
                jnp.sum(pre_mixer_sensitivity * mixer_unit_spread1, axis=0),
                jnp.sum(pre_mixer_sensitivity, axis=0),
                qv_part,
            ]
        ),
        2 * D,
        tensor_rank,
    )
    gain_one_grad, shift_one_grad = jnp.split(late, 2)
    packed_triple_slope, mixer_merge_sensitivity, expansion_sensitivity, contraction_sensitivity = (
        part.astype(jnp.float32)
        for part in (
            lax.psum_scatter(packed_triple_slope, "dp", scatter_dimension=0, tiled=True),
            lax.psum_scatter(mixer_merge_sensitivity, "dp", scatter_dimension=1, tiled=True),
            lax.psum_scatter(expansion_sensitivity, "dp", scatter_dimension=0, tiled=True),
            lax.psum_scatter(contraction_sensitivity, "dp", scatter_dimension=1, tiled=True),
        )
    )
    return block_out, entering_activation_slope, (
        packed_triple_slope,
        qv_bias_grad,
        mixer_merge_sensitivity,
        dense_bias_grad,
        expansion_sensitivity,
        up_bias_grad,
        contraction_sensitivity,
        down_bias_grad,
        gain_one_grad,
        shift_one_grad,
        gain_two_grad,
        shift_two_grad,
    )


def local(
    entering_activations,
    segment_ids,
    leaving_activation_slope,
    qkv_weight,
    qv_bias,
    dense_weight,
    dense_bias,
    up_weight,
    up_bias,
    down_weight,
    down_bias,
    mixer_scale_factor,
    mixer_offset_term,
    perceptron_scale_factor,
    perceptron_offset_term,
    first_qkv_weight,
    first_qv_bias,
    first_dense_weight,
    first_dense_bias,
    first_up_weight,
    first_up_bias,
    first_down_weight,
    first_down_bias,
    first_norm1_gain,
    first_norm1_bias,
    first_norm2_gain,
    first_norm2_bias,
    second_qkv_weight,
    second_qv_bias,
    second_dense_weight,
    second_dense_bias,
    second_up_weight,
    second_up_bias,
    second_down_weight,
    second_down_bias,
    second_norm1_gain,
    second_norm1_bias,
    second_norm2_gain,
    second_norm2_bias,
):
    params = (
        qkv_weight,
        qv_bias,
        dense_weight,
        dense_bias,
        up_weight,
        up_bias,
        down_weight,
        down_bias,
        mixer_scale_factor,
        mixer_offset_term,
        perceptron_scale_factor,
        perceptron_offset_term,
    )
    firsts = (
        first_qkv_weight,
        first_qv_bias,
        first_dense_weight,
        first_dense_bias,
        first_up_weight,
        first_up_bias,
        first_down_weight,
        first_down_bias,
        first_norm1_gain,
        first_norm1_bias,
        first_norm2_gain,
        first_norm2_bias,
    )
    seconds = (
        second_qkv_weight,
        second_qv_bias,
        second_dense_weight,
        second_dense_bias,
        second_up_weight,
        second_up_bias,
        second_down_weight,
        second_down_bias,
        second_norm1_gain,
        second_norm1_bias,
        second_norm2_gain,
        second_norm2_bias,
    )
    whole_line = lax.axis_size("tensor") == 2 and lax.axis_size("dp") % 4 == 0
    route = linked if whole_line and segment_ids.shape[0] == 1 else general
    block_out, entering_activation_slope, parameter_slopes = route(
        entering_activations,
        segment_ids,
        leaving_activation_slope,
        qkv_weight,
        qv_bias,
        dense_weight,
        dense_bias,
        up_weight,
        up_bias,
        down_weight,
        down_bias,
        mixer_scale_factor,
        mixer_offset_term,
        perceptron_scale_factor,
        perceptron_offset_term,
    )
    if route is linked:
        parameter_slopes, news, moments_one, moments_two = update_call(
            params, parameter_slopes, firsts, seconds
        )
        return (
            block_out,
            entering_activation_slope,
            *parameter_slopes,
            *news,
            *moments_one,
            *moments_two,
        )
    results = []
    for index in range(12):
        matrix = index in (0, 2, 4, 6)
        results.append(
            adamw(
                params[index],
                parameter_slopes[index],
                firsts[index],
                seconds[index],
                0.01 if matrix else 0.1,
                0.1 if matrix else 0.0,
            )
        )
    news = [r[0] for r in results]
    moments_one = [r[1] for r in results]
    moments_two = [r[2] for r in results]
    return (
        block_out,
        entering_activation_slope,
        *parameter_slopes,
        *news,
        *moments_one,
        *moments_two,
    )


def solution(mesh):
    in_specs = (
        P(("dp", "tensor"), None),
        P("dp", None),
        P(("dp", "tensor"), None),
        P("dp", "tensor"),
        P("tensor"),
        P("tensor", "dp"),
        P(),
        P("dp", "tensor"),
        P("tensor"),
        P("tensor", "dp"),
        P(),
        P(),
        P(),
        P(),
        P(),
        P("dp", "tensor"),
        P("tensor"),
        P("tensor", "dp"),
        P(),
        P("dp", "tensor"),
        P("tensor"),
        P("tensor", "dp"),
        P(),
        P(),
        P(),
        P(),
        P(),
        P("dp", "tensor"),
        P("tensor"),
        P("tensor", "dp"),
        P(),
        P("dp", "tensor"),
        P("tensor"),
        P("tensor", "dp"),
        P(),
        P(),
        P(),
        P(),
        P(),
    )
    out_specs = (
        P(("dp", "tensor"), None),
        P(("dp", "tensor"), None),
        P("dp", "tensor"),
        P("tensor"),
        P("tensor", "dp"),
        P(),
        P("dp", "tensor"),
        P("tensor"),
        P("tensor", "dp"),
        P(),
        P(),
        P(),
        P(),
        P(),
        P("dp", "tensor"),
        P("tensor"),
        P("tensor", "dp"),
        P(),
        P("dp", "tensor"),
        P("tensor"),
        P("tensor", "dp"),
        P(),
        P(),
        P(),
        P(),
        P(),
        P("dp", "tensor"),
        P("tensor"),
        P("tensor", "dp"),
        P(),
        P("dp", "tensor"),
        P("tensor"),
        P("tensor", "dp"),
        P(),
        P(),
        P(),
        P(),
        P(),
        P("dp", "tensor"),
        P("tensor"),
        P("tensor", "dp"),
        P(),
        P("dp", "tensor"),
        P("tensor"),
        P("tensor", "dp"),
        P(),
        P(),
        P(),
        P(),
        P(),
    )
    return jax.shard_map(local, mesh=mesh, in_specs=in_specs, out_specs=out_specs, check_vma=False)
```

```python
import functools

import jax
import jax.numpy as jnp
from jax import lax
from jax.experimental import pallas as pl
from jax.experimental.pallas import tpu as pltpu
from jax.sharding import PartitionSpec as P

D = 1024
FOCUS_COUNT = 16
FF = 4096
ADAM_STEP = 4
HEAD_DIM = 64
MAX_SPAN = 512


beta_first = 0.9
beta_second = 0.95


def standardise_features(values, elementwise_multiplier, additive_offset):
    feature_midpoint = jnp.mean(values, axis=-1, keepdims=True)
    demeaned_entries = values - feature_midpoint
    reciprocal_spread = lax.rsqrt(
        jnp.mean(demeaned_entries * demeaned_entries, axis=-1, keepdims=True) + 1e-05
    )
    unit_spread_entries = demeaned_entries * reciprocal_spread
    return (
        (unit_spread_entries * elementwise_multiplier + additive_offset).astype(jnp.bfloat16),
        unit_spread_entries,
        reciprocal_spread,
    )


def standardise_features_reverse(
    loss_slope, unit_spread_entries, reciprocal_spread, elementwise_multiplier
):
    multiplied_entries = loss_slope * elementwise_multiplier
    return reciprocal_spread * (
        multiplied_entries
        - jnp.mean(multiplied_entries, axis=-1, keepdims=True)
        - unit_spread_entries
        * jnp.mean(multiplied_entries * unit_spread_entries, axis=-1, keepdims=True)
    )


def gelu_parts(pre):
    inner = 0.7978845608 * (pre + 0.044715 * pre * pre * pre)
    tanh_val = jnp.tanh(inner)
    value = 0.5 * pre * (1.0 + tanh_val)
    slope = 0.5 * (1.0 + tanh_val) + 0.5 * pre * (1.0 - tanh_val * tanh_val) * 0.7978845608 * (
        1.0 + 3.0 * 0.044715 * pre * pre
    )
    return (value, slope)


def inner_rows(left, right):
    return lax.dot_general(
        left, right, (((0,), (0,)), ((), ())), preferred_element_type=jnp.float32
    )


def times_transposed(left, right):
    return lax.dot_general(
        left, right, (((1,), (1,)), ((), ())), preferred_element_type=jnp.float32
    )


def head_slopes(first, count):
    index = (first + jnp.arange(count)).astype(jnp.float32)
    return jnp.exp2(-8.0 * (index + 1.0) / FOCUS_COUNT)


def full_bias(qv_bias, heads):
    pair = qv_bias.reshape(heads, 2, HEAD_DIM)
    return jnp.stack([pair[:, 0], jnp.zeros_like(pair[:, 0]), pair[:, 1]], axis=1).reshape(
        heads * 3 * HEAD_DIM
    )


def window(start, block, length):
    return (max(0, start - MAX_SPAN), min(length, start + block))


def fill_offsets(offsets, rows_seg, cols_seg, rows_first, length, block):
    for start in range(0, length, block):
        low, high = window(start, block, length)
        shape = (block, high - low) if rows_first else (high - low, block)
        axis = 0 if rows_first else 1
        row = start + lax.broadcasted_iota(jnp.int32, shape, axis)
        col = low + lax.broadcasted_iota(jnp.int32, shape, 1 - axis)
        if rows_first:
            same = rows_seg[start : start + block, :] == cols_seg[:, low:high]
        else:
            same = rows_seg[low:high, :] == cols_seg[:, start : start + block]
        allowed = (col <= row) & same
        value = jnp.where(allowed, (col - row).astype(jnp.float32), -1e30)
        if rows_first:
            offsets[start : start + block, 0 : high - low] = value
        else:
            offsets[0 : high - low, start : start + block] = value


def forward_kernel(block, slopes, x, rows_seg, cols_seg, out, offsets):
    length = x.shape[0]
    step = pl.program_id(0)

    @pl.when(step == 0)
    def _():
        fill_offsets(offsets, rows_seg, cols_seg, True, length, block)

    for i in range(2):
        base = 3 * HEAD_DIM * i
        slope = slopes[2 * step + i]
        query = x[:, base : base + HEAD_DIM] * HEAD_DIM ** (-0.5)
        keys = x[:, base + HEAD_DIM : base + 2 * HEAD_DIM]
        values = x[:, base + 2 * HEAD_DIM : base + 3 * HEAD_DIM]
        for start in range(0, length, block):
            low, high = window(start, block, length)
            scores = (
                times_transposed(query[start : start + block], keys[low:high])
                + slope * offsets[start : start + block, 0 : high - low]
            )
            peak = jnp.max(scores, axis=1, keepdims=True)
            raised = jnp.exp(scores - peak)
            total = jnp.sum(raised, axis=1, keepdims=True)
            probs = (raised * (1.0 / total)).astype(jnp.bfloat16)
            context = jnp.dot(probs, values[low:high], preferred_element_type=jnp.float32)
            out[start : start + block, HEAD_DIM * i : HEAD_DIM * (i + 1)] = context.astype(
                jnp.bfloat16
            )


def backward_kernel(
    block, slopes, x, grad, rows_seg, cols_seg, out, sums, offsets, dkeys, dvalues, dquery,
    compact=False,
):
    length = x.shape[0]
    step = pl.program_id(0)
    scale = HEAD_DIM ** (-0.5)

    @pl.when(step == 0)
    def _():
        fill_offsets(offsets, rows_seg, cols_seg, False, length, block)

    for i in range(2):
        base = 3 * HEAD_DIM * i
        slope = slopes[2 * step + i]
        query = x[:, base : base + HEAD_DIM] * scale
        keys = x[:, base + HEAD_DIM : base + 2 * HEAD_DIM]
        values = x[:, base + 2 * HEAD_DIM : base + 3 * HEAD_DIM]
        slopes_out = grad[:, HEAD_DIM * i : HEAD_DIM * (i + 1)]
        dkeys[...] = jnp.zeros_like(dkeys)
        dvalues[...] = jnp.zeros_like(dvalues)
        for start in range(0, length, block):
            low, high = window(start, block, length)
            query_block = query[start : start + block]
            grad_block = slopes_out[start : start + block]
            scores = (
                times_transposed(keys[low:high], query_block)
                + slope * offsets[0 : high - low, start : start + block]
            )
            peak = jnp.max(scores, axis=0, keepdims=True)
            raised = jnp.exp(scores - peak)
            total = jnp.sum(raised, axis=0, keepdims=True)
            probs = raised * (1.0 / total)
            dprob = times_transposed(values[low:high], grad_block)
            delta = jnp.sum(probs * dprob, axis=0, keepdims=True)
            dscore = (probs * (dprob - delta)).astype(jnp.bfloat16)
            dvalues[low:high, :] += jnp.dot(
                probs.astype(jnp.bfloat16), grad_block, preferred_element_type=jnp.float32
            )
            dkeys[low:high, :] += jnp.dot(dscore, query_block, preferred_element_type=jnp.float32)
            dquery[start : start + block, :] = inner_rows(dscore, keys[low:high]) * scale
        for place, part in enumerate((dquery, dkeys, dvalues)):
            first = base + HEAD_DIM * place
            out[:, first : first + HEAD_DIM] = part[...].astype(jnp.bfloat16)
            if compact and place == 1:
                continue
            if compact:
                first = HEAD_DIM * (2 * i + place // 2)
            sums[:, first : first + HEAD_DIM] = jnp.sum(part[...], axis=0, keepdims=True)


def attention_forward(qkv, segments, slopes):
    length, width = qkv.shape
    pairs = width // (6 * HEAD_DIM)
    block = min(256, length)
    span = min(length, block + MAX_SPAN)
    return pl.pallas_call(
        functools.partial(forward_kernel, block),
        grid=(pairs,),
        out_shape=jax.ShapeDtypeStruct((length, width // 3), jnp.bfloat16),
        in_specs=[
            pl.BlockSpec(memory_space=pltpu.SMEM),
            pl.BlockSpec((length, 6 * HEAD_DIM), lambda p: (0, p)),
            pl.BlockSpec((length, 1), lambda p: (0, 0)),
            pl.BlockSpec((1, length), lambda p: (0, 0)),
        ],
        out_specs=pl.BlockSpec((length, 2 * HEAD_DIM), lambda p: (0, p)),
        scratch_shapes=[pltpu.VMEM((length, span), jnp.float32)],
        cost_estimate=pl.CostEstimate(
            flops=4 * length * span * width // 3,
            bytes_accessed=8 * length * width // 3,
            transcendentals=length * span * pairs * 2,
        ),
        compiler_params=pltpu.CompilerParams(vmem_limit_bytes=40 * 1024 * 1024),
        name="attention_forward",
    )(slopes, qkv, segments[:, None], segments[None, :])


def attention_backward(qkv, segments, slopes, dcontext):
    length, width = qkv.shape
    pairs = width // (6 * HEAD_DIM)
    block = min(256, length)
    span = min(length, block + MAX_SPAN)
    return pl.pallas_call(
        functools.partial(backward_kernel, block),
        grid=(pairs,),
        out_shape=(
            jax.ShapeDtypeStruct((length, width), jnp.bfloat16),
            jax.ShapeDtypeStruct((1, width), jnp.float32),
        ),
        in_specs=[
            pl.BlockSpec(memory_space=pltpu.SMEM),
            pl.BlockSpec((length, 6 * HEAD_DIM), lambda p: (0, p)),
            pl.BlockSpec((length, 2 * HEAD_DIM), lambda p: (0, p)),
            pl.BlockSpec((length, 1), lambda p: (0, 0)),
            pl.BlockSpec((1, length), lambda p: (0, 0)),
        ],
        out_specs=(
            pl.BlockSpec((length, 6 * HEAD_DIM), lambda p: (0, p)),
            pl.BlockSpec((1, 6 * HEAD_DIM), lambda p: (0, p)),
        ),
        scratch_shapes=[
            pltpu.VMEM((span, length), jnp.float32),
            pltpu.VMEM((length, HEAD_DIM), jnp.float32),
            pltpu.VMEM((length, HEAD_DIM), jnp.float32),
            pltpu.VMEM((length, HEAD_DIM), jnp.float32),
        ],
        cost_estimate=pl.CostEstimate(
            flops=10 * length * span * width // 3,
            bytes_accessed=14 * length * width // 3,
            transcendentals=length * span * pairs * 2,
        ),
        compiler_params=pltpu.CompilerParams(vmem_limit_bytes=40 * 1024 * 1024),
        name="attention_backward",
    )(slopes, qkv, dcontext, segments[:, None], segments[None, :])


def swap(values):
    return lax.ppermute(values, "tensor", [(0, 1), (1, 0)])


def spread(values, count):
    if count == 2:
        return [values, swap(values)]
    return [lax.all_gather(values, "tensor", axis=0, tiled=True)]


def fold(parts, count):
    if count == 2:
        return swap(parts[1]).astype(jnp.float32) + parts[0].astype(jnp.float32)
    return lax.psum_scatter(parts[0], "tensor", scatter_dimension=0, tiled=True).astype(
        jnp.float32
    )


def to_order(parts, rank):
    if len(parts) == 2:
        own, other = parts
        return jnp.concatenate(
            [jnp.where(rank == 0, own, other), jnp.where(rank == 0, other, own)], axis=0
        )
    return parts[0]


def from_order(values, rank, count):
    if count == 2:
        half = values.shape[0] // 2
        return [
            lax.dynamic_slice_in_dim(values, rank * half, half, 0),
            lax.dynamic_slice_in_dim(values, (1 - rank) * half, half, 0),
        ]
    return [values]


def product(left, right):
    return jnp.dot(left, right, preferred_element_type=jnp.float32)


def add_up(lefts, rights):
    total = inner_rows(lefts[0], rights[0])
    for left, right in zip(lefts[1:], rights[1:]):
        total = total + inner_rows(left, right)
    return total


def total_over_all(vector, shared, rank):
    rows = lax.all_gather(vector[None], ("dp", "tensor"), axis=0, tiled=True)
    everyone = jnp.sum(rows[:, :shared], axis=0)
    count = lax.axis_size("tensor")
    split = rows[:, shared:].reshape(rows.shape[0] // count, count, -1)
    mine = lax.dynamic_index_in_dim(jnp.sum(split, axis=0), rank, 0, keepdims=False)
    return everyone, mine


def adamw(param, loss_slope, first, second, rate, decay):
    first_new = beta_first * first + (1.0 - beta_first) * loss_slope
    second_new = beta_second * second + (1.0 - beta_second) * loss_slope * loss_slope
    update = (
        first_new
        / (1.0 - beta_first**ADAM_STEP)
        / (jnp.sqrt(second_new / (1.0 - beta_second**ADAM_STEP)) + 1e-08)
    )
    return (param - rate * (update + decay * param), first_new, second_new)


MESH = pl.DeviceIdType.MESH
CHUNK = 64
MIB = 1024 * 1024


class Spot:
    def __init__(self, depth):
        dp = lax.axis_index("dp")
        self.depth = depth
        self.t = lax.axis_index("tensor")
        self.c = lax.rem(dp, 2)
        self.x = lax.rem(lax.div(dp, 2), 2)
        self.z = lax.div(dp, 4)
        self.twin = self.at(self.z, self.x, 1 - self.c)
        self.cross = self.at(self.z, 1 - self.x, self.c)
        self.pair = (dp, 1 - self.t)

    def index(self, z, x, c):
        return (z * 2 + x) * 2 + c

    def at(self, z, x, c):
        return (self.index(z, x, c), self.t)

    def farthest(self, i):
        n = self.depth
        if i == n - 1:
            return self.z
        down = jnp.where(n - 1 - i > self.z, n - 1 - i, n - 2 - i)
        up = jnp.where(i < self.z, i, i + 1)
        return jnp.where(2 * self.z < n, down, up)

    def greet(self, everyone=True):
        barrier = pltpu.get_barrier_semaphore()
        others = [self.twin, self.cross, self.pair] if everyone else [self.pair]
        for step in range(1, self.depth if everyone else 1):
            others.append(self.at(lax.rem(self.z + step, self.depth), self.x, self.c))
        for other in others:
            pl.semaphore_signal(barrier, inc=1, device_id=other, device_id_type=MESH)
        pl.semaphore_wait(barrier, len(others))


def push(source, target, send, arrive, to):
    return pltpu.make_async_remote_copy(
        src_ref=source,
        dst_ref=target,
        send_sem=send,
        recv_sem=arrive,
        device_id=to,
        device_id_type=MESH,
    )


def rows_of(ref, first, size):
    return ref.at[pl.ds(pl.multiple_of(first, size), size)]


class Gather:
    def __init__(self, spot, shards, fulls, zs, zr, xs, xr, cs, cr, ls):
        self.spot, self.shards, self.fulls = spot, shards, fulls
        self.zs, self.zr, self.xs, self.xr, self.cs, self.cr, self.ls = zs, zr, xs, xr, cs, cr, ls
        self.count = len(shards)

    @staticmethod
    def semaphores(count, depth):
        dma = pltpu.SemaphoreType.DMA
        return [
            dma((count, depth, 2)),
            dma((count, depth)),
            dma((count, depth)),
            dma((count, depth)),
            dma((count, 2 * depth)),
            dma((count, 2 * depth)),
            dma((count,)),
        ]

    def block(self, a, z, x, c):
        size = self.shards[a].shape[0]
        return rows_of(self.fulls[a], self.spot.index(z, x, c) * size, size)

    def along(self, a, bz, way, own=False):
        s = self.spot
        region = self.block(a, bz, s.x, s.c)
        to = s.at(s.z + (1 if way == 0 else -1), s.x, s.c)
        return push(
            self.shards[a] if own else region, region, self.zs.at[a, bz, way], self.zr.at[a, bz], to
        )

    def over(self, a, bz, own=False):
        s = self.spot
        region = self.block(a, bz, s.x, s.c)
        return push(
            self.shards[a] if own else region, region, self.xs.at[a, bz], self.xr.at[a, bz], s.cross
        )

    def across(self, a, bz, bx, own=False):
        s = self.spot
        region = self.block(a, bz, bx, s.c)
        k = bz * 2 + bx
        return push(
            self.shards[a] if own else region, region, self.cs.at[a, k], self.cr.at[a, k], s.twin
        )

    def keep(self, a):
        s = self.spot
        return pltpu.make_async_copy(
            self.shards[a], self.block(a, s.z, s.x, s.c), self.ls.at[a]
        )

    def start(self):
        s = self.spot
        for a in range(self.count):
            pl.when(s.z + 1 < s.depth)(lambda a=a: self.along(a, s.z, 0, True).start())
            pl.when(s.z > 0)(lambda a=a: self.along(a, s.z, 1, True).start())
            self.over(a, s.z, True).start()
        for a in range(self.count):
            self.across(a, s.z, s.x, True).start()
            self.keep(a).start()

    def z_step(self, a, step):
        s = self.spot
        for way in (0, 1):
            bz = s.z - step if way == 0 else s.z + step
            here = bz >= 0 if way == 0 else bz < s.depth
            onward = s.z + 1 < s.depth if way == 0 else s.z > 0

            @pl.when(here)
            def _():
                self.along(a, bz, way).wait_recv()
                pl.when(onward)(lambda: self.along(a, bz, way).start())
                self.over(a, bz).start()
                self.across(a, bz, s.x).start()

    def x_step(self, a, step):
        s = self.spot

        def take(bz):
            self.over(a, bz).wait_recv()
            self.across(a, bz, 1 - s.x).start()

        if step == 0:
            take(s.z)
            return
        pl.when(s.z - step >= 0)(lambda: take(s.z - step))
        pl.when(s.z + step < s.depth)(lambda: take(s.z + step))

    def finish(self):
        s = self.spot
        for a in range(self.count):
            self.keep(a).wait()
            for bz in range(s.depth):
                for bx in range(2):
                    self.across(a, bz, bx).wait()
                self.over(a, bz).wait_send()
                pl.when((bz <= s.z) & (s.z + 1 < s.depth))(
                    lambda a=a, bz=bz: self.along(a, bz, 0).wait_send()
                )
                pl.when((bz >= s.z) & (s.z > 0))(
                    lambda a=a, bz=bz: self.along(a, bz, 1).wait_send()
                )


STRIP = 16
BAND = 64


def strips(size, step, body):
    def one(i, carry):
        body(pl.multiple_of(i * step, step))
        return carry

    lax.fori_loop(0, size // step, one, 0)


class Scatter:
    def __init__(self, spot, grads, sums, cins, xins, zins, cs, cr, xs, xr, zs, zr):
        self.spot, self.grads, self.sums = spot, grads, sums
        self.cins, self.xins, self.zins = cins, xins, zins
        self.cs, self.cr, self.xs, self.xr, self.zs, self.zr = cs, cr, xs, xr, zs, zr
        self.count = len(grads)

    @staticmethod
    def scratch(shapes, depth):
        count, low = len(shapes), jnp.bfloat16
        dma = pltpu.SemaphoreType.DMA
        buffers = []
        for slots in (2 * depth, depth, depth):
            for rows, width in shapes:
                buffers.append(pltpu.VMEM((slots, rows, width), low))
        return buffers + [
            dma((count, 2 * depth)),
            dma((count, 2 * depth)),
            dma((count, depth)),
            dma((count, depth)),
            dma((count, depth)),
            dma((count, depth)),
        ]

    def first(self, a, z, x, c):
        return self.spot.index(z, x, c) * self.sums[a].shape[0]

    def across(self, a, bz, bx):
        s = self.spot
        k = bz * 2 + bx
        return push(
            rows_of(self.grads[a], self.first(a, bz, bx, 1 - s.c), self.sums[a].shape[0]),
            self.cins[a].at[k],
            self.cs.at[a, k],
            self.cr.at[a, k],
            s.twin,
        )

    def over(self, a, bz):
        s = self.spot
        return push(
            self.cins[a].at[bz * 2 + 1 - s.x],
            self.xins[a].at[bz],
            self.xs.at[a, bz],
            self.xr.at[a, bz],
            s.cross,
        )

    def along(self, a, bz, arriving=False):
        s = self.spot
        slot = bz if arriving else s.z
        return push(
            self.cins[a].at[bz * 2 + s.x],
            self.zins[a].at[slot],
            self.zs.at[a, bz],
            self.zr.at[a, slot],
            s.at(bz, s.x, s.c),
        )

    def start(self, a):
        s = self.spot
        for bx in (1 - s.x, s.x):
            for i in range(s.depth):
                self.across(a, s.farthest(i), bx).start()

    def own(self, a, bz, bx, r):
        here = pl.multiple_of(self.first(a, bz, bx, self.spot.c) + r, STRIP)
        return self.grads[a][pl.ds(here, STRIP), :].astype(jnp.float32)

    def c_step(self, a, i):
        s = self.spot
        bz = s.farthest(i)
        k = bz * 2 + 1 - s.x
        self.across(a, bz, 1 - s.x).wait_recv()
        cin = self.cins[a]

        def add(r):
            part = pl.ds(r, STRIP)
            total = self.own(a, bz, 1 - s.x, r) + cin[k, part, :].astype(jnp.float32)
            cin[k, part, :] = total.astype(jnp.bfloat16)

        strips(cin.shape[1], STRIP, add)
        self.over(a, bz).start()

    def x_step(self, a, i):
        s = self.spot
        bz = s.farthest(i)
        k = bz * 2 + s.x
        self.across(a, bz, s.x).wait_recv()
        self.over(a, bz).wait_recv()
        cin, xin, out = self.cins[a], self.xins[a], self.sums[a]

        def add(r):
            part = pl.ds(r, STRIP)
            total = (
                self.own(a, bz, s.x, r)
                + cin[k, part, :].astype(jnp.float32)
                + xin[bz, part, :].astype(jnp.float32)
            )
            if i < s.depth - 1:
                cin[k, part, :] = total.astype(jnp.bfloat16)
            else:
                out[part, :] = total

        strips(cin.shape[1], STRIP, add)
        if i < s.depth - 1:
            self.along(a, bz).start()

    def last_step(self, a):
        s = self.spot
        zin, out = self.zins[a], self.sums[a]
        slots = [lax.rem(s.z + step, s.depth) for step in range(1, s.depth)]
        for slot in slots:
            self.along(a, slot, True).wait_recv()

        def add(r):
            part = pl.ds(r, STRIP)
            total = out[part, :]
            for slot in slots:
                total = total + zin[slot, part, :].astype(jnp.float32)
            out[part, :] = total

        strips(out.shape[0], STRIP, add)

    def finish(self):
        s = self.spot
        for a in range(self.count):
            for i in range(s.depth):
                bz = s.farthest(i)
                for bx in range(2):
                    self.across(a, bz, bx).wait_send()
                self.over(a, bz).wait_send()
                if i < s.depth - 1:
                    self.along(a, bz).wait_send()


class Totals:
    def __init__(self, spot, stage, inbox, send, arrive, shared):
        self.spot, self.stage, self.inbox, self.send, self.arrive, self.shared = (
            spot, stage, inbox, send, arrive, shared,
        )

    @staticmethod
    def scratch(shape, depth):
        dma = pltpu.SemaphoreType.DMA
        return [
            pltpu.VMEM((4, *shape), jnp.float32),
            pltpu.VMEM((3 + depth, *shape), jnp.float32),
            dma((3 + depth,)),
            dma((3 + depth,)),
        ]

    def hop(self, number):
        to = (self.spot.twin, self.spot.cross)[number]
        return push(
            self.stage.at[number], self.inbox.at[number], self.send.at[number], self.arrive.at[number], to
        )

    def along(self, z, arriving=False):
        s = self.spot
        slot = 2 + (z if arriving else s.z)
        return push(
            self.stage.at[2], self.inbox.at[slot], self.send.at[2 + z], self.arrive.at[slot], s.at(z, s.x, s.c)
        )

    def pair(self):
        last = 2 + self.spot.depth
        part = pl.ds(0, self.shared)
        return push(
            self.stage.at[3, part], self.inbox.at[last, part], self.send.at[last], self.arrive.at[last], self.spot.pair
        )

    def others(self):
        s = self.spot
        return [lax.rem(s.z + step, s.depth) for step in range(1, s.depth)]

    def step(self, number):
        s = self.spot
        if number == 0:
            self.hop(0).start()
        elif number < 3:
            self.hop(number - 1).wait_recv()
            self.stage[number] = self.stage[number - 1] + self.inbox[number - 1]
            if number == 1:
                self.hop(1).start()
            else:
                for z in self.others():
                    self.along(z).start()
                self.inbox[2 + s.z] = self.stage[2]
        elif number == 3:
            for z in self.others():
                self.along(z, True).wait_recv()
            total = self.inbox[2]
            for z in range(1, s.depth):
                total = total + self.inbox[2 + z]
            self.stage[3] = total
            self.pair().start()
        else:
            self.pair().wait_recv()

    def result(self):
        part = slice(0, self.shared)
        return self.stage[3, part, :] + self.inbox[2 + self.spot.depth, part, :]

    def finish(self):
        self.hop(0).wait_send()
        self.hop(1).wait_send()
        for z in self.others():
            self.along(z).wait_send()
        self.pair().wait_send()


class Swap:
    def __init__(self, spot, source, target, send, arrive):
        self.spot, self.source, self.target, self.send, self.arrive = (
            spot,
            source,
            target,
            send,
            arrive,
        )

    def chunk(self, i, source_first=0, target_first=0):
        return push(
            rows_of(self.source, source_first + i * CHUNK, CHUNK),
            rows_of(self.target, target_first + i * CHUNK, CHUNK),
            self.send.at[i],
            self.arrive.at[i],
            self.spot.pair,
        )


def loop(first, last, body):
    def one(i, carry):
        body(i)
        return carry

    lax.fori_loop(first, last, one, 0)


def cast_into(source, target, start=0):
    def one(r):
        part = pl.ds(r, STRIP)
        target[part, :] = source[part, start : start + target.shape[1]].astype(target.dtype)

    strips(source.shape[0], STRIP, one)


def spread_kernel(depth, x, gain, shift, wide0, wide1, normed, full0, full1, own, low0, low1, ys, yr, yl, *sems):
    spot = Spot(depth)
    half = x.shape[0]
    base = spot.t * half
    cast_into(wide0, low0)
    cast_into(wide1, low1)
    spot.greet()
    gather = Gather(spot, (low0, low1), (full0, full1), *sems)
    gather.start()
    swap = Swap(spot, own, normed, ys, yr)

    def keep(i):
        return pltpu.make_async_copy(
            rows_of(own, i * CHUNK, CHUNK), rows_of(normed, base + i * CHUNK, CHUNK), yl.at[i]
        )

    def work(i):
        def one(r):
            part = pl.ds(i * CHUNK + r, BAND)
            own[part, :] = standardise_features(x[part, :], gain[...], shift[...])[0]

        strips(CHUNK, BAND, one)
        swap.chunk(i, 0, base).start()
        keep(i).start()

    loop(0, half // CHUNK, work)
    for step in range(1, depth):
        for a in range(2):
            gather.z_step(a, step)
        for a in range(2):
            gather.x_step(a, step - 1)
    for a in range(2):
        gather.x_step(a, depth - 1)

    def done(i):
        keep(i).wait()
        swap.chunk(i, 0, base).wait_send()
        swap.chunk(i, 0, half - base).wait_recv()

    loop(0, half // CHUNK, done)
    gather.finish()


def fold_rows(values):
    return jnp.sum(values.reshape(-1, 8, values.shape[-1]), axis=0)


def core_kernel(depth, part, x, bias, gain, shift, slope, other, shard, shard2, down_part, up_bias, resid, dresid, low, gup, contracted, sum0, sums, ups, up, shard_low, down, shard2_low, dk, gdown, twos, outs, act, dpre, twos_t, outs_t, normed, own, inbox, inbox2, totals, ps, pr, ys, yr, ns, nr, ls, lr, lk, *rest):
    spot = Spot(depth)
    half, model = x.shape
    hidden = down.shape[1]
    width = min(512, hidden)
    side = min(256, half)
    blocks = hidden // width
    base = pl.multiple_of(spot.t * half, half)
    away = pl.multiple_of(half - base, half)
    chunks = half // CHUNK
    cut = hidden // 2
    cast_into(shard, shard_low)
    cast_into(shard2, shard2_low, cut)
    spot.greet()
    near = pltpu.make_async_copy(down_part, down.at[:, pl.ds(0, cut)], dk)
    near.start()
    gather = Gather(
        spot, (shard_low, shard2_low), (up, down.at[:, pl.ds(cut, cut)]), *rest[9:]
    )
    first = Swap(spot, part, inbox, ps, pr)
    second = Swap(spot, twos, twos, ys, yr)
    third = Swap(spot, normed, inbox2, ns, nr)
    fourth = Swap(spot, own, low, ls, lr)
    loop(0, chunks, lambda i: first.chunk(i, away, 0).start())
    gather.start()

    def place(i):
        here = pl.ds(pl.multiple_of(base + i * side, side), side)
        there = pl.ds(pl.multiple_of(away + i * side, side), side)
        piece = pl.ds(pl.multiple_of(i * side, side), side)
        outs[here, :] = slope[piece, :].astype(jnp.bfloat16)
        outs[there, :] = other[piece, :]
        outs_t[:, here] = outs[here, :].T
        outs_t[:, there] = outs[there, :].T

    loop(0, half // side, place)

    def enter(i):
        first.chunk(i, away, 0).wait_recv()

        def one(r):
            here = pl.ds(i * CHUNK + r, BAND)
            there = pl.ds(pl.multiple_of(base + i * CHUNK + r, BAND), BAND)
            total = (
                x[here, :]
                + (inbox[here, :].astype(jnp.float32) + part[there, :].astype(jnp.float32))
                + bias[...]
            )
            resid[here, :] = total
            twos[there, :] = standardise_features(total, gain[...], shift[...])[0]

        strips(CHUNK, BAND, one)
        second.chunk(i, base, base).start()

    todo = []
    for step in range(depth):
        if step + 1 < depth:
            todo.append((gather.z_step, step + 1))
        todo.append((gather.x_step, step))
    for i in range(chunks):
        enter(i)
        if i > 0 and todo:
            act_on, step = todo.pop(0)
            act_on(0, step)
            act_on(1, step)
    for act_on, step in todo:
        act_on(0, step)
        act_on(1, step)
    gather.finish()
    near.wait()

    def forward(start, again):
        here = pl.ds(start, half)
        twos_t[:, here] = twos[here, :].T

        def block(n):
            cols = pl.ds(pl.multiple_of(n * width, width), width)
            pre = product(twos[here, :], up[:, cols]) + up_bias[:, cols]
            square = pre * pre
            inner = 0.7978845608 * pre * (1.0 + 0.044715 * square)
            gate = 0.5 + 0.5 * jnp.tanh(inner)
            value = pre * gate
            act[here, cols] = value.astype(jnp.bfloat16)
            tilt = gate + value * (1.0 - gate) * (
                2.0 * 0.7978845608 + (6.0 * 0.7978845608 * 0.044715) * square
            )
            grad = product(outs[here, :], down[:, cols]) * tilt
            dpre[here, cols] = grad.astype(jnp.bfloat16)
            total = jnp.sum(fold_rows(grad), axis=0, keepdims=True)
            ups[:, cols] = ups[:, cols] + total if again else total

        loop(0, blocks, block)

    def contract(start, target):
        def one(i):
            here = pl.ds(pl.multiple_of(start + i * side, side), side)
            there = pl.ds(pl.multiple_of(target + i * side, side), side)
            contracted[there, :] = times_transposed(act[here, :], down[...]).astype(
                jnp.bfloat16
            )

        loop(0, half // side, one)

    def reduce_norm(i, start):
        here = pl.ds(pl.multiple_of(start + i * side, side), side)
        normed[here, :] = times_transposed(dpre[here, :], up[...]).astype(jnp.bfloat16)

    forward(base, False)
    contract(base, 0)
    loop(0, chunks, lambda i: second.chunk(i, away, away).wait_recv())
    forward(away, True)

    def send_norm(i):
        reduce_norm(i, away)
        for j in range(side // CHUNK):
            third.chunk(i * (side // CHUNK) + j, away, 0).start()

    loop(0, half // side, send_norm)
    loop(0, half // side, lambda i: reduce_norm(i, base))

    def weights(target, left, right):
        def one(n):
            cols = pl.ds(pl.multiple_of(n * width, width), width)
            target[:, cols] = product(left[...], right[:, cols]).astype(jnp.bfloat16)

        loop(0, blocks, one)

    weights(gdown, outs_t, act)
    scatter = Scatter(spot, (gdown,), (sum0,), rest[0:1], rest[1:2], rest[2:3], *rest[3:9])
    scatter.start(0)
    totals[...] = jnp.zeros_like(totals)
    weights(gup, twos_t, dpre)
    for i in range(depth):
        scatter.c_step(0, i)

    def keep(i):
        return pltpu.make_async_copy(
            rows_of(own, i * CHUNK, CHUNK), rows_of(low, base + i * CHUNK, CHUNK), lk.at[i]
        )

    def leave(i):
        third.chunk(i, away, 0).wait_recv()

        def one(r):
            here = pl.ds(i * CHUNK + r, BAND)
            there = pl.ds(pl.multiple_of(base + i * CHUNK + r, BAND), BAND)
            grad = inbox2[here, :].astype(jnp.float32) + normed[there, :].astype(jnp.float32)
            values = resid[here, :]
            centred = values - jnp.mean(values, axis=-1, keepdims=True)
            spread = lax.rsqrt(jnp.mean(centred * centred, axis=-1, keepdims=True) + 1e-05)
            unit = centred * spread
            out = slope[here, :]
            total = out + standardise_features_reverse(grad, unit, spread, gain[...])
            dresid[here, :] = total
            own[here, :] = total.astype(jnp.bfloat16)
            for spot_in, term in enumerate((total, out, grad * unit, grad)):
                totals[spot_in] += fold_rows(term)

        strips(CHUNK, BAND, one)
        fourth.chunk(i, 0, base).start()
        keep(i).start()

    loop(0, chunks, leave)
    contract(away, half)
    for i in range(depth):
        scatter.x_step(0, i)
    sums[...] = jnp.zeros_like(sums)
    for number in range(4):
        sums[number : number + 1, :] = jnp.sum(totals[number], axis=0, keepdims=True)
    scatter.last_step(0)

    def done(i):
        keep(i).wait()
        first.chunk(i, away, 0).wait_send()
        second.chunk(i, base, base).wait_send()
        third.chunk(i, away, 0).wait_send()
        fourth.chunk(i, 0, base).wait_send()
        fourth.chunk(i, 0, away).wait_recv()

    loop(0, chunks, done)
    scatter.finish()


def leave_kernel(depth, ones, dqkv, low, dresid, x, gain, early, ups, qv, grad_dense, slope, sum0, sum1, vector, ups_sum, qv_sum, grad, ones_t, part, inbox, totals, ps, pr, *rest):
    spot = Spot(depth)
    half = x.shape[0]
    base = pl.multiple_of(spot.t * half, half)
    away = pl.multiple_of(half - base, half)
    first = Swap(spot, part, inbox, ps, pr)
    chunks = half // CHUNK
    side = min(256, half)
    width = min(512, dqkv.shape[1])

    def turn(i):
        here = pl.ds(pl.multiple_of(i * half, half), half)
        ones_t[:, here] = ones[here, :].T

    loop(0, 2, turn)
    spot.greet()
    scatter = Scatter(
        spot, (grad, grad_dense), (sum0, sum1), rest[0:2], rest[2:4], rest[4:6], *rest[6:12]
    )
    scatter.start(1)

    def weights(n):
        cols = pl.ds(pl.multiple_of(n * width, width), width)
        grad[:, cols] = product(ones_t[...], dqkv[:, cols]).astype(jnp.bfloat16)

    loop(0, dqkv.shape[1] // width, weights)
    scatter.start(0)

    def reduce_norm(i, start):
        here = pl.ds(pl.multiple_of(start + i * side, side), side)
        part[here, :] = times_transposed(dqkv[here, :], low[...]).astype(jnp.bfloat16)

    def send_norm(i):
        reduce_norm(i, away)
        for j in range(side // CHUNK):
            first.chunk(i * (side // CHUNK) + j, away, 0).start()

    loop(0, half // side, send_norm)
    for a in (1, 0):
        for i in range(depth):
            scatter.c_step(a, i)
    loop(0, half // side, lambda i: reduce_norm(i, base))
    model = x.shape[1]
    every = Totals(spot, *rest[12:16], 8)
    totals[...] = jnp.zeros_like(totals)
    every.stage[0] = jnp.zeros_like(every.stage[0])
    every.stage[0, 0:8, :] = early[...]
    row, pieces = 8, []
    for source, target in ((ups, ups_sum), (qv, qv_sum)):
        for start in range(0, source.shape[1], model):
            every.stage[0, row : row + 1, :] = source[:, start : start + model]
            pieces.append((target, start, row))
            row += 1

    def work(i):
        first.chunk(i, half - base, 0).wait_recv()

        def one(r):
            here = pl.ds(i * CHUNK + r, BAND)
            there = pl.ds(pl.multiple_of(base + i * CHUNK + r, BAND), BAND)
            grad = inbox[here, :].astype(jnp.float32) + part[there, :].astype(jnp.float32)
            values = x[here, :]
            centred = values - jnp.mean(values, axis=-1, keepdims=True)
            spread = lax.rsqrt(jnp.mean(centred * centred, axis=-1, keepdims=True) + 1e-05)
            unit = centred * spread
            slope[here, :] = dresid[here, :] + standardise_features_reverse(
                grad, unit, spread, gain[...]
            )
            for place, term in enumerate((grad * unit, grad)):
                totals[place] += fold_rows(term)

        strips(CHUNK, BAND, one)

    todo = [(scatter.x_step, a, i) for i in range(depth) for a in (1, 0)]
    for i in range(chunks):
        work(i)
        if todo:
            act, a, step = todo.pop(0)
            act(a, step)
    for place in range(2):
        every.stage[0, 4 + place : 5 + place, :] = jnp.sum(totals[place], axis=0, keepdims=True)
    every.step(0)
    for act, a, step in todo:
        act(a, step)
    for number in range(1, 4):
        every.step(number)
    for a in range(2):
        scatter.last_step(a)
    every.step(4)
    vector[...] = every.result()
    for target, start, row in pieces:
        target[:, start : start + model] = every.stage[3, row : row + 1, :]
    loop(0, chunks, lambda i: first.chunk(i, half - base, 0).wait_send())
    every.finish()
    scatter.finish()


def vmem(count=1):
    return [pl.BlockSpec(memory_space=pltpu.VMEM)] * count


def anywhere(count=1):
    return [pl.BlockSpec(memory_space=pl.ANY)] * count


def call(body, number, name, depth, outs, in_specs, out_specs, scratch, args, mib=48):
    size = sum(a.size * a.dtype.itemsize for a in args) + sum(
        o.size * jnp.dtype(o.dtype).itemsize for o in outs
    )
    return pl.pallas_call(
        functools.partial(body, depth),
        out_shape=outs,
        in_specs=in_specs,
        out_specs=out_specs,
        scratch_shapes=scratch,
        cost_estimate=pl.CostEstimate(flops=0, bytes_accessed=size, transcendentals=0),
        compiler_params=pltpu.CompilerParams(
            collective_id=number, has_side_effects=True, vmem_limit_bytes=mib * MIB
        ),
        name=name,
    )(*args)


def shaped(shape, dtype=jnp.bfloat16):
    return jax.ShapeDtypeStruct(shape, dtype)


def spread_call(depth, x, gain, shift, shards):
    half, width = x.shape
    dma = pltpu.SemaphoreType.DMA
    chunks = half // CHUNK
    outs = [shaped((2 * half, width))]
    outs += [shaped((4 * depth * s.shape[0], s.shape[1])) for s in shards]
    scratch = [pltpu.VMEM((half, width), jnp.bfloat16)]
    scratch += [pltpu.VMEM(s.shape, jnp.bfloat16) for s in shards]
    scratch += [dma((chunks,))] * 3 + Gather.semaphores(2, depth)
    return call(
        spread_kernel, 0, "spread", depth, outs, vmem(5), anywhere(3), scratch,
        (x, gain[None], shift[None], *shards),
    )


def core_call(depth, part, x, bias, gain, shift, slope, other, shard, shard2, down_part, up_bias):
    half, model = x.shape
    tokens, hidden = 2 * half, shard.shape[1]
    low, full, dma = jnp.bfloat16, jnp.float32, pltpu.SemaphoreType.DMA
    chunks = half // CHUNK
    shapes = [(model // (4 * depth), hidden)]
    outs = [
        shaped((half, model), full),
        shaped((half, model), full),
        shaped((tokens, model)),
        shaped((model, hidden)),
        shaped((tokens, model)),
        shaped(shapes[0], full),
        shaped((8, model), full),
        shaped((1, hidden), full),
    ]
    scratch = [
        pltpu.VMEM((model, hidden), low),
        pltpu.VMEM(shard.shape, low),
        pltpu.VMEM((model, hidden), low),
        pltpu.VMEM((shard.shape[0], hidden // 2), low),
        dma(()),
        pltpu.VMEM((model, hidden), low),
        pltpu.VMEM((tokens, model), low),
        pltpu.VMEM((tokens, model), low),
        pltpu.VMEM((tokens, hidden), low),
        pltpu.VMEM((tokens, hidden), low),
        pltpu.VMEM((model, tokens), low),
        pltpu.VMEM((model, tokens), low),
        pltpu.VMEM((tokens, model), low),
        pltpu.VMEM((half, model), low),
        pltpu.VMEM((half, model), low),
        pltpu.VMEM((half, model), low),
        pltpu.VMEM((4, 8, model), full),
    ]
    scratch += [dma((chunks,))] * 9 + Scatter.scratch(shapes, depth)
    scratch += Gather.semaphores(2, depth)
    return call(
        core_kernel, 1, "core", depth, outs, vmem(9) + anywhere() + vmem(),
        vmem(2) + anywhere() + vmem(5), scratch,
        (part, x, bias[None], gain[None], shift[None], slope, other, shard, shard2, down_part, up_bias[None]),
        60,
    )


def leave_call(depth, ones, dqkv, low, dresid, x, gain, early, ups, qv, grad_dense):
    half, width = x.shape
    dma = pltpu.SemaphoreType.DMA
    chunks = half // CHUNK
    full = jnp.float32
    grads = ((width, dqkv.shape[1]), grad_dense.shape)
    shapes = [(g[0] // (4 * depth), g[1]) for g in grads]
    outs = [shaped((half, width), full)]
    outs += [shaped(s, full) for s in shapes]
    outs += [shaped((8, width), full), shaped(ups.shape, full), shaped(qv.shape, full)]
    scratch = [
        pltpu.VMEM(grads[0], jnp.bfloat16),
        pltpu.VMEM((width, 2 * half), jnp.bfloat16),
        pltpu.VMEM((2 * half, width), jnp.bfloat16),
        pltpu.VMEM((half, width), jnp.bfloat16),
        pltpu.VMEM((2, 8, width), full),
    ]
    scratch += [dma((chunks,))] * 2 + Scatter.scratch(shapes, depth)
    scratch += Totals.scratch((16, width), depth)
    return call(
        leave_kernel, 2, "leave", depth, outs, vmem(10), vmem(6), scratch,
        (ones, dqkv, low, dresid, x, gain[None], early, ups, qv, grad_dense),
    )


def reverse_kernel(
    depth, block, slopes, x, grad, rows_seg, cols_seg, gup, contracted, out, sums, sum0, arrived,
    offsets, dkeys, dvalues, dquery, ds, dr, *rest
):
    step = pl.program_id(0)
    last = pl.num_programs(0) - 1
    spot = Spot(depth)
    chunks, half = arrived.shape[0] // CHUNK, arrived.shape[0]
    swap = Swap(spot, contracted, arrived, ds, dr)
    scatter = Scatter(spot, (gup,), (sum0,), rest[0:1], rest[1:2], rest[2:3], *rest[3:])

    @pl.when(step == 0)
    def _():
        spot.greet()
        scatter.start(0)
        loop(0, chunks, lambda i: swap.chunk(i, half, 0).start())

    backward_kernel(
        block, slopes, x, grad, rows_seg, cols_seg, out, sums, offsets, dkeys, dvalues, dquery, True
    )

    @pl.when(step == 0)
    def _():
        for i in range(depth):
            scatter.c_step(0, i)

    for i in range(depth - 1):
        @pl.when(step == jnp.minimum(i + 1, last))
        def _():
            scatter.x_step(0, i)

    @pl.when(step == last)
    def _():
        scatter.x_step(0, depth - 1)
        scatter.last_step(0)
        loop(0, chunks, lambda i: swap.chunk(i, half, 0).wait())
        scatter.finish()


def reverse_call(depth, qkv, segments, slopes, dcontext, gup, contracted):
    length, width = qkv.shape
    model, hidden = gup.shape
    pairs = width // (6 * HEAD_DIM)
    block = min(256, length)
    span = min(length, block + MAX_SPAN)
    half = length // 2
    dma = pltpu.SemaphoreType.DMA
    shapes = [(model // (4 * depth), hidden)]
    return pl.pallas_call(
        functools.partial(reverse_kernel, depth, block),
        grid=(pairs,),
        out_shape=(
            shaped((length, width)),
            shaped((1, 4 * HEAD_DIM * pairs), jnp.float32),
            shaped(shapes[0], jnp.float32),
            shaped((half, model)),
        ),
        in_specs=[
            pl.BlockSpec(memory_space=pltpu.SMEM),
            pl.BlockSpec((length, 6 * HEAD_DIM), lambda p: (0, p)),
            pl.BlockSpec((length, 2 * HEAD_DIM), lambda p: (0, p)),
            pl.BlockSpec((length, 1), lambda p: (0, 0)),
            pl.BlockSpec((1, length), lambda p: (0, 0)),
            pl.BlockSpec(memory_space=pltpu.VMEM),
            pl.BlockSpec(memory_space=pl.ANY),
        ],
        out_specs=(
            pl.BlockSpec((length, 6 * HEAD_DIM), lambda p: (0, p)),
            pl.BlockSpec((1, 4 * HEAD_DIM), lambda p: (0, p)),
            pl.BlockSpec(memory_space=pltpu.VMEM),
            pl.BlockSpec(memory_space=pl.ANY),
        ),
        scratch_shapes=[
            pltpu.VMEM((span, length), jnp.float32),
            pltpu.VMEM((length, HEAD_DIM), jnp.float32),
            pltpu.VMEM((length, HEAD_DIM), jnp.float32),
            pltpu.VMEM((length, HEAD_DIM), jnp.float32),
        ]
        + [dma((half // CHUNK,))] * 2
        + Scatter.scratch(shapes, depth),
        cost_estimate=pl.CostEstimate(
            flops=10 * length * span * width // 3,
            bytes_accessed=14 * length * width // 3,
            transcendentals=length * span * pairs * 2,
        ),
        compiler_params=pltpu.CompilerParams(
            collective_id=3, has_side_effects=True, vmem_limit_bytes=48 * MIB
        ),
        name="attention_backward",
    )(slopes, qkv, dcontext, segments[:, None], segments[None, :], gup, contracted)


def direct_kernel(
    depth, block, slopes, x, rows_seg, cols_seg, shard, out, full, offsets, shard_low, *sems
):
    step = pl.program_id(0)
    last = pl.num_programs(0) - 1
    spot = Spot(depth)
    gather = Gather(spot, (shard_low,), (full,), *sems)

    @pl.when(step == 0)
    def _():
        cast_into(shard, shard_low, 0)
        spot.greet()
        gather.start()

    forward_kernel(block, slopes, x, rows_seg, cols_seg, out, offsets)

    for i in range(depth):

        @pl.when(step == jnp.minimum(i, last))
        def _():
            if i + 1 < depth:
                gather.z_step(0, i + 1)
            if i > 0:
                gather.x_step(0, i - 1)

    @pl.when(step == last)
    def _():
        gather.x_step(0, depth - 1)
        gather.finish()


def direct_call(depth, qkv, segments, slopes, shard):
    length, width = qkv.shape
    pairs = width // (6 * HEAD_DIM)
    block = min(256, length)
    span = min(length, block + MAX_SPAN)
    cut = shard.shape[1] // 2
    return pl.pallas_call(
        functools.partial(direct_kernel, depth, block),
        grid=(pairs,),
        out_shape=(
            shaped((length, width // 3)),
            shaped((4 * depth * shard.shape[0], cut)),
        ),
        in_specs=[
            pl.BlockSpec(memory_space=pltpu.SMEM),
            pl.BlockSpec((length, 6 * HEAD_DIM), lambda p: (0, p)),
            pl.BlockSpec((length, 1), lambda p: (0, 0)),
            pl.BlockSpec((1, length), lambda p: (0, 0)),
            pl.BlockSpec(memory_space=pltpu.VMEM),
        ],
        out_specs=(
            pl.BlockSpec((length, 2 * HEAD_DIM), lambda p: (0, p)),
            pl.BlockSpec(memory_space=pl.ANY),
        ),
        scratch_shapes=[
            pltpu.VMEM((length, span), jnp.float32),
            pltpu.VMEM((shard.shape[0], cut), jnp.bfloat16),
        ]
        + Gather.semaphores(1, depth),
        cost_estimate=pl.CostEstimate(
            flops=4 * length * span * width // 3,
            bytes_accessed=8 * length * width // 3,
            transcendentals=length * span * pairs * 2,
        ),
        compiler_params=pltpu.CompilerParams(
            collective_id=4, has_side_effects=True, vmem_limit_bytes=40 * MIB
        ),
        name="attention_forward",
    )(slopes, qkv, segments[:, None], segments[None, :], shard)


def update_kernel(kinds, *refs):
    count = len(kinds)
    ins, outs = refs[: 4 * count], refs[4 * count :]
    for number, (rate, decay) in enumerate(kinds):
        given, made = ins[4 * number : 4 * number + 4], outs[4 * number : 4 * number + 4]

        def one(part, given=given, made=made, rate=rate, decay=decay):
            param, grad, first, second = (ref[part, :] for ref in given)
            made[0][part, :] = grad
            for target, value in zip(made[1:], adamw(param, grad, first, second, rate, decay)):
                target[part, :] = value

        rows = given[0].shape[0]
        if rows == 1:
            one(slice(0, 1))
        else:
            strips(rows, STRIP, lambda r, one=one: one(pl.ds(r, STRIP)))


def update_call(params, grads, firsts, seconds):
    kinds, args, outs, turned = [], [], [], (2, 6)
    for index in range(12):
        matrix = index in (0, 2, 4, 6)
        kinds.append((0.01, 0.1) if matrix else (0.1, 0.0))
        for value in (params[index], grads[index], firsts[index], seconds[index]):
            value = value.T if index in turned else value if matrix else value[None]
            args.append(value)
            outs.append(shaped(value.shape, jnp.float32))
    size = 8 * sum(a.size for a in args)
    made = pl.pallas_call(
        functools.partial(update_kernel, kinds),
        out_shape=outs,
        in_specs=vmem(48),
        out_specs=vmem(48),
        cost_estimate=pl.CostEstimate(flops=0, bytes_accessed=size, transcendentals=0),
        compiler_params=pltpu.CompilerParams(vmem_limit_bytes=32 * MIB),
        name="update",
    )(*args)
    groups = []
    for index in range(12):
        plain = index in (0, 4)
        groups.append(
            [
                v if plain else v.T if index in turned else v[0]
                for v in made[4 * index : 4 * index + 4]
            ]
        )
    return tuple([g[place] for g in groups] for place in range(4))


def linked(
    entering_activations,
    segment_ids,
    leaving_activation_slope,
    qkv_weight,
    qv_bias,
    dense_weight,
    dense_bias,
    up_weight,
    up_bias,
    down_weight,
    down_bias,
    mixer_scale_factor,
    mixer_offset_term,
    perceptron_scale_factor,
    perceptron_offset_term,
):
    depth = lax.axis_size("dp") // 4
    rank = lax.axis_index("tensor")
    local_heads = qkv_weight.shape[1] // (3 * HEAD_DIM)
    slopes = head_slopes(rank * local_heads, local_heads)
    segments = segment_ids[0]
    ones, qkv_low, dense_low = spread_call(
        depth,
        entering_activations,
        mixer_scale_factor,
        mixer_offset_term,
        (qkv_weight, dense_weight.T),
    )
    out_own, ones = lax.optimization_barrier(
        (leaving_activation_slope.astype(jnp.bfloat16), ones)
    )
    out_other = swap(out_own)
    qkv = (product(ones, qkv_low) + full_bias(qv_bias, local_heads)).astype(jnp.bfloat16)
    context, down_low = direct_call(depth, qkv, segments, slopes, down_weight.T)
    dense_part = times_transposed(context, dense_low).astype(jnp.bfloat16)
    resid, dresid, resid_low, grad_up, down_part, grad_down, early, up_bias_part = core_call(
        depth,
        dense_part,
        entering_activations,
        dense_bias,
        perceptron_scale_factor,
        perceptron_offset_term,
        leaving_activation_slope,
        out_other,
        up_weight,
        down_weight.T,
        down_low,
        up_bias,
    )
    dcontext = times_transposed(resid_low, jnp.swapaxes(dense_low, 0, 1)).astype(jnp.bfloat16)
    grad_dense = inner_rows(resid_low, context).astype(jnp.bfloat16)
    dqkv_low, qv_part, grad_up, arrived = reverse_call(
        depth, qkv, segments, slopes, dcontext, grad_up, down_part
    )
    half = resid.shape[0]
    block_out = (
        resid + (arrived.astype(jnp.float32) + down_part[:half].astype(jnp.float32)) + down_bias
    )
    entering_slope, grad_qkv, grad_dense, vector, ups, qvs = leave_call(
        depth,
        ones,
        dqkv_low,
        qkv_low,
        dresid,
        entering_activations,
        mixer_scale_factor,
        early,
        up_bias_part,
        qv_part,
        grad_dense,
    )
    return (
        block_out,
        entering_slope,
        (
            grad_qkv,
            qvs[0],
            grad_dense.T,
            vector[0],
            grad_up,
            ups[0],
            grad_down.T,
            vector[1],
            vector[4],
            vector[5],
            vector[2],
            vector[3],
        ),
    )


def general(
    entering_activations,
    segment_ids,
    leaving_activation_slope,
    qkv_weight,
    qv_bias,
    dense_weight,
    dense_bias,
    up_weight,
    up_bias,
    down_weight,
    down_bias,
    mixer_scale_factor,
    mixer_offset_term,
    perceptron_scale_factor,
    perceptron_offset_term,
):
    qkv_low, dense_low, up_low, down_low = (
        lax.all_gather(qkv_weight.astype(jnp.bfloat16), "dp", axis=0, tiled=True),
        lax.all_gather(dense_weight.astype(jnp.bfloat16), "dp", axis=1, tiled=True),
        lax.all_gather(up_weight.astype(jnp.bfloat16), "dp", axis=0, tiled=True),
        lax.all_gather(down_weight.astype(jnp.bfloat16), "dp", axis=1, tiled=True),
    )
    local_heads = qkv_low.shape[1] // (3 * HEAD_DIM)
    tensor_rank = lax.axis_index("tensor")
    count = lax.axis_size("tensor")
    slopes = head_slopes(tensor_rank * local_heads, local_heads)
    segments = segment_ids[0]
    mixer_standardised, mixer_unit_spread1, mixer_reciprocal_spread1 = standardise_features(
        entering_activations, mixer_scale_factor, mixer_offset_term
    )
    ones = spread(mixer_standardised, count)
    outs = spread(leaving_activation_slope.astype(jnp.bfloat16), count)
    qkv_bias = full_bias(qv_bias, local_heads)
    qkv = to_order([(product(one, qkv_low) + qkv_bias).astype(jnp.bfloat16) for one in ones], tensor_rank)
    context = attention_forward(qkv, segments, slopes)
    contexts = from_order(context, tensor_rank, count)
    skip_path_sum = (
        entering_activations
        + fold([product(part, dense_low).astype(jnp.bfloat16) for part in contexts], count)
        + dense_bias
    )
    perceptron_standardised, perceptron_unit_spread2, perceptron_reciprocal_spread2 = (
        standardise_features(skip_path_sum, perceptron_scale_factor, perceptron_offset_term)
    )
    twos = spread(perceptron_standardised, count)
    acts, dpres, dpre_lows, pre_parts = [], [], [], []
    for two, out in zip(twos, outs):
        act_val, act_slope = gelu_parts(product(two, up_low) + up_bias)
        acts.append(act_val.astype(jnp.bfloat16))
        dpres.append(times_transposed(out, down_low) * act_slope)
        dpre_lows.append(dpres[-1].astype(jnp.bfloat16))
        pre_parts.append(times_transposed(dpre_lows[-1], up_low).astype(jnp.bfloat16))
    pre_perceptron_sensitivity = fold(pre_parts, count)
    block_out = (
        skip_path_sum
        + fold([product(act, down_low).astype(jnp.bfloat16) for act in acts], count)
        + down_bias
    )
    contraction_sensitivity = add_up(acts, outs).astype(jnp.bfloat16)
    expansion_sensitivity = add_up(twos, dpre_lows).astype(jnp.bfloat16)
    up_bias_part = sum(jnp.sum(dpre, axis=0) for dpre in dpres)
    skip_path_sensitivity = leaving_activation_slope + standardise_features_reverse(
        pre_perceptron_sensitivity,
        perceptron_unit_spread2,
        perceptron_reciprocal_spread2,
        perceptron_scale_factor,
    )
    resids = spread(skip_path_sensitivity.astype(jnp.bfloat16), count)
    mixer_merge_sensitivity = add_up(contexts, resids).astype(jnp.bfloat16)
    dcontext = to_order(
        [times_transposed(resid, dense_low).astype(jnp.bfloat16) for resid in resids], tensor_rank
    )
    dqkv_low, dqkv_sums = attention_backward(qkv, segments, slopes, dcontext)
    dqkv_lows = from_order(dqkv_low, tensor_rank, count)
    packed_triple_slope = add_up(ones, dqkv_lows).astype(jnp.bfloat16)
    triple = dqkv_sums.reshape(local_heads, 3, HEAD_DIM)
    qv_part = jnp.stack([triple[:, 0], triple[:, 2]], axis=1).reshape(-1)
    pre_mixer_sensitivity = fold(
        [times_transposed(part, qkv_low).astype(jnp.bfloat16) for part in dqkv_lows], count
    )
    entering_activation_slope = skip_path_sensitivity + standardise_features_reverse(
        pre_mixer_sensitivity, mixer_unit_spread1, mixer_reciprocal_spread1, mixer_scale_factor
    )
    early, up_bias_grad = total_over_all(
        jnp.concatenate(
            [
                jnp.sum(skip_path_sensitivity, axis=0),
                jnp.sum(leaving_activation_slope, axis=0),
                jnp.sum(pre_perceptron_sensitivity * perceptron_unit_spread2, axis=0),
                jnp.sum(pre_perceptron_sensitivity, axis=0),
                up_bias_part,
            ]
        ),
        4 * D,
        tensor_rank,
    )
    dense_bias_grad, down_bias_grad, gain_two_grad, shift_two_grad = jnp.split(early, 4)
    late, qv_bias_grad = total_over_all(
        jnp.concatenate(
            [
                jnp.sum(pre_mixer_sensitivity * mixer_unit_spread1, axis=0),
                jnp.sum(pre_mixer_sensitivity, axis=0),
                qv_part,
            ]
        ),
        2 * D,
        tensor_rank,
    )
    gain_one_grad, shift_one_grad = jnp.split(late, 2)
    packed_triple_slope, mixer_merge_sensitivity, expansion_sensitivity, contraction_sensitivity = (
        part.astype(jnp.float32)
        for part in (
            lax.psum_scatter(packed_triple_slope, "dp", scatter_dimension=0, tiled=True),
            lax.psum_scatter(mixer_merge_sensitivity, "dp", scatter_dimension=1, tiled=True),
            lax.psum_scatter(expansion_sensitivity, "dp", scatter_dimension=0, tiled=True),
            lax.psum_scatter(contraction_sensitivity, "dp", scatter_dimension=1, tiled=True),
        )
    )
    return block_out, entering_activation_slope, (
        packed_triple_slope,
        qv_bias_grad,
        mixer_merge_sensitivity,
        dense_bias_grad,
        expansion_sensitivity,
        up_bias_grad,
        contraction_sensitivity,
        down_bias_grad,
        gain_one_grad,
        shift_one_grad,
        gain_two_grad,
        shift_two_grad,
    )


def local(
    entering_activations,
    segment_ids,
    leaving_activation_slope,
    qkv_weight,
    qv_bias,
    dense_weight,
    dense_bias,
    up_weight,
    up_bias,
    down_weight,
    down_bias,
    mixer_scale_factor,
    mixer_offset_term,
    perceptron_scale_factor,
    perceptron_offset_term,
    first_qkv_weight,
    first_qv_bias,
    first_dense_weight,
    first_dense_bias,
    first_up_weight,
    first_up_bias,
    first_down_weight,
    first_down_bias,
    first_norm1_gain,
    first_norm1_bias,
    first_norm2_gain,
    first_norm2_bias,
    second_qkv_weight,
    second_qv_bias,
    second_dense_weight,
    second_dense_bias,
    second_up_weight,
    second_up_bias,
    second_down_weight,
    second_down_bias,
    second_norm1_gain,
    second_norm1_bias,
    second_norm2_gain,
    second_norm2_bias,
):
    params = (
        qkv_weight,
        qv_bias,
        dense_weight,
        dense_bias,
        up_weight,
        up_bias,
        down_weight,
        down_bias,
        mixer_scale_factor,
        mixer_offset_term,
        perceptron_scale_factor,
        perceptron_offset_term,
    )
    firsts = (
        first_qkv_weight,
        first_qv_bias,
        first_dense_weight,
        first_dense_bias,
        first_up_weight,
        first_up_bias,
        first_down_weight,
        first_down_bias,
        first_norm1_gain,
        first_norm1_bias,
        first_norm2_gain,
        first_norm2_bias,
    )
    seconds = (
        second_qkv_weight,
        second_qv_bias,
        second_dense_weight,
        second_dense_bias,
        second_up_weight,
        second_up_bias,
        second_down_weight,
        second_down_bias,
        second_norm1_gain,
        second_norm1_bias,
        second_norm2_gain,
        second_norm2_bias,
    )
    whole_line = lax.axis_size("tensor") == 2 and lax.axis_size("dp") % 4 == 0
    route = linked if whole_line and segment_ids.shape[0] == 1 else general
    block_out, entering_activation_slope, parameter_slopes = route(
        entering_activations,
        segment_ids,
        leaving_activation_slope,
        qkv_weight,
        qv_bias,
        dense_weight,
        dense_bias,
        up_weight,
        up_bias,
        down_weight,
        down_bias,
        mixer_scale_factor,
        mixer_offset_term,
        perceptron_scale_factor,
        perceptron_offset_term,
    )
    if route is linked:
        parameter_slopes, news, moments_one, moments_two = update_call(
            params, parameter_slopes, firsts, seconds
        )
        return (
            block_out,
            entering_activation_slope,
            *parameter_slopes,
            *news,
            *moments_one,
            *moments_two,
        )
    results = []
    for index in range(12):
        matrix = index in (0, 2, 4, 6)
        results.append(
            adamw(
                params[index],
                parameter_slopes[index],
                firsts[index],
                seconds[index],
                0.01 if matrix else 0.1,
                0.1 if matrix else 0.0,
            )
        )
    news = [r[0] for r in results]
    moments_one = [r[1] for r in results]
    moments_two = [r[2] for r in results]
    return (
        block_out,
        entering_activation_slope,
        *parameter_slopes,
        *news,
        *moments_one,
        *moments_two,
    )


def solution(mesh):
    in_specs = (
        P(("dp", "tensor"), None),
        P("dp", None),
        P(("dp", "tensor"), None),
        P("dp", "tensor"),
        P("tensor"),
        P("tensor", "dp"),
        P(),
        P("dp", "tensor"),
        P("tensor"),
        P("tensor", "dp"),
        P(),
        P(),
        P(),
        P(),
        P(),
        P("dp", "tensor"),
        P("tensor"),
        P("tensor", "dp"),
        P(),
        P("dp", "tensor"),
        P("tensor"),
        P("tensor", "dp"),
        P(),
        P(),
        P(),
        P(),
        P(),
        P("dp", "tensor"),
        P("tensor"),
        P("tensor", "dp"),
        P(),
        P("dp", "tensor"),
        P("tensor"),
        P("tensor", "dp"),
        P(),
        P(),
        P(),
        P(),
        P(),
    )
    out_specs = (
        P(("dp", "tensor"), None),
        P(("dp", "tensor"), None),
        P("dp", "tensor"),
        P("tensor"),
        P("tensor", "dp"),
        P(),
        P("dp", "tensor"),
        P("tensor"),
        P("tensor", "dp"),
        P(),
        P(),
        P(),
        P(),
        P(),
        P("dp", "tensor"),
        P("tensor"),
        P("tensor", "dp"),
        P(),
        P("dp", "tensor"),
        P("tensor"),
        P("tensor", "dp"),
        P(),
        P(),
        P(),
        P(),
        P(),
        P("dp", "tensor"),
        P("tensor"),
        P("tensor", "dp"),
        P(),
        P("dp", "tensor"),
        P("tensor"),
        P("tensor", "dp"),
        P(),
        P(),
        P(),
        P(),
        P(),
        P("dp", "tensor"),
        P("tensor"),
        P("tensor", "dp"),
        P(),
        P("dp", "tensor"),
        P("tensor"),
        P("tensor", "dp"),
        P(),
        P(),
        P(),
        P(),
        P(),
    )
    return jax.shard_map(local, mesh=mesh, in_specs=in_specs, out_specs=out_specs, check_vma=False)
```
